128 devices in a mesh: row: 16 (over x_hi, y, core), rep: 8 (over x_lo, z).
Axes of the slice: x: 4 (x_hi: 2, x_lo: 2; x = x_hi * 2 + x_lo), y: 4, z: 4, core: 2. Of those that a mesh axis runs over, the one named last changes fastest.
Arguments:
- features: bfloat16 [65536, 1024], P('row', 'rep'), may hold values from -6 to 6
- tiles: bfloat16 [512, 16, 128, 128], P('row'), may hold values from -0.1875 to 0.1875
- columns: int32 [512, 16], P('row'), may hold values from 0 to 511
- counts: int32 [512], P('row'), may hold values from 1 to 16, as said below
- weight: bfloat16 [1024, 1024], P(None, 'rep'), may hold values from -0.1875 to 0.1875
- cotangent: bfloat16 [65536, 1024], P('row', 'rep'), may hold values from -6 to 6
Outputs:
- activations: bfloat16 [65536, 1024], P('row', 'rep')
- feature_grad: bfloat16 [65536, 1024], P('row', 'rep')
- weight_grad: float32 [1024, 1024], P('rep', 'row')
The draws below stay inside these ranges and needn't reach their ends.
Inputs may be any that keep to these rules, and one draw needn't show every extreme that they name: `counts`: in every draw some row block has all 16 slots in use.
All inputs are finite; a program needn't handle non-finite values.
Results may differ from the reference program's by a relative error of at most 0.014.
Values may be sent and summed in bfloat16 or wider, within the bound.
A program may use at most 192 MiB of HBM per device.

```python
import math
import jax
import jax.numpy as jnp
import numpy as np
from jax import lax

F = 1024
H = 1024
TILE = 128
KMAX = 16
BLK_DEV = 32
NBLK = 512
NODES = 65536
N_ROW = 16


def draw_counts(key, part):
    first_key, second_key = jax.random.split(jax.random.fold_in(key, 17))
    drawn = jax.random.randint(first_key, (NBLK,), 1, KMAX + 1)
    chosen = jax.random.randint(second_key, (), 0, NBLK)
    return jnp.where(jnp.arange(NBLK) == chosen, KMAX, drawn).astype(jnp.int32)


def plant(result, rng, low, top_value):
    index_at = [jax.random.randint(jax.random.fold_in(rng, axis), (), 0, length) for axis, length in enumerate(result.shape)]
    widest = result.shape.index(max(result.shape))
    next_to = index_at[:widest] + [(index_at[widest] + 1) % result.shape[widest]] + index_at[widest + 1:]
    return result.at[tuple(index_at)].set(low).at[tuple(next_to)].set(top_value)


def block_scale(key, extent, shards, least, high):
    def one(position, parts):
        draws = jax.random.uniform(jax.random.fold_in(jax.random.fold_in(key, 6), position), (parts,), jnp.float32, least / len(shards), high / len(shards))
        return jnp.repeat(jnp.exp(draws), extent[position] // parts).reshape((-1,) + (1,) * (len(extent) - position - 1))

    factor_of = one(*shards[0])
    for cut in shards[1:]:
        factor_of = factor_of * one(*cut)
    return factor_of


def rank_table(number_of, skew):
    weights = [(1 << 20) // math.isqrt(rank ** skew) + 1 for rank in range(1, number_of + 1)]
    width = 1 + sum(weights) // (1 << 30)
    return np.cumsum(np.array([max(1, weight // width) for weight in weights]))


def ranked_ids(key, shape, amount, skew):
    table = rank_table(amount, skew)
    ticket = jax.random.randint(jax.random.fold_in(key, 1), shape, 0, int(table[amount - 1]))
    grade = jnp.searchsorted(jnp.asarray(table, jnp.int32), ticket, side="right")
    return jax.random.permutation(jax.random.fold_in(key, 2), amount)[grade].astype(jnp.int32)


def bell_draw(key, extent, spread, most, shards=(), dtype=jnp.bfloat16):
    array = spread * jax.random.normal(key, extent, jnp.float32)
    if shards:
        array = array * block_scale(key, extent, shards, -0.22, 0.18)
    return jnp.clip(array, -most, most).astype(dtype)


def setup_inputs(seed: int = 0) -> dict:
    key_of = jax.random.split(jax.random.key(seed), 7)
    features = bell_draw(key_of[0], (NODES, F), 1.0, 6.0, ((0, 16), (1, 8)))
    tiles = bell_draw(key_of[1], (NBLK, KMAX, TILE, TILE), (KMAX * TILE // 2) ** -0.5, 0.1875, ((0, 16),))
    columns = plant(ranked_ids(key_of[2], (NBLK, KMAX), NBLK, 2), jax.random.fold_in(key_of[2], 3), 0, NBLK - 1).astype(jnp.int32)
    counts = draw_counts(jax.random.fold_in(key_of[6], 71), 0)
    weight = bell_draw(key_of[4], (F, H), F ** -0.5, 0.1875, ((1, 8),))
    cotangent = bell_draw(key_of[5], (NODES, H), 1.0, 6.0, ((0, 16), (1, 8)))
    return dict(features=features, tiles=tiles, columns=columns, counts=counts, weight=weight, cotangent=cotangent)


def reference(features, tiles, columns, counts, weight, cotangent):
    alive_mask = jnp.arange(KMAX)[None, :] < counts[:, None]
    masked_tiles = jnp.where(alive_mask[:, :, None, None], tiles.astype(jnp.float32), jnp.float32(0.0))
    source_blocks = features.reshape(NBLK, TILE, F)

    def one_block(packed):
        tile_block, column_block = packed
        operand = jnp.take(source_blocks, column_block, axis=0).astype(jnp.float32)
        return jnp.einsum("kij,kjf->if", tile_block, operand)

    mixed = lax.map(one_block, (masked_tiles, columns)).reshape(NODES, F).astype(jnp.bfloat16)
    preact = jnp.dot(mixed, weight, preferred_element_type=jnp.float32)
    sigmoid_pre = jax.nn.sigmoid(preact)
    activations = (preact * sigmoid_pre).astype(jnp.bfloat16)
    grad_out = (cotangent.astype(jnp.float32) * sigmoid_pre * (1.0 + preact * (1.0 - sigmoid_pre))).astype(jnp.bfloat16)
    weight_grad = jnp.dot(mixed.T, grad_out, preferred_element_type=jnp.float32)
    mixed_grad = jnp.dot(grad_out, weight.T, preferred_element_type=jnp.float32).astype(jnp.bfloat16)
    grad_blocks = mixed_grad.reshape(N_ROW, BLK_DEV, TILE, F).astype(jnp.float32)
    tiles_dev = masked_tiles.reshape(N_ROW, BLK_DEV, KMAX, TILE, TILE)
    columns_dev = columns.reshape(N_ROW, BLK_DEV * KMAX).astype(jnp.int32)

    def one_device(accum, packed):
        tile_group, column_group, grad_group = packed
        contrib = jnp.einsum("bkij,bif->bkjf", tile_group, grad_group)
        term = jax.ops.segment_sum(contrib.reshape(BLK_DEV * KMAX, TILE, F), column_group, num_segments=NBLK)
        rounded = lax.optimization_barrier(term.astype(jnp.bfloat16))
        return accum + rounded.astype(jnp.float32), None

    total, unused = lax.scan(one_device, jnp.zeros((NBLK, TILE, F), jnp.float32), (tiles_dev, columns_dev, grad_blocks))
    feature_grad = total.reshape(NODES, F).astype(jnp.bfloat16)
    return activations, feature_grad, weight_grad
```

```python
import functools

import jax
import jax.numpy as jnp
from jax import lax
from jax.experimental import pallas as pl
from jax.experimental.pallas import tpu as pltpu
from jax.sharding import PartitionSpec as P

F32 = jnp.float32
BF16 = jnp.bfloat16
SLOTS_AHEAD = 4


def fwd_kernel(cols, counts, tiles, gathered, out, tbuf, gbuf, sems):
    blocks, slots, t, _ = tiles.shape

    def copies(b, k):
        s = lax.rem(b, SLOTS_AHEAD)
        at = pl.ds(pl.multiple_of(k * t, t), t)
        return (
            pltpu.make_async_copy(tiles.at[b, k], tbuf.at[s, :, at], sems.at[s, k, 0]),
            pltpu.make_async_copy(gathered.at[cols[b, k]], gbuf.at[s, at, :], sems.at[s, k, 1]),
        )

    def start(b):
        @pl.loop(0, counts[b])
        def _(k):
            for c in copies(b, k):
                c.start()

    for b in range(SLOTS_AHEAD - 1):
        start(b)

    @pl.loop(0, blocks)
    def _(b):
        s = lax.rem(b, SLOTS_AHEAD)

        @pl.when(b + SLOTS_AHEAD - 1 < blocks)
        def _():
            start(b + SLOTS_AHEAD - 1)

        n = counts[b]

        @pl.loop(0, n)
        def _(k):
            for c in copies(b, k):
                c.wait()

        @pl.when(lax.rem(n, 2) == 1)
        def _():
            at = pl.ds(pl.multiple_of(n * t, t), t)
            tbuf[s, :, at] = jnp.zeros((t, t), BF16)
            gbuf[s, at, :] = jnp.zeros((t, t), BF16)

        row = pl.ds(pl.multiple_of(b * t, t), t)
        for p in range(1, slots // 2 + 1):

            @pl.when((n + 1) // 2 == p)
            def _():
                w = 2 * p * t
                out[row, :] = jnp.dot(
                    tbuf[s, :, :w], gbuf[s, :w, :], preferred_element_type=F32
                ).astype(BF16)


def spmm(gathered, tiles, columns, counts):
    blocks, slots, t, _ = tiles.shape
    width = gathered.shape[-1]
    return pl.pallas_call(
        fwd_kernel,
        grid_spec=pltpu.PrefetchScalarGridSpec(
            num_scalar_prefetch=2,
            grid=(1,),
            in_specs=[pl.BlockSpec(memory_space=pl.ANY)] * 2,
            out_specs=pl.BlockSpec((blocks * t, width), lambda i, *_: (0, 0)),
            scratch_shapes=[
                pltpu.VMEM((SLOTS_AHEAD, t, slots * t), BF16),
                pltpu.VMEM((SLOTS_AHEAD, slots * t, width), BF16),
                pltpu.SemaphoreType.DMA((SLOTS_AHEAD, slots, 2)),
            ],
        ),
        out_shape=jax.ShapeDtypeStruct((blocks * t, width), BF16),
        name="spmm",
    )(columns, counts, tiles, gathered)


GROUP = 4
OUT_CHUNK = 16


def bwd_kernel(cols, counts, tiles, grad, out, acc, tbuf, stage, sems, out_sems):
    blocks, slots, t, _ = tiles.shape
    total = acc.shape[0]

    def copy(b, k):
        s = lax.rem(b, SLOTS_AHEAD)
        return pltpu.make_async_copy(tiles.at[b, k], tbuf.at[s, k], sems.at[s, k])

    def start(b):
        @pl.loop(0, counts[b])
        def _(k):
            copy(b, k).start()

    for b in range(SLOTS_AHEAD - 1):
        start(b)

    @pl.loop(0, total)
    def _(j):
        acc[j] = jnp.zeros(acc.shape[1:], F32)

    @pl.loop(0, blocks)
    def _(b):
        s = lax.rem(b, SLOTS_AHEAD)

        @pl.when(b + SLOTS_AHEAD - 1 < blocks)
        def _():
            start(b + SLOTS_AHEAD - 1)

        n = counts[b]

        @pl.loop(0, n)
        def _(k):
            copy(b, k).wait()

        g = grad[pl.ds(pl.multiple_of(b * t, t), t), :]

        @pl.loop(0, (n + GROUP - 1) // GROUP)
        def _(q):
            terms = []
            for i in range(GROUP):
                k = q * GROUP + i
                term = lax.dot_general(
                    tbuf[s, k], g, (((0,), (0,)), ((), ())), preferred_element_type=F32
                )
                terms.append(jnp.where(k < n, term, 0.0))
            for i in range(GROUP):
                acc[cols[b, q * GROUP + i]] += terms[i]

    def flush(c):
        s = lax.rem(c, 2)
        return pltpu.make_async_copy(
            stage.at[s], out.at[pl.ds(c * OUT_CHUNK, OUT_CHUNK)], out_sems.at[s]
        )

    @pl.loop(0, total // OUT_CHUNK)
    def _(c):
        s = lax.rem(c, 2)

        @pl.when(c >= 2)
        def _():
            flush(c - 2).wait()

        @pl.loop(0, OUT_CHUNK)
        def _(j):
            stage[s, j] = acc[c * OUT_CHUNK + j].astype(BF16)

        flush(c).start()

    for c in (total // OUT_CHUNK - 2, total // OUT_CHUNK - 1):
        flush(c).wait()


def spmm_t(grad, tiles, columns, counts, total):
    blocks, slots, t, _ = tiles.shape
    width = grad.shape[-1]
    return pl.pallas_call(
        bwd_kernel,
        grid_spec=pltpu.PrefetchScalarGridSpec(
            num_scalar_prefetch=2,
            grid=(1,),
            in_specs=[
                pl.BlockSpec(memory_space=pl.ANY),
                pl.BlockSpec((blocks * t, width), lambda i, *_: (0, 0)),
            ],
            out_specs=pl.BlockSpec(memory_space=pl.ANY),
            scratch_shapes=[
                pltpu.VMEM((total, t, width), F32),
                pltpu.VMEM((SLOTS_AHEAD, slots, t, t), BF16),
                pltpu.VMEM((2, OUT_CHUNK, t, width), BF16),
                pltpu.SemaphoreType.DMA((SLOTS_AHEAD, slots)),
                pltpu.SemaphoreType.DMA((2,)),
            ],
        ),
        out_shape=jax.ShapeDtypeStruct((total, t, width), BF16),
        compiler_params=pltpu.CompilerParams(vmem_limit_bytes=60 * 1024 * 1024),
        name="spmm_t",
    )(columns, counts, tiles, grad)


def local(features, tiles, columns, counts, weight, cotangent):
    rows_here, feat_local = features.shape
    blocks_here, slots, t, _ = tiles.shape
    total_blocks = blocks_here * lax.axis_size("row")
    gathered = lax.all_gather(features, "row", axis=0, tiled=True)
    cot = lax.all_to_all(cotangent, "rep", 0, 1, tiled=True)
    w = lax.all_gather(weight, "rep", axis=1, tiled=True)
    mixed = spmm(gathered.reshape(total_blocks, t, feat_local), tiles, columns, counts)
    mixed = lax.all_to_all(mixed, "rep", 0, 1, tiled=True)
    preact = jnp.dot(mixed, w, preferred_element_type=F32)
    sig = jax.nn.sigmoid(preact)
    act = (preact * sig).astype(BF16)
    activations = lax.all_to_all(act, "rep", 1, 0, tiled=True)
    grad_out = (cot.astype(F32) * sig * (1.0 + preact * (1.0 - sig))).astype(BF16)
    mixed_grad = lax.dot_general(
        grad_out, w, (((1,), (1,)), ((), ())), preferred_element_type=F32
    ).astype(BF16)
    mixed_grad = lax.all_to_all(mixed_grad, "rep", 1, 0, tiled=True)
    terms = lax.dot_general(mixed, grad_out, (((0,), (0,)), ((), ())), preferred_element_type=F32)
    terms = lax.psum_scatter(terms.astype(BF16), "rep", scatter_dimension=0, tiled=True)
    weight_grad = lax.psum_scatter(terms, "row", scatter_dimension=1, tiled=True).astype(F32)
    partial = spmm_t(mixed_grad, tiles, columns, counts, total_blocks)
    feature_grad = lax.psum_scatter(
        partial.reshape(total_blocks * t, feat_local), "row", scatter_dimension=0, tiled=True
    )
    return activations, feature_grad, weight_grad


def solution(mesh):
    in_specs = (
        P("row", "rep"),
        P("row", None, None, None),
        P("row", None),
        P("row"),
        P(None, "rep"),
        P("row", "rep"),
    )
    out_specs = (P("row", "rep"), P("row", "rep"), P("rep", "row"))
    return jax.shard_map(local, mesh=mesh, in_specs=in_specs, out_specs=out_specs, check_vma=False)
```

```python
import functools

import jax
import jax.numpy as jnp
from jax import lax
from jax.experimental import pallas as pl
from jax.experimental.pallas import tpu as pltpu
from jax.sharding import PartitionSpec as P

F32 = jnp.float32
BF16 = jnp.bfloat16
MESH = pl.DeviceIdType.MESH
ROWS_Y = 4
N_ROW = 16
N_REP = 8
ANY = pl.BlockSpec(memory_space=pl.ANY)
VM = pl.BlockSpec(memory_space=pltpu.VMEM)


class Place:
    def __init__(self):
        self.row = lax.axis_index("row")
        self.rep = lax.axis_index("rep")
        self.c = lax.rem(self.row, 2)
        self.y = lax.rem(self.row // 2, ROWS_Y)
        self.h = self.row // (2 * ROWS_Y)

    def slot(self, other, dy, sib=False):
        h = 1 - self.h if other else self.h
        c = 1 - self.c if sib else self.c
        return (h * ROWS_Y + lax.rem(self.y + dy + ROWS_Y, ROWS_Y)) * 2 + c

    def at(self, other, dy, sib=False):
        return (self.slot(other, dy, sib), self.rep)

    def peer(self, d):
        x, z = self.rep // 4, lax.rem(self.rep, 4)
        if d >= 4:
            x = 1 - x
        if d % 4 == 1:
            z = z + 1 - 2 * lax.rem(z, 2)
        elif d % 4 == 2:
            z = lax.rem(z + 2, 4)
        elif d % 4 == 3:
            z = 3 - z
        return x * 4 + z


def greet(partners):
    barrier = pltpu.get_barrier_semaphore()
    for partner in partners:
        pl.semaphore_signal(barrier, inc=1, device_id=partner, device_id_type=MESH)
    pl.semaphore_wait(barrier, len(partners))


class Sends:
    def __init__(self, sems):
        self.sems, self.live = sems, []

    def __call__(self, src, dst, recv_sem, device):
        copy = pltpu.make_async_remote_copy(
            src_ref=src,
            dst_ref=dst,
            send_sem=self.sems.at[len(self.live)],
            recv_sem=recv_sem,
            device_id=device,
            device_id_type=MESH,
        )
        copy.start()
        self.live.append(copy)

    def finish(self):
        for copy in self.live:
            copy.wait_send()


def arrived(dst, recv_sem):
    pltpu.make_async_copy(dst, dst, recv_sem).wait()


CHUNKS = 4


def gather_kernel(
    feats, cot, weight, gathered, cots, ws, own, own_w, own_c,
    send_sems, recv_sems, cot_recv, w_recv, w_sib, local_sems,
):
    here = Place()
    step = feats.shape[0] // CHUNKS
    piece = cot.shape[0] // N_REP
    half = weight.shape[0] // 2
    peers = [here.peer(d) for d in range(1, N_REP)]
    sib = here.at(False, 0, True)
    up, down, across = here.at(False, 1), here.at(False, -1), here.at(True, 0)

    loads = [
        pltpu.make_async_copy(feats, own, local_sems.at[0]),
        pltpu.make_async_copy(weight, own_w, local_sems.at[1]),
        pltpu.make_async_copy(
            cot.at[pl.ds(pl.multiple_of(here.rep * piece, piece), piece)], own_c, local_sems.at[2]
        ),
    ]
    for load in loads:
        load.start()
    greet([sib, up, down, across] + [(here.row, q) for q in peers])

    send = Sends(send_sems)

    def rows(chunk):
        return pl.ds(chunk * step, step)

    def place(slot, chunk):
        return gathered.at[slot, rows(chunk)]

    slots = [
        here.slot(False, -1), here.slot(False, 1), here.slot(False, 2), here.slot(True, 0),
        here.slot(True, -1), here.slot(True, 1), here.slot(True, 2),
    ]

    def launch(src_of, slot, order, base, to_x, sib_kind):
        for i in range(CHUNKS):
            if to_x:
                send(src_of(i), place(slot, i), recv_sems.at[3, i], across)
        for i in range(CHUNKS):
            a, b = i, (i + CHUNKS // 2) % CHUNKS
            send(src_of(a), place(slot, a), recv_sems.at[base, a], up)
            send(src_of(b), place(slot, b), recv_sems.at[base + 1, b], down)
        for i in range(CHUNKS):
            send(src_of(i), place(slot, i), recv_sems.at[sib_kind, i], sib)

    launch(lambda i: feats.at[rows(i)], here.row, None, 0, True, 7)

    mine = pl.ds(pl.multiple_of(here.c * half, half), half)
    for d in range(1, N_REP):
        q = peers[d - 1]
        send(weight.at[mine], ws.at[here.rep, mine], w_recv.at[d - 1], (here.row, q))
    for d in range(1, N_REP):
        q = peers[d - 1]
        send(
            cot.at[pl.ds(pl.multiple_of(q * piece, piece), piece)],
            cots.at[here.rep], cot_recv.at[d - 1], (here.row, q),
        )

    stores = [
        pltpu.make_async_copy(own, gathered.at[here.row], local_sems.at[3]),
        pltpu.make_async_copy(own_w, ws.at[here.rep], local_sems.at[4]),
        pltpu.make_async_copy(own_c, cots.at[here.rep], local_sems.at[5]),
    ]
    for load, store in zip(loads, stores):
        load.wait()
        store.start()

    def take(kind, chunk, to_up, to_down):
        slot = slots[kind]
        arrived(place(slot, chunk), recv_sems.at[kind, chunk])
        far = 2 if kind < 3 else 6
        if to_up:
            send(place(slot, chunk), place(slot, chunk), recv_sems.at[far, chunk], up)
        if to_down:
            send(place(slot, chunk), place(slot, chunk), recv_sems.at[far, chunk], down)
        send(place(slot, chunk), place(slot, chunk), recv_sems.at[8 + kind, chunk], sib)

    for base in (0, 4):
        for i in range(CHUNKS):
            a, b = i, (i + CHUNKS // 2) % CHUNKS
            take(base, a, a < CHUNKS // 2, False)
            take(base + 1, b, False, b >= CHUNKS // 2)
            if base == 0:
                arrived(place(slots[3], i), recv_sems.at[3, i])
                src = place(slots[3], i)
                send(src, src, recv_sems.at[4, i], up)
                send(src, src, recv_sems.at[5, i], down)
                send(src, src, recv_sems.at[11, i], sib)
        for i in range(CHUNKS):
            take(2 if base == 0 else 6, i, False, False)
        if base == 0:
            for d in range(1, N_REP):
                q = peers[d - 1]
                arrived(ws.at[q, mine], w_recv.at[d - 1])
                send(ws.at[q, mine], ws.at[q, mine], w_sib.at[d - 1], sib)

    theirs = pl.ds(pl.multiple_of((1 - here.c) * half, half), half)
    for d in range(1, N_REP):
        q = peers[d - 1]
        arrived(ws.at[q, theirs], w_sib.at[d - 1])
        arrived(cots.at[q], cot_recv.at[d - 1])
    sib_slots = [here.slot(False, 0, True)] + [
        here.slot(other, dy, True)
        for other, dy in ((False, -1), (False, 1), (False, 2), (True, 0), (True, -1), (True, 1), (True, 2))
    ]
    for kind in range(8):
        for i in range(CHUNKS):
            arrived(place(sib_slots[kind], i), recv_sems.at[7 + kind, i])
    for store in stores:
        store.wait()
    send.finish()


def gather_all(features, cotangent, weight):
    rows, width = features.shape
    n_sends = 15 * CHUNKS + 21
    return pl.pallas_call(
        gather_kernel,
        in_specs=[ANY] * 3,
        out_specs=[ANY] * 3,
        out_shape=[
            jax.ShapeDtypeStruct((N_ROW, rows, width), BF16),
            jax.ShapeDtypeStruct((N_REP, rows // N_REP, width), BF16),
            jax.ShapeDtypeStruct((N_REP,) + weight.shape, BF16),
        ],
        scratch_shapes=[
            pltpu.VMEM((rows, width), BF16),
            pltpu.VMEM(weight.shape, BF16),
            pltpu.VMEM((rows // N_REP, width), BF16),
            pltpu.SemaphoreType.DMA((n_sends,)),
            pltpu.SemaphoreType.DMA((15, CHUNKS)),
            pltpu.SemaphoreType.DMA((N_REP - 1,)),
            pltpu.SemaphoreType.DMA((N_REP - 1,)),
            pltpu.SemaphoreType.DMA((N_REP - 1,)),
            pltpu.SemaphoreType.DMA((6,)),
        ],
        compiler_params=pltpu.CompilerParams(collective_id=0, has_side_effects=True),
        name="gather_all",
    )(features, cotangent, weight)


SLOTS_AHEAD = 4


def fwd_kernel(cols, counts, tiles, gathered, out, tbuf, gbuf, sems):
    blocks, slots, t, _ = tiles.shape

    def copies(b, k):
        s = lax.rem(b, SLOTS_AHEAD)
        at = pl.ds(pl.multiple_of(k * t, t), t)
        return (
            pltpu.make_async_copy(tiles.at[b, k], tbuf.at[s, :, at], sems.at[s, k, 0]),
            pltpu.make_async_copy(gathered.at[cols[b, k]], gbuf.at[s, at, :], sems.at[s, k, 1]),
        )

    def start(b):
        @pl.loop(0, counts[b])
        def _(k):
            for c in copies(b, k):
                c.start()

    for b in range(SLOTS_AHEAD - 1):
        start(b)

    @pl.loop(0, blocks)
    def _(b):
        s = lax.rem(b, SLOTS_AHEAD)

        @pl.when(b + SLOTS_AHEAD - 1 < blocks)
        def _():
            start(b + SLOTS_AHEAD - 1)

        n = counts[b]

        @pl.loop(0, n)
        def _(k):
            for c in copies(b, k):
                c.wait()

        @pl.when(lax.rem(n, 2) == 1)
        def _():
            at = pl.ds(pl.multiple_of(n * t, t), t)
            tbuf[s, :, at] = jnp.zeros((t, t), BF16)
            gbuf[s, at, :] = jnp.zeros((t, t), BF16)

        row = pl.ds(pl.multiple_of(b * t, t), t)
        for p in range(1, slots // 2 + 1):

            @pl.when((n + 1) // 2 == p)
            def _():
                w = 2 * p * t
                out[row, :] = jnp.dot(
                    tbuf[s, :, :w], gbuf[s, :w, :], preferred_element_type=F32
                ).astype(BF16)


def spmm(gathered, tiles, columns, counts):
    blocks, slots, t, _ = tiles.shape
    width = gathered.shape[-1]
    return pl.pallas_call(
        fwd_kernel,
        grid_spec=pltpu.PrefetchScalarGridSpec(
            num_scalar_prefetch=2,
            grid=(1,),
            in_specs=[pl.BlockSpec(memory_space=pl.ANY)] * 2,
            out_specs=pl.BlockSpec((blocks * t, width), lambda i, *_: (0, 0)),
            scratch_shapes=[
                pltpu.VMEM((SLOTS_AHEAD, t, slots * t), BF16),
                pltpu.VMEM((SLOTS_AHEAD, slots * t, width), BF16),
                pltpu.SemaphoreType.DMA((SLOTS_AHEAD, slots, 2)),
            ],
        ),
        out_shape=jax.ShapeDtypeStruct((blocks * t, width), BF16),
        name="spmm",
    )(columns, counts, tiles, gathered)


GROUP = 4
OUT_CHUNK = 16


def bwd_kernel(cols, counts, tiles, grad, out, acc, tbuf, stage, sems, out_sems):
    blocks, slots, t, _ = tiles.shape
    total = acc.shape[0]

    def copy(b, k):
        s = lax.rem(b, SLOTS_AHEAD)
        return pltpu.make_async_copy(tiles.at[b, k], tbuf.at[s, k], sems.at[s, k])

    def start(b):
        @pl.loop(0, counts[b])
        def _(k):
            copy(b, k).start()

    for b in range(SLOTS_AHEAD - 1):
        start(b)

    @pl.loop(0, total)
    def _(j):
        acc[j] = jnp.zeros(acc.shape[1:], F32)

    @pl.loop(0, blocks)
    def _(b):
        s = lax.rem(b, SLOTS_AHEAD)

        @pl.when(b + SLOTS_AHEAD - 1 < blocks)
        def _():
            start(b + SLOTS_AHEAD - 1)

        n = counts[b]

        @pl.loop(0, n)
        def _(k):
            copy(b, k).wait()

        g = grad[pl.ds(pl.multiple_of(b * t, t), t), :]

        @pl.loop(0, (n + GROUP - 1) // GROUP)
        def _(q):
            terms = []
            for i in range(GROUP):
                k = q * GROUP + i
                term = lax.dot_general(
                    tbuf[s, k], g, (((0,), (0,)), ((), ())), preferred_element_type=F32
                )
                terms.append(jnp.where(k < n, term, 0.0))
            for i in range(GROUP):
                acc[cols[b, q * GROUP + i]] += terms[i]

    def flush(c):
        s = lax.rem(c, 2)
        return pltpu.make_async_copy(
            stage.at[s], out.at[pl.ds(c * OUT_CHUNK, OUT_CHUNK)], out_sems.at[s]
        )

    @pl.loop(0, total // OUT_CHUNK)
    def _(c):
        s = lax.rem(c, 2)

        @pl.when(c >= 2)
        def _():
            flush(c - 2).wait()

        @pl.loop(0, OUT_CHUNK)
        def _(j):
            stage[s, j] = acc[c * OUT_CHUNK + j].astype(BF16)

        flush(c).start()

    for c in (total // OUT_CHUNK - 2, total // OUT_CHUNK - 1):
        flush(c).wait()


def spmm_t(grad, tiles, columns, counts, total):
    blocks, slots, t, _ = tiles.shape
    width = grad.shape[-1]
    return pl.pallas_call(
        bwd_kernel,
        grid_spec=pltpu.PrefetchScalarGridSpec(
            num_scalar_prefetch=2,
            grid=(1,),
            in_specs=[
                pl.BlockSpec(memory_space=pl.ANY),
                pl.BlockSpec((blocks * t, width), lambda i, *_: (0, 0)),
            ],
            out_specs=pl.BlockSpec(memory_space=pl.ANY),
            scratch_shapes=[
                pltpu.VMEM((total, t, width), F32),
                pltpu.VMEM((SLOTS_AHEAD, slots, t, t), BF16),
                pltpu.VMEM((2, OUT_CHUNK, t, width), BF16),
                pltpu.SemaphoreType.DMA((SLOTS_AHEAD, slots)),
                pltpu.SemaphoreType.DMA((2,)),
            ],
        ),
        out_shape=jax.ShapeDtypeStruct((total, t, width), BF16),
        compiler_params=pltpu.CompilerParams(vmem_limit_bytes=60 * 1024 * 1024),
        name="spmm_t",
    )(columns, counts, tiles, grad)


def local(features, tiles, columns, counts, weight, cotangent):
    rows_here, feat_local = features.shape
    blocks_here, slots, t, _ = tiles.shape
    total_blocks = blocks_here * lax.axis_size("row")
    gathered, cot, w = gather_all(features, cotangent, weight)
    cot = jnp.swapaxes(cot, 0, 1).reshape(-1, N_REP * feat_local)
    w = jnp.swapaxes(w, 0, 1).reshape(-1, N_REP * feat_local)
    mixed = spmm(gathered.reshape(total_blocks, t, feat_local), tiles, columns, counts)
    mixed = lax.all_to_all(mixed, "rep", 0, 1, tiled=True)
    preact = jnp.dot(mixed, w, preferred_element_type=F32)
    sig = jax.nn.sigmoid(preact)
    act = (preact * sig).astype(BF16)
    activations = lax.all_to_all(act, "rep", 1, 0, tiled=True)
    grad_out = (cot.astype(F32) * sig * (1.0 + preact * (1.0 - sig))).astype(BF16)
    mixed_grad = lax.dot_general(
        grad_out, w, (((1,), (1,)), ((), ())), preferred_element_type=F32
    ).astype(BF16)
    mixed_grad = lax.all_to_all(mixed_grad, "rep", 1, 0, tiled=True)
    terms = lax.dot_general(mixed, grad_out, (((0,), (0,)), ((), ())), preferred_element_type=F32)
    terms = lax.psum_scatter(terms.astype(BF16), "rep", scatter_dimension=0, tiled=True)
    weight_grad = lax.psum_scatter(terms, "row", scatter_dimension=1, tiled=True).astype(F32)
    partial = spmm_t(mixed_grad, tiles, columns, counts, total_blocks)
    feature_grad = lax.psum_scatter(
        partial.reshape(total_blocks * t, feat_local), "row", scatter_dimension=0, tiled=True
    )
    return activations, feature_grad, weight_grad


def solution(mesh):
    in_specs = (
        P("row", "rep"),
        P("row", None, None, None),
        P("row", None),
        P("row"),
        P(None, "rep"),
        P("row", "rep"),
    )
    out_specs = (P("row", "rep"), P("row", "rep"), P("rep", "row"))
    return jax.shard_map(local, mesh=mesh, in_specs=in_specs, out_specs=out_specs, check_vma=False)
```

```python
import functools

import jax
import jax.numpy as jnp
from jax import lax
from jax.experimental import pallas as pl
from jax.experimental.pallas import tpu as pltpu
from jax.sharding import PartitionSpec as P

F32 = jnp.float32
BF16 = jnp.bfloat16
MESH = pl.DeviceIdType.MESH
ROWS_Y = 4
N_ROW = 16
N_REP = 8
ANY = pl.BlockSpec(memory_space=pl.ANY)
VM = pl.BlockSpec(memory_space=pltpu.VMEM)


class Place:
    def __init__(self):
        self.row = lax.axis_index("row")
        self.rep = lax.axis_index("rep")
        self.c = lax.rem(self.row, 2)
        self.y = lax.rem(self.row // 2, ROWS_Y)
        self.h = self.row // (2 * ROWS_Y)

    def slot(self, other, dy, sib=False):
        h = 1 - self.h if other else self.h
        c = 1 - self.c if sib else self.c
        return (h * ROWS_Y + lax.rem(self.y + dy + ROWS_Y, ROWS_Y)) * 2 + c

    def at(self, other, dy, sib=False):
        return (self.slot(other, dy, sib), self.rep)

    def peer(self, d):
        x, z = self.rep // 4, lax.rem(self.rep, 4)
        if d >= 4:
            x = 1 - x
        if d % 4 == 1:
            z = z + 1 - 2 * lax.rem(z, 2)
        elif d % 4 == 2:
            z = lax.rem(z + 2, 4)
        elif d % 4 == 3:
            z = 3 - z
        return x * 4 + z


def greet(partners):
    barrier = pltpu.get_barrier_semaphore()
    for partner in partners:
        pl.semaphore_signal(barrier, inc=1, device_id=partner, device_id_type=MESH)
    pl.semaphore_wait(barrier, len(partners))


class Sends:
    def __init__(self, sems):
        self.sems, self.live = sems, []

    def __call__(self, src, dst, recv_sem, device):
        copy = pltpu.make_async_remote_copy(
            src_ref=src,
            dst_ref=dst,
            send_sem=self.sems.at[len(self.live)],
            recv_sem=recv_sem,
            device_id=device,
            device_id_type=MESH,
        )
        copy.start()
        self.live.append(copy)

    def finish(self):
        for copy in self.live:
            copy.wait_send()


def arrived(dst, recv_sem):
    pltpu.make_async_copy(dst, dst, recv_sem).wait()


CHUNKS = 4


def gather_kernel(
    feats, cot, weight, gathered, cots, ws, own, own_w, own_c,
    send_sems, recv_sems, cot_recv, w_recv, w_sib, local_sems,
):
    here = Place()
    step = feats.shape[0] // CHUNKS
    piece = cot.shape[0] // N_REP
    half = weight.shape[0] // 2
    peers = [here.peer(d) for d in range(1, N_REP)]
    sib = here.at(False, 0, True)
    up, down, across = here.at(False, 1), here.at(False, -1), here.at(True, 0)

    loads = [
        pltpu.make_async_copy(feats, own, local_sems.at[0]),
        pltpu.make_async_copy(weight, own_w, local_sems.at[1]),
        pltpu.make_async_copy(
            cot.at[pl.ds(pl.multiple_of(here.rep * piece, piece), piece)], own_c, local_sems.at[2]
        ),
    ]
    for load in loads:
        load.start()
    greet([sib, up, down, across] + [(here.row, q) for q in peers])

    send = Sends(send_sems)

    def rows(chunk):
        return pl.ds(chunk * step, step)

    def place(slot, chunk):
        return gathered.at[slot, rows(chunk)]

    slots = [
        here.slot(False, -1), here.slot(False, 1), here.slot(False, 2), here.slot(True, 0),
        here.slot(True, -1), here.slot(True, 1), here.slot(True, 2),
    ]

    def launch(src_of, slot, order, base, to_x, sib_kind):
        for i in range(CHUNKS):
            if to_x:
                send(src_of(i), place(slot, i), recv_sems.at[3, i], across)
        for i in range(CHUNKS):
            a, b = i, (i + CHUNKS // 2) % CHUNKS
            send(src_of(a), place(slot, a), recv_sems.at[base, a], up)
            send(src_of(b), place(slot, b), recv_sems.at[base + 1, b], down)
        for i in range(CHUNKS):
            send(src_of(i), place(slot, i), recv_sems.at[sib_kind, i], sib)

    launch(lambda i: feats.at[rows(i)], here.row, None, 0, True, 7)

    mine = pl.ds(pl.multiple_of(here.c * half, half), half)
    for d in range(1, N_REP):
        q = peers[d - 1]
        send(weight.at[mine], ws.at[here.rep, mine], w_recv.at[d - 1], (here.row, q))
    for d in range(1, N_REP):
        q = peers[d - 1]
        send(
            cot.at[pl.ds(pl.multiple_of(q * piece, piece), piece)],
            cots.at[here.rep], cot_recv.at[d - 1], (here.row, q),
        )

    stores = [
        pltpu.make_async_copy(own, gathered.at[here.row], local_sems.at[3]),
        pltpu.make_async_copy(own_w, ws.at[here.rep], local_sems.at[4]),
        pltpu.make_async_copy(own_c, cots.at[here.rep], local_sems.at[5]),
    ]
    for load, store in zip(loads, stores):
        load.wait()
        store.start()

    def take(kind, chunk, to_up, to_down):
        slot = slots[kind]
        arrived(place(slot, chunk), recv_sems.at[kind, chunk])
        far = 2 if kind < 3 else 6
        if to_up:
            send(place(slot, chunk), place(slot, chunk), recv_sems.at[far, chunk], up)
        if to_down:
            send(place(slot, chunk), place(slot, chunk), recv_sems.at[far, chunk], down)
        send(place(slot, chunk), place(slot, chunk), recv_sems.at[8 + kind, chunk], sib)

    for base in (0, 4):
        for i in range(CHUNKS):
            a, b = i, (i + CHUNKS // 2) % CHUNKS
            take(base, a, a < CHUNKS // 2, False)
            take(base + 1, b, False, b >= CHUNKS // 2)
            if base == 0:
                arrived(place(slots[3], i), recv_sems.at[3, i])
                src = place(slots[3], i)
                send(src, src, recv_sems.at[4, i], up)
                send(src, src, recv_sems.at[5, i], down)
                send(src, src, recv_sems.at[11, i], sib)
        for i in range(CHUNKS):
            take(2 if base == 0 else 6, i, False, False)
        if base == 0:
            for d in range(1, N_REP):
                q = peers[d - 1]
                arrived(ws.at[q, mine], w_recv.at[d - 1])
                send(ws.at[q, mine], ws.at[q, mine], w_sib.at[d - 1], sib)

    theirs = pl.ds(pl.multiple_of((1 - here.c) * half, half), half)
    for d in range(1, N_REP):
        q = peers[d - 1]
        arrived(ws.at[q, theirs], w_sib.at[d - 1])
        arrived(cots.at[q], cot_recv.at[d - 1])
    sib_slots = [here.slot(False, 0, True)] + [
        here.slot(other, dy, True)
        for other, dy in ((False, -1), (False, 1), (False, 2), (True, 0), (True, -1), (True, 1), (True, 2))
    ]
    for kind in range(8):
        for i in range(CHUNKS):
            arrived(place(sib_slots[kind], i), recv_sems.at[7 + kind, i])
    for store in stores:
        store.wait()
    send.finish()


def gather_all(features, cotangent, weight):
    rows, width = features.shape
    n_sends = 15 * CHUNKS + 21
    return pl.pallas_call(
        gather_kernel,
        in_specs=[ANY] * 3,
        out_specs=[ANY] * 3,
        out_shape=[
            jax.ShapeDtypeStruct((N_ROW, rows, width), BF16),
            jax.ShapeDtypeStruct((N_REP, rows // N_REP, width), BF16),
            jax.ShapeDtypeStruct((N_REP,) + weight.shape, BF16),
        ],
        scratch_shapes=[
            pltpu.VMEM((rows, width), BF16),
            pltpu.VMEM(weight.shape, BF16),
            pltpu.VMEM((rows // N_REP, width), BF16),
            pltpu.SemaphoreType.DMA((n_sends,)),
            pltpu.SemaphoreType.DMA((15, CHUNKS)),
            pltpu.SemaphoreType.DMA((N_REP - 1,)),
            pltpu.SemaphoreType.DMA((N_REP - 1,)),
            pltpu.SemaphoreType.DMA((N_REP - 1,)),
            pltpu.SemaphoreType.DMA((6,)),
        ],
        compiler_params=pltpu.CompilerParams(collective_id=0, has_side_effects=True),
        name="gather_all",
    )(features, cotangent, weight)


STRIP = 128


def dense_kernel(
    mixed, cots, ws, mixed_grad, act, wgrad, m, w, cot, grad, back,
    send_sems, m_recv, back_recv, local_sems,
):
    here = Place()
    piece, width = mixed.shape[1:]
    peers = [here.peer(d) for d in range(1, N_REP)]
    first = pltpu.make_async_copy(mixed.at[here.rep], m.at[here.rep], local_sems.at[0])
    first.start()
    loads = []
    for r in range(N_REP):
        at = pl.ds(r * width, width)
        loads.append(pltpu.make_async_copy(ws.at[r], w.at[:, at], local_sems.at[1 + r]))
        loads.append(pltpu.make_async_copy(cots.at[r], cot.at[:, at], local_sems.at[9 + r]))
    greet([(here.row, q) for q in peers])
    send = Sends(send_sems)
    for d, q in enumerate(peers):
        send(mixed.at[q], m.at[here.rep], m_recv.at[d], (here.row, q))
    for load in loads:
        load.start()
    for load in loads:
        load.wait()
    first.wait()
    for d, q in enumerate(peers):
        arrived(m.at[q], m_recv.at[d])

    for i in range(piece // STRIP):
        rows = pl.ds(i * STRIP, STRIP)
        x = jnp.concatenate([m[r, rows, :] for r in range(N_REP)], axis=1)
        pre = jnp.dot(x, w[...], preferred_element_type=F32)
        sig = jax.nn.sigmoid(pre)
        out = (pre * sig).astype(BF16)
        g = (cot[rows, :].astype(F32) * sig * (1.0 + pre * (1.0 - sig))).astype(BF16)
        grad[rows, :] = g
        b = lax.dot_general(
            g, w[...], (((1,), (1,)), ((), ())), preferred_element_type=F32
        ).astype(BF16)
        for r in range(N_REP):
            act[r, rows, :] = out[:, r * width : (r + 1) * width]
            back[r, rows, :] = b[:, r * width : (r + 1) * width]
        for d, q in enumerate(peers):
            send(
                back.at[q, rows], mixed_grad.at[here.rep, rows], back_recv.at[d, i],
                (here.row, q),
            )
    last = pltpu.make_async_copy(back.at[here.rep], mixed_grad.at[here.rep], local_sems.at[0])
    last.start()
    for r in range(N_REP):
        wgrad[r] = lax.dot_general(
            m[r], grad[...], (((0,), (0,)), ((), ())), preferred_element_type=F32
        ).astype(BF16)
    last.wait()
    for d, q in enumerate(peers):
        for i in range(piece // STRIP):
            arrived(mixed_grad.at[q, pl.ds(i * STRIP, STRIP)], back_recv.at[d, i])
    send.finish()


def dense(mixed, cots, ws):
    n, piece, width = mixed.shape
    strips = piece // STRIP
    return pl.pallas_call(
        dense_kernel,
        in_specs=[ANY] * 3,
        out_specs=[ANY, VM, VM],
        out_shape=[
            jax.ShapeDtypeStruct(mixed.shape, BF16),
            jax.ShapeDtypeStruct(mixed.shape, BF16),
            jax.ShapeDtypeStruct((n, width, n * width), BF16),
        ],
        scratch_shapes=[
            pltpu.VMEM((n, piece, width), BF16),
            pltpu.VMEM((n * width, n * width), BF16),
            pltpu.VMEM((piece, n * width), BF16),
            pltpu.VMEM((piece, n * width), BF16),
            pltpu.VMEM((n, piece, width), BF16),
            pltpu.SemaphoreType.DMA(((n - 1) * (1 + strips),)),
            pltpu.SemaphoreType.DMA((n - 1,)),
            pltpu.SemaphoreType.DMA((n - 1, strips)),
            pltpu.SemaphoreType.DMA((17,)),
        ],
        compiler_params=pltpu.CompilerParams(collective_id=1, has_side_effects=True),
        name="dense",
    )(mixed, cots, ws)


OFFSETS = (2, 1, -1, 0)
SUM_ROWS = 128


def reduce_kernel(
    part, act, wgrad, act_out, out, wg_out,
    own, theirs, far_up, far_down, near_up, near_down, cross, own_act,
    wg_in, wg_sum, wg_sib, wg_half, wg_row, wg_fin, wg_fin_sib,
    send_sems, load_sems, sib_recv, far_recv, near_recv, cross_recv,
    act_recv, wg_recv, row_recv, pair_recv, local_sems,
):
    here = Place()
    step = own.shape[1] // CHUNKS
    half = CHUNKS // 2
    peers = [here.peer(d) for d in range(1, N_REP)]
    sib = here.at(False, 0, True)
    up, down, across = here.at(False, 1), here.at(False, -1), here.at(True, 0)
    columns = [(o, dy) for o in (True, False) for dy in OFFSETS][:-1]

    def rows(i):
        return pl.ds(i * step, step)

    loads = {}
    for r in range(8):
        slot = here.slot(r < 4, OFFSETS[r % 4])
        for i in range(CHUNKS):
            loads[r, i] = pltpu.make_async_copy(
                part.at[slot, rows(i)], own.at[r, rows(i)], load_sems.at[r, i]
            )
    extra = [
        pltpu.make_async_copy(act.at[here.rep], own_act, local_sems.at[0]),
        pltpu.make_async_copy(wgrad.at[here.rep], wg_in.at[N_REP - 1], local_sems.at[1]),
    ]
    for load in extra:
        load.start()
    for load in loads.values():
        load.start()
    greet([sib] + [here.at(*column) for column in columns] + [(here.row, q) for q in peers])

    send = Sends(send_sems)
    order = [0, 4, 1, 2, 3, 5, 6, 7]
    for r in order:
        slot = here.slot(r < 4, OFFSETS[r % 4], True)
        for i in range(CHUNKS):
            send(part.at[slot, rows(i)], theirs.at[r, rows(i)], sib_recv.at[r, i], sib)

    def total(r, i, more, dst=None):
        loads[r, i].wait()
        arrived(theirs.at[r, rows(i)], sib_recv.at[r, i])
        target = own.at[r] if dst is None else dst

        @pl.loop(0, step // SUM_ROWS)
        def _(j):
            at = pl.ds(pl.multiple_of(i * step + j * SUM_ROWS, SUM_ROWS), SUM_ROWS)
            acc = own[r, at, :].astype(F32) + theirs[r, at, :].astype(F32)
            for ref, base in more:
                at2 = pl.ds(pl.multiple_of(base * step + j * SUM_ROWS, SUM_ROWS), SUM_ROWS)
                acc = acc + ref[at2, :].astype(F32)
            target[at, :] = acc.astype(BF16)

    def far(hh):
        for i in range(half):
            total(4 * hh, i, [])
            send(own.at[4 * hh, rows(i)], far_up.at[hh, rows(i)], far_recv.at[hh, 0, i], up)
            total(4 * hh, i + half, [])
            send(
                own.at[4 * hh, rows(i + half)], far_down.at[hh, rows(i)],
                far_recv.at[hh, 1, i], down,
            )

    def near(hh, i, j, up_more, down_more):
        r, s = 4 * hh + 1, 4 * hh + 2
        total(r, i, up_more)
        send(own.at[r, rows(i)], near_up.at[hh, rows(i)], near_recv.at[hh, 0, i], up)
        total(s, j, down_more)
        send(own.at[s, rows(j)], near_down.at[hh, rows(j)], near_recv.at[hh, 1, j], down)

    def near_first(hh):
        for i in range(half):
            near(hh, i + half, i, [], [])

    def near_last(hh):
        for i in range(half):
            arrived(far_up.at[hh, rows(i)], far_recv.at[hh, 0, i])
            arrived(far_down.at[hh, rows(i)], far_recv.at[hh, 1, i])
            near(hh, i, i + half, [(far_up.at[hh], i)], [(far_down.at[hh], i)])

    def final(hh):
        for i in (0, 2, 1, 3):
            arrived(near_up.at[hh, rows(i)], near_recv.at[hh, 0, i])
            arrived(near_down.at[hh, rows(i)], near_recv.at[hh, 1, i])
            more = [(near_up.at[hh], i), (near_down.at[hh], i)]
            if hh == 0:
                total(3, i, more)
                send(own.at[3, rows(i)], cross.at[rows(i)], cross_recv.at[i], across)
            else:
                arrived(cross.at[rows(i)], cross_recv.at[i])
                total(7, i, more + [(cross, i)], out)

    far(0)
    for d, q in enumerate(peers):
        send(wgrad.at[q], wg_in.at[d], wg_recv.at[d], (here.row, q))
    for d, q in enumerate(peers):
        send(act.at[q], act_out.at[here.rep], act_recv.at[d], (here.row, q))
    extra[0].wait()
    keep = pltpu.make_async_copy(own_act, act_out.at[here.rep], local_sems.at[0])
    keep.start()
    near_first(0)
    far(1)
    near_last(0)
    near_first(1)
    final(0)

    extra[1].wait()
    for d in range(N_REP - 1):
        arrived(wg_in.at[d], wg_recv.at[d])
    wide = wg_in.shape[2]
    edge = wg_half.shape[1]

    @pl.loop(0, wide // 128)
    def _(j):
        at = pl.ds(pl.multiple_of(j * 128, 128), 128)
        acc = wg_in[0, :, at].astype(F32)
        for d in range(1, N_REP):
            acc = acc + wg_in[d, :, at].astype(F32)
        acc = acc.astype(BF16)
        wg_sum[0, j] = acc[:edge]
        wg_sum[1, j] = acc[edge:]

    send(wg_sum.at[1 - here.c], wg_sib, pair_recv.at[0], sib)
    near_last(1)
    arrived(wg_sib, pair_recv.at[0])

    @pl.loop(0, wide // 128)
    def _(j):
        wg_half[j] = (wg_sum[here.c, j].astype(F32) + wg_sib[j].astype(F32)).astype(BF16)

    for k, (o, dy) in enumerate(columns):
        send(
            wg_half.at[here.slot(o, dy) // 2], wg_row.at[k], row_recv.at[k], here.at(o, dy)
        )
    for k in range(len(columns)):
        arrived(wg_row.at[k], row_recv.at[k])
    acc = wg_half[here.row // 2].astype(F32)
    for k in range(len(columns)):
        acc = acc + wg_row[k].astype(F32)
    wg_fin[...] = acc
    send(wg_fin, wg_fin_sib, pair_recv.at[1], sib)
    final(1)
    arrived(wg_fin_sib, pair_recv.at[1])

    @pl.when(here.c == 0)
    def _():
        wg_out[:edge, :] = wg_fin[:, :edge]
        wg_out[edge:, :] = wg_fin_sib[:, :edge]

    @pl.when(here.c == 1)
    def _():
        wg_out[:edge, :] = wg_fin_sib[:, edge:]
        wg_out[edge:, :] = wg_fin[:, edge:]

    keep.wait()
    for d, q in enumerate(peers):
        arrived(act_out.at[q], act_recv.at[d])
    send.finish()


def reduce_all(part, act, wgrad):
    n, rows, width = part.shape
    n_rep, k, wide = wgrad.shape
    edge = k // 2
    dma = pltpu.SemaphoreType.DMA
    return pl.pallas_call(
        reduce_kernel,
        in_specs=[ANY] * 3,
        out_specs=[ANY, VM, VM],
        out_shape=[
            jax.ShapeDtypeStruct(act.shape, BF16),
            jax.ShapeDtypeStruct((rows, width), BF16),
            jax.ShapeDtypeStruct((k, wide // n), F32),
        ],
        scratch_shapes=[
            pltpu.VMEM((8, rows, width), BF16),
            pltpu.VMEM((8, rows, width), BF16),
            pltpu.VMEM((2, rows // 2, width), BF16),
            pltpu.VMEM((2, rows // 2, width), BF16),
            pltpu.VMEM((2, rows, width), BF16),
            pltpu.VMEM((2, rows, width), BF16),
            pltpu.VMEM((rows, width), BF16),
            pltpu.VMEM(act.shape[1:], BF16),
            pltpu.VMEM(wgrad.shape, BF16),
            pltpu.VMEM((2, wide // 128, edge, 128), BF16),
            pltpu.VMEM((wide // 128, edge, 128), BF16),
            pltpu.VMEM((wide // 128, edge, 128), BF16),
            pltpu.VMEM((7, edge, 128), BF16),
            pltpu.VMEM((edge, 128), F32),
            pltpu.VMEM((edge, 128), F32),
            dma((83,)), dma((8, CHUNKS)), dma((8, CHUNKS)), dma((2, 2, 2)), dma((2, 2, CHUNKS)),
            dma((CHUNKS,)), dma((7,)), dma((7,)), dma((7,)), dma((2,)), dma((2,)),
        ],
        compiler_params=pltpu.CompilerParams(collective_id=2, has_side_effects=True),
        name="reduce_all",
    )(part, act, wgrad)


SLOTS_AHEAD = 4


def fwd_kernel(cols, counts, tiles, gathered, out, tbuf, gbuf, sems):
    blocks, slots, t, _ = tiles.shape

    def copies(b, k):
        s = lax.rem(b, SLOTS_AHEAD)
        at = pl.ds(pl.multiple_of(k * t, t), t)
        return (
            pltpu.make_async_copy(tiles.at[b, k], tbuf.at[s, :, at], sems.at[s, k, 0]),
            pltpu.make_async_copy(gathered.at[cols[b, k]], gbuf.at[s, at, :], sems.at[s, k, 1]),
        )

    def start(b):
        @pl.loop(0, counts[b])
        def _(k):
            for c in copies(b, k):
                c.start()

    for b in range(SLOTS_AHEAD - 1):
        start(b)

    @pl.loop(0, blocks)
    def _(b):
        s = lax.rem(b, SLOTS_AHEAD)

        @pl.when(b + SLOTS_AHEAD - 1 < blocks)
        def _():
            start(b + SLOTS_AHEAD - 1)

        n = counts[b]

        @pl.loop(0, n)
        def _(k):
            for c in copies(b, k):
                c.wait()

        @pl.when(lax.rem(n, 2) == 1)
        def _():
            at = pl.ds(pl.multiple_of(n * t, t), t)
            tbuf[s, :, at] = jnp.zeros((t, t), BF16)
            gbuf[s, at, :] = jnp.zeros((t, t), BF16)

        row = pl.ds(pl.multiple_of(b * t, t), t)
        for p in range(1, slots // 2 + 1):

            @pl.when((n + 1) // 2 == p)
            def _():
                w = 2 * p * t
                out[row, :] = jnp.dot(
                    tbuf[s, :, :w], gbuf[s, :w, :], preferred_element_type=F32
                ).astype(BF16)


def spmm(gathered, tiles, columns, counts):
    blocks, slots, t, _ = tiles.shape
    width = gathered.shape[-1]
    return pl.pallas_call(
        fwd_kernel,
        grid_spec=pltpu.PrefetchScalarGridSpec(
            num_scalar_prefetch=2,
            grid=(1,),
            in_specs=[pl.BlockSpec(memory_space=pl.ANY)] * 2,
            out_specs=pl.BlockSpec((blocks * t, width), lambda i, *_: (0, 0)),
            scratch_shapes=[
                pltpu.VMEM((SLOTS_AHEAD, t, slots * t), BF16),
                pltpu.VMEM((SLOTS_AHEAD, slots * t, width), BF16),
                pltpu.SemaphoreType.DMA((SLOTS_AHEAD, slots, 2)),
            ],
        ),
        out_shape=jax.ShapeDtypeStruct((blocks * t, width), BF16),
        name="spmm",
    )(columns, counts, tiles, gathered)


GROUP = 4
OUT_CHUNK = 16


def bwd_kernel(cols, counts, tiles, grad, out, acc, tbuf, stage, sems, out_sems):
    blocks, slots, t, _ = tiles.shape
    total = acc.shape[0]

    def copy(b, k):
        s = lax.rem(b, SLOTS_AHEAD)
        return pltpu.make_async_copy(tiles.at[b, k], tbuf.at[s, k], sems.at[s, k])

    def start(b):
        @pl.loop(0, counts[b])
        def _(k):
            copy(b, k).start()

    for b in range(SLOTS_AHEAD - 1):
        start(b)

    @pl.loop(0, total)
    def _(j):
        acc[j] = jnp.zeros(acc.shape[1:], F32)

    @pl.loop(0, blocks)
    def _(b):
        s = lax.rem(b, SLOTS_AHEAD)

        @pl.when(b + SLOTS_AHEAD - 1 < blocks)
        def _():
            start(b + SLOTS_AHEAD - 1)

        n = counts[b]

        @pl.loop(0, n)
        def _(k):
            copy(b, k).wait()

        g = grad[pl.ds(pl.multiple_of(b * t, t), t), :]

        @pl.loop(0, (n + GROUP - 1) // GROUP)
        def _(q):
            terms = []
            for i in range(GROUP):
                k = q * GROUP + i
                term = lax.dot_general(
                    tbuf[s, k], g, (((0,), (0,)), ((), ())), preferred_element_type=F32
                )
                terms.append(jnp.where(k < n, term, 0.0))
            for i in range(GROUP):
                acc[cols[b, q * GROUP + i]] += terms[i]

    def flush(c):
        s = lax.rem(c, 2)
        return pltpu.make_async_copy(
            stage.at[s], out.at[pl.ds(c * OUT_CHUNK, OUT_CHUNK)], out_sems.at[s]
        )

    @pl.loop(0, total // OUT_CHUNK)
    def _(c):
        s = lax.rem(c, 2)

        @pl.when(c >= 2)
        def _():
            flush(c - 2).wait()

        @pl.loop(0, OUT_CHUNK)
        def _(j):
            stage[s, j] = acc[c * OUT_CHUNK + j].astype(BF16)

        flush(c).start()

    for c in (total // OUT_CHUNK - 2, total // OUT_CHUNK - 1):
        flush(c).wait()


def spmm_t(grad, tiles, columns, counts, total):
    blocks, slots, t, _ = tiles.shape
    width = grad.shape[-1]
    return pl.pallas_call(
        bwd_kernel,
        grid_spec=pltpu.PrefetchScalarGridSpec(
            num_scalar_prefetch=2,
            grid=(1,),
            in_specs=[
                pl.BlockSpec(memory_space=pl.ANY),
                pl.BlockSpec((blocks * t, width), lambda i, *_: (0, 0)),
            ],
            out_specs=pl.BlockSpec(memory_space=pl.ANY),
            scratch_shapes=[
                pltpu.VMEM((total, t, width), F32),
                pltpu.VMEM((SLOTS_AHEAD, slots, t, t), BF16),
                pltpu.VMEM((2, OUT_CHUNK, t, width), BF16),
                pltpu.SemaphoreType.DMA((SLOTS_AHEAD, slots)),
                pltpu.SemaphoreType.DMA((2,)),
            ],
        ),
        out_shape=jax.ShapeDtypeStruct((total, t, width), BF16),
        compiler_params=pltpu.CompilerParams(vmem_limit_bytes=60 * 1024 * 1024),
        name="spmm_t",
    )(columns, counts, tiles, grad)


def local(features, tiles, columns, counts, weight, cotangent):
    rows_here, feat_local = features.shape
    blocks_here, slots, t, _ = tiles.shape
    total_blocks = blocks_here * lax.axis_size("row")
    gathered, cots, ws = gather_all(features, cotangent, weight)
    mixed = spmm(gathered.reshape(total_blocks, t, feat_local), tiles, columns, counts)
    mixed_grad, act, wgrad = dense(mixed.reshape(N_REP, -1, feat_local), cots, ws)
    part = spmm_t(mixed_grad.reshape(mixed.shape), tiles, columns, counts, total_blocks)
    act, feature_grad, weight_grad = reduce_all(
        part.reshape(N_ROW, rows_here, feat_local), act, wgrad
    )
    return act.reshape(features.shape), feature_grad, weight_grad


def solution(mesh):
    in_specs = (
        P("row", "rep"),
        P("row", None, None, None),
        P("row", None),
        P("row"),
        P(None, "rep"),
        P("row", "rep"),
    )
    out_specs = (P("row", "rep"), P("row", "rep"), P("rep", "row"))
    return jax.shard_map(local, mesh=mesh, in_specs=in_specs, out_specs=out_specs, check_vma=False)
```

```python
import functools

import jax
import jax.numpy as jnp
from jax import lax
from jax.experimental import pallas as pl
from jax.experimental.pallas import tpu as pltpu
from jax.sharding import PartitionSpec as P

F32 = jnp.float32
BF16 = jnp.bfloat16
MESH = pl.DeviceIdType.MESH
ROWS_Y = 4
N_ROW = 16
N_REP = 8
ANY = pl.BlockSpec(memory_space=pl.ANY)
VM = pl.BlockSpec(memory_space=pltpu.VMEM)


class Place:
    def __init__(self):
        self.row = lax.axis_index("row")
        self.rep = lax.axis_index("rep")
        self.c = lax.rem(self.row, 2)
        self.y = lax.rem(self.row // 2, ROWS_Y)
        self.h = self.row // (2 * ROWS_Y)

    def slot(self, other, dy, sib=False):
        h = 1 - self.h if other else self.h
        c = 1 - self.c if sib else self.c
        return (h * ROWS_Y + lax.rem(self.y + dy + ROWS_Y, ROWS_Y)) * 2 + c

    def at(self, other, dy, sib=False):
        return (self.slot(other, dy, sib), self.rep)

    def peer(self, d):
        x, z = self.rep // 4, lax.rem(self.rep, 4)
        if d >= 4:
            x = 1 - x
        if d % 4 == 1:
            z = z + 1 - 2 * lax.rem(z, 2)
        elif d % 4 == 2:
            z = lax.rem(z + 2, 4)
        elif d % 4 == 3:
            z = 3 - z
        return x * 4 + z


def greet(partners):
    barrier = pltpu.get_barrier_semaphore()
    for partner in partners:
        pl.semaphore_signal(barrier, inc=1, device_id=partner, device_id_type=MESH)
    pl.semaphore_wait(barrier, len(partners))


class Sends:
    def __init__(self, sems):
        self.sems, self.live = sems, []

    def __call__(self, src, dst, recv_sem, device):
        copy = pltpu.make_async_remote_copy(
            src_ref=src,
            dst_ref=dst,
            send_sem=self.sems.at[len(self.live)],
            recv_sem=recv_sem,
            device_id=device,
            device_id_type=MESH,
        )
        copy.start()
        self.live.append(copy)

    def finish(self):
        for copy in self.live:
            copy.wait_send()


def arrived(dst, recv_sem):
    pltpu.make_async_copy(dst, dst, recv_sem).wait()


CHUNKS = 8


def gather_kernel(
    feats, cot, weight, gathered, cots, ws, own, own_w, own_c,
    send_sems, recv_sems, cot_recv, w_recv, w_sib, local_sems,
):
    here = Place()
    step = feats.shape[0] // CHUNKS
    piece = cot.shape[0] // N_REP
    half = weight.shape[0] // 2
    peers = [here.peer(d) for d in range(1, N_REP)]
    sib = here.at(False, 0, True)
    up, down, across = here.at(False, 1), here.at(False, -1), here.at(True, 0)

    loads = [
        pltpu.make_async_copy(feats, own, local_sems.at[0]),
        pltpu.make_async_copy(weight, own_w, local_sems.at[1]),
        pltpu.make_async_copy(
            cot.at[pl.ds(pl.multiple_of(here.rep * piece, piece), piece)], own_c, local_sems.at[2]
        ),
    ]
    for load in loads:
        load.start()
    greet([sib, up, down, across] + [(here.row, q) for q in peers])

    send = Sends(send_sems)

    def rows(chunk):
        return pl.ds(chunk * step, step)

    def place(slot, chunk):
        return gathered.at[slot, rows(chunk)]

    slots = [
        here.slot(False, -1), here.slot(False, 1), here.slot(False, 2), here.slot(True, 0),
        here.slot(True, -1), here.slot(True, 1), here.slot(True, 2),
    ]

    def launch(src_of, slot, order, base, to_x, sib_kind):
        for i in range(CHUNKS):
            if to_x:
                send(src_of(i), place(slot, i), recv_sems.at[3, i], across)
        for i in range(CHUNKS):
            a, b = i, (i + CHUNKS // 2) % CHUNKS
            send(src_of(a), place(slot, a), recv_sems.at[base, a], up)
            send(src_of(b), place(slot, b), recv_sems.at[base + 1, b], down)
        for i in range(CHUNKS):
            send(src_of(i), place(slot, i), recv_sems.at[sib_kind, i], sib)

    launch(lambda i: feats.at[rows(i)], here.row, None, 0, True, 7)

    mine = pl.ds(pl.multiple_of(here.c * half, half), half)
    for d in range(1, N_REP):
        q = peers[d - 1]
        send(weight.at[mine], ws.at[here.rep, mine], w_recv.at[d - 1], (here.row, q))
    for d in range(1, N_REP):
        q = peers[d - 1]
        send(
            cot.at[pl.ds(pl.multiple_of(q * piece, piece), piece)],
            cots.at[here.rep], cot_recv.at[d - 1], (here.row, q),
        )

    stores = [
        pltpu.make_async_copy(own, gathered.at[here.row], local_sems.at[3]),
        pltpu.make_async_copy(own_w, ws.at[here.rep], local_sems.at[4]),
        pltpu.make_async_copy(own_c, cots.at[here.rep], local_sems.at[5]),
    ]
    for load, store in zip(loads, stores):
        load.wait()
        store.start()

    def take(kind, chunk, to_up, to_down):
        slot = slots[kind]
        arrived(place(slot, chunk), recv_sems.at[kind, chunk])
        far = 2 if kind < 3 else 6
        if to_up:
            send(place(slot, chunk), place(slot, chunk), recv_sems.at[far, chunk], up)
        if to_down:
            send(place(slot, chunk), place(slot, chunk), recv_sems.at[far, chunk], down)
        send(place(slot, chunk), place(slot, chunk), recv_sems.at[8 + kind, chunk], sib)

    for base in (0, 4):
        for i in range(CHUNKS):
            a, b = i, (i + CHUNKS // 2) % CHUNKS
            take(base, a, a < CHUNKS // 2, False)
            take(base + 1, b, False, b >= CHUNKS // 2)
            if base == 0:
                arrived(place(slots[3], i), recv_sems.at[3, i])
                src = place(slots[3], i)
                send(src, src, recv_sems.at[4, i], up)
                send(src, src, recv_sems.at[5, i], down)
                send(src, src, recv_sems.at[11, i], sib)
        for i in range(CHUNKS):
            take(2 if base == 0 else 6, i, False, False)
        if base == 0:
            for d in range(1, N_REP):
                q = peers[d - 1]
                arrived(ws.at[q, mine], w_recv.at[d - 1])
                send(ws.at[q, mine], ws.at[q, mine], w_sib.at[d - 1], sib)

    theirs = pl.ds(pl.multiple_of((1 - here.c) * half, half), half)
    for d in range(1, N_REP):
        q = peers[d - 1]
        arrived(ws.at[q, theirs], w_sib.at[d - 1])
        arrived(cots.at[q], cot_recv.at[d - 1])
    sib_slots = [here.slot(False, 0, True)] + [
        here.slot(other, dy, True)
        for other, dy in ((False, -1), (False, 1), (False, 2), (True, 0), (True, -1), (True, 1), (True, 2))
    ]
    for kind in range(8):
        for i in range(CHUNKS):
            arrived(place(sib_slots[kind], i), recv_sems.at[7 + kind, i])
    for store in stores:
        store.wait()
    send.finish()


def gather_all(features, cotangent, weight):
    rows, width = features.shape
    n_sends = 15 * CHUNKS + 21
    return pl.pallas_call(
        gather_kernel,
        in_specs=[ANY] * 3,
        out_specs=[ANY] * 3,
        out_shape=[
            jax.ShapeDtypeStruct((N_ROW, rows, width), BF16),
            jax.ShapeDtypeStruct((N_REP, rows // N_REP, width), BF16),
            jax.ShapeDtypeStruct((N_REP,) + weight.shape, BF16),
        ],
        scratch_shapes=[
            pltpu.VMEM((rows, width), BF16),
            pltpu.VMEM(weight.shape, BF16),
            pltpu.VMEM((rows // N_REP, width), BF16),
            pltpu.SemaphoreType.DMA((n_sends,)),
            pltpu.SemaphoreType.DMA((15, CHUNKS)),
            pltpu.SemaphoreType.DMA((N_REP - 1,)),
            pltpu.SemaphoreType.DMA((N_REP - 1,)),
            pltpu.SemaphoreType.DMA((N_REP - 1,)),
            pltpu.SemaphoreType.DMA((6,)),
        ],
        compiler_params=pltpu.CompilerParams(collective_id=0, has_side_effects=True),
        name="gather_all",
    )(features, cotangent, weight)


STRIP = 128


def dense_kernel(
    mixed, cots, ws, mixed_grad, act, wgrad, m, w, cot, grad, back,
    send_sems, m_recv, back_recv, local_sems,
):
    here = Place()
    piece, width = mixed.shape[1:]
    peers = [here.peer(d) for d in range(1, N_REP)]
    first = pltpu.make_async_copy(mixed.at[here.rep], m.at[here.rep], local_sems.at[0])
    first.start()
    loads = []
    for r in range(N_REP):
        at = pl.ds(r * width, width)
        loads.append(pltpu.make_async_copy(ws.at[r], w.at[:, at], local_sems.at[1 + r]))
        loads.append(pltpu.make_async_copy(cots.at[r], cot.at[:, at], local_sems.at[9 + r]))
    greet([(here.row, q) for q in peers])
    send = Sends(send_sems)
    for d, q in enumerate(peers):
        send(mixed.at[q], m.at[here.rep], m_recv.at[d], (here.row, q))
    for load in loads:
        load.start()
    for load in loads:
        load.wait()
    first.wait()
    for d, q in enumerate(peers):
        arrived(m.at[q], m_recv.at[d])

    for i in range(piece // STRIP):
        rows = pl.ds(i * STRIP, STRIP)
        x = jnp.concatenate([m[r, rows, :] for r in range(N_REP)], axis=1)
        pre = jnp.dot(x, w[...], preferred_element_type=F32)
        sig = jax.nn.sigmoid(pre)
        out = (pre * sig).astype(BF16)
        g = (cot[rows, :].astype(F32) * sig * (1.0 + pre * (1.0 - sig))).astype(BF16)
        grad[rows, :] = g
        b = lax.dot_general(
            g, w[...], (((1,), (1,)), ((), ())), preferred_element_type=F32
        ).astype(BF16)
        for r in range(N_REP):
            act[r, rows, :] = out[:, r * width : (r + 1) * width]
            back[r, rows, :] = b[:, r * width : (r + 1) * width]
        for d, q in enumerate(peers):
            send(
                back.at[q, rows], mixed_grad.at[here.rep, rows], back_recv.at[d, i],
                (here.row, q),
            )
    last = pltpu.make_async_copy(back.at[here.rep], mixed_grad.at[here.rep], local_sems.at[0])
    last.start()
    for r in range(N_REP):
        wgrad[r] = lax.dot_general(
            m[r], grad[...], (((0,), (0,)), ((), ())), preferred_element_type=F32
        ).astype(BF16)
    last.wait()
    for d, q in enumerate(peers):
        for i in range(piece // STRIP):
            arrived(mixed_grad.at[q, pl.ds(i * STRIP, STRIP)], back_recv.at[d, i])
    send.finish()


def dense(mixed, cots, ws):
    n, piece, width = mixed.shape
    strips = piece // STRIP
    return pl.pallas_call(
        dense_kernel,
        in_specs=[ANY] * 3,
        out_specs=[ANY, VM, VM],
        out_shape=[
            jax.ShapeDtypeStruct(mixed.shape, BF16),
            jax.ShapeDtypeStruct(mixed.shape, BF16),
            jax.ShapeDtypeStruct((n, width, n * width), BF16),
        ],
        scratch_shapes=[
            pltpu.VMEM((n, piece, width), BF16),
            pltpu.VMEM((n * width, n * width), BF16),
            pltpu.VMEM((piece, n * width), BF16),
            pltpu.VMEM((piece, n * width), BF16),
            pltpu.VMEM((n, piece, width), BF16),
            pltpu.SemaphoreType.DMA(((n - 1) * (1 + strips),)),
            pltpu.SemaphoreType.DMA((n - 1,)),
            pltpu.SemaphoreType.DMA((n - 1, strips)),
            pltpu.SemaphoreType.DMA((17,)),
        ],
        compiler_params=pltpu.CompilerParams(collective_id=1, has_side_effects=True),
        name="dense",
    )(mixed, cots, ws)


OFFSETS = (2, 1, -1, 0)
SUM_ROWS = 128


def reduce_kernel(
    part, act, wgrad, act_out, out, wg_out,
    own, theirs, far_up, far_down, near_up, near_down, cross, own_act,
    wg_in, wg_sum, wg_sib, wg_half, wg_row, wg_fin, wg_fin_sib,
    send_sems, load_sems, sib_recv, far_recv, near_recv, cross_recv,
    act_recv, wg_recv, row_recv, pair_recv, local_sems,
):
    here = Place()
    step = own.shape[1] // CHUNKS
    half = CHUNKS // 2
    peers = [here.peer(d) for d in range(1, N_REP)]
    sib = here.at(False, 0, True)
    up, down, across = here.at(False, 1), here.at(False, -1), here.at(True, 0)
    columns = [(o, dy) for o in (True, False) for dy in OFFSETS][:-1]

    def rows(i):
        return pl.ds(i * step, step)

    loads = {}
    for r in range(8):
        slot = here.slot(r < 4, OFFSETS[r % 4])
        for i in range(CHUNKS):
            loads[r, i] = pltpu.make_async_copy(
                part.at[slot, rows(i)], own.at[r, rows(i)], load_sems.at[r, i]
            )
    extra = [
        pltpu.make_async_copy(act.at[here.rep], own_act, local_sems.at[0]),
        pltpu.make_async_copy(wgrad.at[here.rep], wg_in.at[N_REP - 1], local_sems.at[1]),
    ]
    for load in extra:
        load.start()
    for load in loads.values():
        load.start()
    greet([sib] + [here.at(*column) for column in columns] + [(here.row, q) for q in peers])

    send = Sends(send_sems)
    order = [0, 4, 1, 2, 3, 5, 6, 7]
    for r in order:
        slot = here.slot(r < 4, OFFSETS[r % 4], True)
        for i in range(CHUNKS):
            send(part.at[slot, rows(i)], theirs.at[r, rows(i)], sib_recv.at[r, i], sib)

    def total(r, i, more, dst=None):
        loads[r, i].wait()
        arrived(theirs.at[r, rows(i)], sib_recv.at[r, i])
        target = own.at[r] if dst is None else dst

        @pl.loop(0, step // SUM_ROWS)
        def _(j):
            at = pl.ds(pl.multiple_of(i * step + j * SUM_ROWS, SUM_ROWS), SUM_ROWS)
            acc = own[r, at, :].astype(F32) + theirs[r, at, :].astype(F32)
            for ref, base in more:
                at2 = pl.ds(pl.multiple_of(base * step + j * SUM_ROWS, SUM_ROWS), SUM_ROWS)
                acc = acc + ref[at2, :].astype(F32)
            target[at, :] = acc.astype(BF16)

    def far(hh):
        for i in range(half):
            total(4 * hh, i, [])
            send(own.at[4 * hh, rows(i)], far_up.at[hh, rows(i)], far_recv.at[hh, 0, i], up)
            total(4 * hh, i + half, [])
            send(
                own.at[4 * hh, rows(i + half)], far_down.at[hh, rows(i)],
                far_recv.at[hh, 1, i], down,
            )

    def near(hh, i, j, up_more, down_more):
        r, s = 4 * hh + 1, 4 * hh + 2
        total(r, i, up_more)
        send(own.at[r, rows(i)], near_up.at[hh, rows(i)], near_recv.at[hh, 0, i], up)
        total(s, j, down_more)
        send(own.at[s, rows(j)], near_down.at[hh, rows(j)], near_recv.at[hh, 1, j], down)

    def near_first(hh):
        for i in range(half):
            near(hh, i + half, i, [], [])

    def near_last(hh):
        for i in range(half):
            arrived(far_up.at[hh, rows(i)], far_recv.at[hh, 0, i])
            arrived(far_down.at[hh, rows(i)], far_recv.at[hh, 1, i])
            near(hh, i, i + half, [(far_up.at[hh], i)], [(far_down.at[hh], i)])

    def final(hh):
        for i in [k + part for k in range(half) for part in (0, half)]:
            arrived(near_up.at[hh, rows(i)], near_recv.at[hh, 0, i])
            arrived(near_down.at[hh, rows(i)], near_recv.at[hh, 1, i])
            more = [(near_up.at[hh], i), (near_down.at[hh], i)]
            if hh == 0:
                total(3, i, more)
                send(own.at[3, rows(i)], cross.at[rows(i)], cross_recv.at[i], across)
            else:
                arrived(cross.at[rows(i)], cross_recv.at[i])
                total(7, i, more + [(cross, i)], out)

    far(0)
    for d, q in enumerate(peers):
        send(wgrad.at[q], wg_in.at[d], wg_recv.at[d], (here.row, q))
    for d, q in enumerate(peers):
        send(act.at[q], act_out.at[here.rep], act_recv.at[d], (here.row, q))
    extra[0].wait()
    keep = pltpu.make_async_copy(own_act, act_out.at[here.rep], local_sems.at[0])
    keep.start()
    near_first(0)
    far(1)
    near_last(0)
    near_first(1)
    final(0)

    extra[1].wait()
    for d in range(N_REP - 1):
        arrived(wg_in.at[d], wg_recv.at[d])
    wide = wg_in.shape[2]
    edge = wg_half.shape[1]

    @pl.loop(0, wide // 128)
    def _(j):
        at = pl.ds(pl.multiple_of(j * 128, 128), 128)
        acc = wg_in[0, :, at].astype(F32)
        for d in range(1, N_REP):
            acc = acc + wg_in[d, :, at].astype(F32)
        acc = acc.astype(BF16)
        wg_sum[0, j] = acc[:edge]
        wg_sum[1, j] = acc[edge:]

    send(wg_sum.at[1 - here.c], wg_sib, pair_recv.at[0], sib)
    near_last(1)
    arrived(wg_sib, pair_recv.at[0])

    @pl.loop(0, wide // 128)
    def _(j):
        wg_half[j] = (wg_sum[here.c, j].astype(F32) + wg_sib[j].astype(F32)).astype(BF16)

    for k, (o, dy) in enumerate(columns):
        send(
            wg_half.at[here.slot(o, dy) // 2], wg_row.at[k], row_recv.at[k], here.at(o, dy)
        )
    for k in range(len(columns)):
        arrived(wg_row.at[k], row_recv.at[k])
    acc = wg_half[here.row // 2].astype(F32)
    for k in range(len(columns)):
        acc = acc + wg_row[k].astype(F32)
    wg_fin[...] = acc
    send(wg_fin, wg_fin_sib, pair_recv.at[1], sib)
    final(1)
    arrived(wg_fin_sib, pair_recv.at[1])

    @pl.when(here.c == 0)
    def _():
        wg_out[:edge, :] = wg_fin[:, :edge]
        wg_out[edge:, :] = wg_fin_sib[:, :edge]

    @pl.when(here.c == 1)
    def _():
        wg_out[:edge, :] = wg_fin_sib[:, edge:]
        wg_out[edge:, :] = wg_fin[:, edge:]

    keep.wait()
    for d, q in enumerate(peers):
        arrived(act_out.at[q], act_recv.at[d])
    send.finish()


def reduce_all(part, act, wgrad):
    n, rows, width = part.shape
    n_rep, k, wide = wgrad.shape
    edge = k // 2
    dma = pltpu.SemaphoreType.DMA
    return pl.pallas_call(
        reduce_kernel,
        in_specs=[ANY] * 3,
        out_specs=[ANY, VM, VM],
        out_shape=[
            jax.ShapeDtypeStruct(act.shape, BF16),
            jax.ShapeDtypeStruct((rows, width), BF16),
            jax.ShapeDtypeStruct((k, wide // n), F32),
        ],
        scratch_shapes=[
            pltpu.VMEM((8, rows, width), BF16),
            pltpu.VMEM((8, rows, width), BF16),
            pltpu.VMEM((2, rows // 2, width), BF16),
            pltpu.VMEM((2, rows // 2, width), BF16),
            pltpu.VMEM((2, rows, width), BF16),
            pltpu.VMEM((2, rows, width), BF16),
            pltpu.VMEM((rows, width), BF16),
            pltpu.VMEM(act.shape[1:], BF16),
            pltpu.VMEM(wgrad.shape, BF16),
            pltpu.VMEM((2, wide // 128, edge, 128), BF16),
            pltpu.VMEM((wide // 128, edge, 128), BF16),
            pltpu.VMEM((wide // 128, edge, 128), BF16),
            pltpu.VMEM((7, edge, 128), BF16),
            pltpu.VMEM((edge, 128), F32),
            pltpu.VMEM((edge, 128), F32),
            dma((15 * CHUNKS + 23,)), dma((8, CHUNKS)), dma((8, CHUNKS)), dma((2, 2, CHUNKS // 2)), dma((2, 2, CHUNKS)),
            dma((CHUNKS,)), dma((7,)), dma((7,)), dma((7,)), dma((2,)), dma((2,)),
        ],
        compiler_params=pltpu.CompilerParams(collective_id=2, has_side_effects=True),
        name="reduce_all",
    )(part, act, wgrad)


SLOTS_AHEAD = 4


def fwd_kernel(cols, counts, tiles, gathered, out, tbuf, gbuf, sems):
    blocks, slots, t, _ = tiles.shape

    def copies(b, k):
        s = lax.rem(b, SLOTS_AHEAD)
        at = pl.ds(pl.multiple_of(k * t, t), t)
        return (
            pltpu.make_async_copy(tiles.at[b, k], tbuf.at[s, :, at], sems.at[s, k, 0]),
            pltpu.make_async_copy(gathered.at[cols[k, b]], gbuf.at[s, at, :], sems.at[s, k, 1]),
        )

    def start(b):
        @pl.loop(0, counts[b])
        def _(k):
            for c in copies(b, k):
                c.start()

    for b in range(SLOTS_AHEAD - 1):
        start(b)

    @pl.loop(0, blocks)
    def _(b):
        s = lax.rem(b, SLOTS_AHEAD)

        @pl.when(b + SLOTS_AHEAD - 1 < blocks)
        def _():
            start(b + SLOTS_AHEAD - 1)

        n = counts[b]

        @pl.loop(0, n)
        def _(k):
            for c in copies(b, k):
                c.wait()

        @pl.when(lax.rem(n, 2) == 1)
        def _():
            at = pl.ds(pl.multiple_of(n * t, t), t)
            tbuf[s, :, at] = jnp.zeros((t, t), BF16)
            gbuf[s, at, :] = jnp.zeros((t, t), BF16)

        row = pl.ds(pl.multiple_of(b * t, t), t)
        for p in range(1, slots // 2 + 1):

            @pl.when((n + 1) // 2 == p)
            def _():
                w = 2 * p * t
                out[row, :] = jnp.dot(
                    tbuf[s, :, :w], gbuf[s, :w, :], preferred_element_type=F32
                ).astype(BF16)


def spmm(gathered, tiles, columns, counts):
    blocks, slots, t, _ = tiles.shape
    width = gathered.shape[-1]
    return pl.pallas_call(
        fwd_kernel,
        grid_spec=pltpu.PrefetchScalarGridSpec(
            num_scalar_prefetch=2,
            grid=(1,),
            in_specs=[pl.BlockSpec(memory_space=pl.ANY)] * 2,
            out_specs=pl.BlockSpec((blocks * t, width), lambda i, *_: (0, 0)),
            scratch_shapes=[
                pltpu.VMEM((SLOTS_AHEAD, t, slots * t), BF16),
                pltpu.VMEM((SLOTS_AHEAD, slots * t, width), BF16),
                pltpu.SemaphoreType.DMA((SLOTS_AHEAD, slots, 2)),
            ],
        ),
        out_shape=jax.ShapeDtypeStruct((blocks * t, width), BF16),
        name="spmm",
    )(columns, counts, tiles, gathered)


GROUP = 4
OUT_CHUNK = 16


def bwd_kernel(cols, counts, tiles, grad, out, acc, tbuf, stage, sems, out_sems):
    blocks, slots, t, _ = tiles.shape
    total = acc.shape[0]
    groups = slots // GROUP

    def copy(b, q):
        s = lax.rem(b, SLOTS_AHEAD)
        at = pl.ds(q * GROUP, GROUP)
        return pltpu.make_async_copy(tiles.at[b, at], tbuf.at[s, at], sems.at[s, q])

    def start(b):
        for q in range(groups):

            @pl.when(q * GROUP < counts[b])
            def _():
                copy(b, q).start()

    for b in range(SLOTS_AHEAD - 1):
        start(b)

    @pl.loop(0, total // 4)
    def _(j):
        for i in range(4):
            acc[4 * j + i] = jnp.zeros(acc.shape[1:], F32)

    @pl.loop(0, blocks)
    def _(b):
        s = lax.rem(b, SLOTS_AHEAD)

        @pl.when(b + SLOTS_AHEAD - 1 < blocks)
        def _():
            start(b + SLOTS_AHEAD - 1)

        n = counts[b]
        for live in range(1, groups + 1):

            @pl.when((n + GROUP - 1) // GROUP == live)
            def _():
                g = grad[pl.ds(pl.multiple_of(b * t, t), t), :]
                for q in range(live):
                    copy(b, q).wait()
                for q in range(live):
                    wide = jnp.concatenate(
                        [tbuf[s, q * GROUP + i] for i in range(GROUP)], axis=1
                    )
                    terms = lax.dot_general(
                        wide, g, (((0,), (0,)), ((), ())), preferred_element_type=F32
                    )
                    for i in range(GROUP):
                        k = q * GROUP + i
                        term = terms[i * t : (i + 1) * t]
                        if q == live - 1 and i > 0:
                            term = jnp.where(k < n, term, 0.0)
                        acc[cols[k, b]] += term

    def flush(c):
        s = lax.rem(c, 2)
        return pltpu.make_async_copy(
            stage.at[s], out.at[pl.ds(c * OUT_CHUNK, OUT_CHUNK)], out_sems.at[s]
        )

    @pl.loop(0, total // OUT_CHUNK)
    def _(c):
        s = lax.rem(c, 2)

        @pl.when(c >= 2)
        def _():
            flush(c - 2).wait()

        @pl.loop(0, OUT_CHUNK // 4)
        def _(j):
            for i in range(4):
                stage[s, 4 * j + i] = acc[c * OUT_CHUNK + 4 * j + i].astype(BF16)

        flush(c).start()

    for c in (total // OUT_CHUNK - 2, total // OUT_CHUNK - 1):
        flush(c).wait()


def spmm_t(grad, tiles, columns, counts, total):
    blocks, slots, t, _ = tiles.shape
    width = grad.shape[-1]
    return pl.pallas_call(
        bwd_kernel,
        grid_spec=pltpu.PrefetchScalarGridSpec(
            num_scalar_prefetch=2,
            grid=(1,),
            in_specs=[
                pl.BlockSpec(memory_space=pl.ANY),
                pl.BlockSpec((blocks * t, width), lambda i, *_: (0, 0)),
            ],
            out_specs=pl.BlockSpec(memory_space=pl.ANY),
            scratch_shapes=[
                pltpu.VMEM((total, t, width), F32),
                pltpu.VMEM((SLOTS_AHEAD, slots, t, t), BF16),
                pltpu.VMEM((2, OUT_CHUNK, t, width), BF16),
                pltpu.SemaphoreType.DMA((SLOTS_AHEAD, slots // GROUP)),
                pltpu.SemaphoreType.DMA((2,)),
            ],
        ),
        out_shape=jax.ShapeDtypeStruct((total, t, width), BF16),
        compiler_params=pltpu.CompilerParams(vmem_limit_bytes=60 * 1024 * 1024),
        name="spmm_t",
    )(columns, counts, tiles, grad)


def local(features, tiles, columns, counts, weight, cotangent):
    rows_here, feat_local = features.shape
    blocks_here, slots, t, _ = tiles.shape
    total_blocks = blocks_here * lax.axis_size("row")
    columns = columns.T
    gathered, cots, ws = gather_all(features, cotangent, weight)
    mixed = spmm(gathered.reshape(total_blocks, t, feat_local), tiles, columns, counts)
    mixed_grad, act, wgrad = dense(mixed.reshape(N_REP, -1, feat_local), cots, ws)
    part = spmm_t(mixed_grad.reshape(mixed.shape), tiles, columns, counts, total_blocks)
    act, feature_grad, weight_grad = reduce_all(
        part.reshape(N_ROW, rows_here, feat_local), act, wgrad
    )
    return act.reshape(features.shape), feature_grad, weight_grad


def solution(mesh):
    in_specs = (
        P("row", "rep"),
        P("row", None, None, None),
        P("row", None),
        P("row"),
        P(None, "rep"),
        P("row", "rep"),
    )
    out_specs = (P("row", "rep"), P("row", "rep"), P("rep", "row"))
    return jax.shard_map(local, mesh=mesh, in_specs=in_specs, out_specs=out_specs, check_vma=False)
```

```python
import functools

import jax
import jax.numpy as jnp
from jax import lax
from jax.experimental import pallas as pl
from jax.experimental.pallas import tpu as pltpu
from jax.sharding import PartitionSpec as P

F32 = jnp.float32
BF16 = jnp.bfloat16
MESH = pl.DeviceIdType.MESH
ROWS_Y = 4
N_ROW = 16
N_REP = 8
ANY = pl.BlockSpec(memory_space=pl.ANY)
VM = pl.BlockSpec(memory_space=pltpu.VMEM)


class Place:
    def __init__(self):
        self.row = lax.axis_index("row")
        self.rep = lax.axis_index("rep")
        self.c = lax.rem(self.row, 2)
        self.y = lax.rem(self.row // 2, ROWS_Y)
        self.h = self.row // (2 * ROWS_Y)

    def slot(self, other, dy, sib=False):
        h = 1 - self.h if other else self.h
        c = 1 - self.c if sib else self.c
        return (h * ROWS_Y + lax.rem(self.y + dy + ROWS_Y, ROWS_Y)) * 2 + c

    def at(self, other, dy, sib=False):
        return (self.slot(other, dy, sib), self.rep)

    def peer_at(self, d):
        x = lax.rem(self.rep // 4 + d // 4, 2)
        z1 = lax.rem(lax.rem(self.rep, 4) // 2 + lax.rem(d, 4) // 2, 2)
        z0 = lax.rem(self.rep + d, 2)
        return x * 4 + z1 * 2 + z0

    def peer(self, d):
        x, z = self.rep // 4, lax.rem(self.rep, 4)
        if d >= 4:
            x = 1 - x
        if d % 4 == 1:
            z = z + 1 - 2 * lax.rem(z, 2)
        elif d % 4 == 2:
            z = lax.rem(z + 2, 4)
        elif d % 4 == 3:
            z = 3 - z
        return x * 4 + z


def greet(partners):
    barrier = pltpu.get_barrier_semaphore()
    for partner in partners:
        pl.semaphore_signal(barrier, inc=1, device_id=partner, device_id_type=MESH)
    pl.semaphore_wait(barrier, len(partners))


class Sends:
    def __init__(self, sems):
        self.sems, self.live = sems, []

    def __call__(self, src, dst, recv_sem, device):
        copy = pltpu.make_async_remote_copy(
            src_ref=src,
            dst_ref=dst,
            send_sem=self.sems.at[len(self.live)],
            recv_sem=recv_sem,
            device_id=device,
            device_id_type=MESH,
        )
        copy.start()
        self.live.append(copy)

    def finish(self):
        for copy in self.live:
            copy.wait_send()


def arrived(dst, recv_sem):
    pltpu.make_async_copy(dst, dst, recv_sem).wait()


CHUNKS = 4


STRIP = 128
PAIR = 2


def forward_kernel(
    feats, cot, weight, tiles, cols, counts, mixed_grad, act, wgrad,
    full, blocks, cots, ws, w, mixed, m, grad, back,
    send_sems, recv_sems, cot_recv, w_recv, w_sib, m_send, m_recv, back_recv, local_sems,
):
    here = Place()
    n_blocks, slots, t, _ = tiles.shape
    step = n_blocks // CHUNKS
    piece = cot.shape[0] // N_REP
    width = cot.shape[1]
    half = weight.shape[0] // 2
    peers = [here.peer(d) for d in range(1, N_REP)]
    sib = here.at(False, 0, True)
    up, down, across = here.at(False, 1), here.at(False, -1), here.at(True, 0)

    def base(slot):
        return slot * n_blocks

    own = [
        pltpu.make_async_copy(feats, full.at[pl.ds(base(here.row), n_blocks)], local_sems.at[0]),
        pltpu.make_async_copy(weight, ws.at[here.rep], local_sems.at[1]),
        pltpu.make_async_copy(
            cot.at[pl.ds(pl.multiple_of(here.rep * piece, piece), piece)],
            cots.at[here.rep], local_sems.at[2],
        ),
        pltpu.make_async_copy(tiles, blocks, local_sems.at[3]),
    ]
    greet([sib, up, down, across] + [(here.row, q) for q in peers])
    send = Sends(send_sems)

    def rows(chunk):
        return pl.ds(chunk * step, step)

    def place(slot, chunk):
        return full.at[pl.ds(base(slot) + chunk * step, step)]

    columns = [
        (False, -1), (False, 1), (False, 2), (True, 0), (True, -1), (True, 1), (True, 2),
    ]
    slots_of = [here.slot(*column) for column in columns]
    opposite = [(i + CHUNKS // 2) % CHUNKS for i in range(CHUNKS)]

    for i in range(CHUNKS):
        send(feats.at[rows(i)], place(here.row, i), recv_sems.at[3, i], across)
    for a, b in enumerate(opposite):
        send(feats.at[rows(a)], place(here.row, a), recv_sems.at[0, a], up)
        send(feats.at[rows(b)], place(here.row, b), recv_sems.at[1, b], down)
    for i in range(CHUNKS):
        send(feats.at[rows(i)], place(here.row, i), recv_sems.at[7, i], sib)
    mine = pl.ds(pl.multiple_of(here.c * half, half), half)
    theirs = pl.ds(pl.multiple_of((1 - here.c) * half, half), half)
    for d, q in enumerate(peers):
        send(weight.at[mine], ws.at[here.rep, mine], w_recv.at[d], (here.row, q))
    for d, q in enumerate(peers):
        send(
            cot.at[pl.ds(pl.multiple_of(q * piece, piece), piece)],
            cots.at[here.rep], cot_recv.at[d], (here.row, q),
        )
    for copy in own:
        copy.start()

    def take(kind, chunk, on=None):
        src = place(slots_of[kind], chunk)
        arrived(src, recv_sems.at[kind, chunk])
        if on is not None:
            send(src, src, recv_sems.at[2 if kind < 3 else 6, chunk], on)
        send(src, src, recv_sems.at[8 + kind, chunk], sib)

    for k in (0, 4):
        for a, b in enumerate(opposite):
            take(k, a, up if a < CHUNKS // 2 else None)
            take(k + 1, b, down if b >= CHUNKS // 2 else None)
            if k == 0:
                src = place(slots_of[3], a)
                arrived(src, recv_sems.at[3, a])
                send(src, src, recv_sems.at[4, a], up)
                send(src, src, recv_sems.at[5, a], down)
                send(src, src, recv_sems.at[11, a], sib)
        for i in range(CHUNKS):
            take(k + 2, i)
        if k == 0:
            for d, q in enumerate(peers):
                arrived(ws.at[q, mine], w_recv.at[d])
                send(ws.at[q, mine], ws.at[q, mine], w_sib.at[d], sib)

    for d, q in enumerate(peers):
        arrived(ws.at[q, theirs], w_sib.at[d])
        arrived(cots.at[q], cot_recv.at[d])
    for copy in own:
        copy.wait()
    for r in range(N_REP):
        w[:, r * width : (r + 1) * width] = ws[r]
    for kind, column in enumerate([(False, 0)] + columns):
        for i in range(CHUNKS):
            arrived(place(here.slot(*column, True), i), recv_sems.at[7 + kind, i])

    def mix(dst, q):
        @pl.loop(0, piece // (t * PAIR))
        def _(j):
            for e in range(PAIR):
                i = j * PAIR + e
                b = q * (piece // t) + i
                n = counts[b]
                left = jnp.concatenate(
                    [jnp.where(k < n, blocks[b, k], jnp.zeros((), BF16)) for k in range(slots)],
                    axis=1,
                )
                right = jnp.concatenate([full[cols[k, b]] for k in range(slots)], axis=0)
                dst[pl.ds(pl.multiple_of(i * t, t), t), :] = jnp.dot(
                    left, right, preferred_element_type=F32
                ).astype(BF16)

    def shift(d):
        q = here.peer_at(d)
        return q, pltpu.make_async_remote_copy(
            src_ref=mixed.at[q], dst_ref=m.at[here.rep],
            send_sem=m_send.at[d - 1], recv_sem=m_recv.at[d - 1],
            device_id=(here.row, q), device_id_type=MESH,
        )

    @pl.loop(1, N_REP)
    def _(d):
        q, copy = shift(d)
        mix(mixed.at[q], q)
        copy.start()

    mix(m.at[here.rep], here.rep)
    for d, q in enumerate(peers):
        arrived(m.at[q], m_recv.at[d])

    for i in range(piece // STRIP):
        at = pl.ds(i * STRIP, STRIP)
        x = jnp.concatenate([m[r, at, :] for r in range(N_REP)], axis=1)
        c = jnp.concatenate([cots[r, at, :] for r in range(N_REP)], axis=1)
        pre = jnp.dot(x, w[...], preferred_element_type=F32)
        sig = jax.nn.sigmoid(pre)
        out = (pre * sig).astype(BF16)
        g = (c.astype(F32) * sig * (1.0 + pre * (1.0 - sig))).astype(BF16)
        grad[at, :] = g
        b = lax.dot_general(
            g, w[...], (((1,), (1,)), ((), ())), preferred_element_type=F32
        ).astype(BF16)
        for r in range(N_REP):
            act[r, at, :] = out[:, r * width : (r + 1) * width]
            back[r, at, :] = b[:, r * width : (r + 1) * width]
        for d, q in enumerate(peers):
            send(back.at[q, at], mixed_grad.at[here.rep, at], back_recv.at[d, i], (here.row, q))
    last = pltpu.make_async_copy(back.at[here.rep], mixed_grad.at[here.rep], local_sems.at[4])
    last.start()
    for r in range(N_REP):
        wgrad[r] = lax.dot_general(
            m[r], grad[...], (((0,), (0,)), ((), ())), preferred_element_type=F32
        ).astype(BF16)
    last.wait()
    for d, q in enumerate(peers):
        for i in range(piece // STRIP):
            arrived(mixed_grad.at[q, pl.ds(i * STRIP, STRIP)], back_recv.at[d, i])
    for d in range(1, N_REP):
        shift(d)[1].wait_send()
    send.finish()


def forward(features, cotangent, weight, tiles, columns, counts):
    rows, width = features.shape
    n_blocks, _, t, _ = tiles.shape
    piece = rows // N_REP
    strips = piece // STRIP
    dma = pltpu.SemaphoreType.DMA
    smem = pl.BlockSpec(memory_space=pltpu.SMEM)
    stack = pltpu.VMEM((N_REP, piece, width), BF16)
    return pl.pallas_call(
        forward_kernel,
        in_specs=[ANY] * 4 + [smem] * 2,
        out_specs=[ANY, VM, VM],
        out_shape=[
            jax.ShapeDtypeStruct((N_REP, piece, width), BF16),
            jax.ShapeDtypeStruct((N_REP, piece, width), BF16),
            jax.ShapeDtypeStruct((N_REP, width, N_REP * width), BF16),
        ],
        scratch_shapes=[
            pltpu.VMEM((N_ROW * n_blocks, t, width), BF16),
            pltpu.VMEM(tiles.shape, BF16),
            stack,
            pltpu.VMEM((N_REP,) + weight.shape, BF16),
            pltpu.VMEM((N_REP * width, N_REP * width), BF16),
            stack, stack,
            pltpu.VMEM((piece, N_REP * width), BF16),
            stack,
            dma((15 * CHUNKS + 21 + 7 * strips,)), dma((15, CHUNKS)),
            dma((7,)), dma((7,)), dma((7,)), dma((7,)), dma((7,)), dma((7, strips)), dma((5,)),
        ],
        compiler_params=pltpu.CompilerParams(
            collective_id=0, has_side_effects=True, vmem_limit_bytes=60 * 1024 * 1024
        ),
        name="forward",
    )(features.reshape(n_blocks, t, width), cotangent, weight, tiles, columns, counts)


OFFSETS = (2, 1, -1, 0)
SUM_ROWS = 128


def reduce_kernel(
    part, act, wgrad, act_out, out, wg_out,
    own, theirs, far_up, far_down, near_up, near_down, cross, own_act,
    wg_in, wg_sum, wg_sib, wg_half, wg_row, wg_fin, wg_fin_sib,
    send_sems, load_sems, sib_recv, far_recv, near_recv, cross_recv,
    act_recv, wg_recv, row_recv, pair_recv, local_sems,
):
    here = Place()
    step = own.shape[1] // CHUNKS
    half = CHUNKS // 2
    peers = [here.peer(d) for d in range(1, N_REP)]
    sib = here.at(False, 0, True)
    up, down, across = here.at(False, 1), here.at(False, -1), here.at(True, 0)
    columns = [(o, dy) for o in (True, False) for dy in OFFSETS][:-1]

    def rows(i):
        return pl.ds(i * step, step)

    loads = {}
    for r in range(8):
        slot = here.slot(r < 4, OFFSETS[r % 4])
        for i in range(CHUNKS):
            loads[r, i] = pltpu.make_async_copy(
                part.at[slot, rows(i)], own.at[r, rows(i)], load_sems.at[r, i]
            )
    extra = [
        pltpu.make_async_copy(act.at[here.rep], own_act, local_sems.at[0]),
        pltpu.make_async_copy(wgrad.at[here.rep], wg_in.at[N_REP - 1], local_sems.at[1]),
    ]
    for load in extra:
        load.start()
    for load in loads.values():
        load.start()
    greet([sib] + [here.at(*column) for column in columns] + [(here.row, q) for q in peers])

    send = Sends(send_sems)
    order = [0, 4, 1, 2, 3, 5, 6, 7]
    for r in order:
        slot = here.slot(r < 4, OFFSETS[r % 4], True)
        for i in range(CHUNKS):
            send(part.at[slot, rows(i)], theirs.at[r, rows(i)], sib_recv.at[r, i], sib)

    def total(r, i, more, dst=None):
        loads[r, i].wait()
        arrived(theirs.at[r, rows(i)], sib_recv.at[r, i])
        target = own.at[r] if dst is None else dst

        @pl.loop(0, step // SUM_ROWS)
        def _(j):
            at = pl.ds(pl.multiple_of(i * step + j * SUM_ROWS, SUM_ROWS), SUM_ROWS)
            acc = own[r, at, :].astype(F32) + theirs[r, at, :].astype(F32)
            for ref, base in more:
                at2 = pl.ds(pl.multiple_of(base * step + j * SUM_ROWS, SUM_ROWS), SUM_ROWS)
                acc = acc + ref[at2, :].astype(F32)
            target[at, :] = acc.astype(BF16)

    def far(hh):
        for i in range(half):
            total(4 * hh, i, [])
            send(own.at[4 * hh, rows(i)], far_up.at[hh, rows(i)], far_recv.at[hh, 0, i], up)
            total(4 * hh, i + half, [])
            send(
                own.at[4 * hh, rows(i + half)], far_down.at[hh, rows(i)],
                far_recv.at[hh, 1, i], down,
            )

    def near(hh, i, j, up_more, down_more):
        r, s = 4 * hh + 1, 4 * hh + 2
        total(r, i, up_more)
        send(own.at[r, rows(i)], near_up.at[hh, rows(i)], near_recv.at[hh, 0, i], up)
        total(s, j, down_more)
        send(own.at[s, rows(j)], near_down.at[hh, rows(j)], near_recv.at[hh, 1, j], down)

    def near_first(hh):
        for i in range(half):
            near(hh, i + half, i, [], [])

    def near_last(hh):
        for i in range(half):
            arrived(far_up.at[hh, rows(i)], far_recv.at[hh, 0, i])
            arrived(far_down.at[hh, rows(i)], far_recv.at[hh, 1, i])
            near(hh, i, i + half, [(far_up.at[hh], i)], [(far_down.at[hh], i)])

    def final(hh):
        for i in [k + part for k in range(half) for part in (0, half)]:
            arrived(near_up.at[hh, rows(i)], near_recv.at[hh, 0, i])
            arrived(near_down.at[hh, rows(i)], near_recv.at[hh, 1, i])
            more = [(near_up.at[hh], i), (near_down.at[hh], i)]
            if hh == 0:
                total(3, i, more)
                send(own.at[3, rows(i)], cross.at[rows(i)], cross_recv.at[i], across)
            else:
                arrived(cross.at[rows(i)], cross_recv.at[i])
                total(7, i, more + [(cross, i)], out)

    far(0)
    for d, q in enumerate(peers):
        send(wgrad.at[q], wg_in.at[d], wg_recv.at[d], (here.row, q))
    for d, q in enumerate(peers):
        send(act.at[q], act_out.at[here.rep], act_recv.at[d], (here.row, q))
    extra[0].wait()
    keep = pltpu.make_async_copy(own_act, act_out.at[here.rep], local_sems.at[0])
    keep.start()
    near_first(0)
    far(1)
    near_last(0)
    near_first(1)
    final(0)

    extra[1].wait()
    for d in range(N_REP - 1):
        arrived(wg_in.at[d], wg_recv.at[d])
    wide = wg_in.shape[2]
    edge = wg_half.shape[1]

    @pl.loop(0, wide // 128)
    def _(j):
        at = pl.ds(pl.multiple_of(j * 128, 128), 128)
        acc = wg_in[0, :, at].astype(F32)
        for d in range(1, N_REP):
            acc = acc + wg_in[d, :, at].astype(F32)
        acc = acc.astype(BF16)
        wg_sum[0, j] = acc[:edge]
        wg_sum[1, j] = acc[edge:]

    send(wg_sum.at[1 - here.c], wg_sib, pair_recv.at[0], sib)
    near_last(1)
    arrived(wg_sib, pair_recv.at[0])

    @pl.loop(0, wide // 128)
    def _(j):
        wg_half[j] = (wg_sum[here.c, j].astype(F32) + wg_sib[j].astype(F32)).astype(BF16)

    for k, (o, dy) in enumerate(columns):
        send(
            wg_half.at[here.slot(o, dy) // 2], wg_row.at[k], row_recv.at[k], here.at(o, dy)
        )
    for k in range(len(columns)):
        arrived(wg_row.at[k], row_recv.at[k])
    acc = wg_half[here.row // 2].astype(F32)
    for k in range(len(columns)):
        acc = acc + wg_row[k].astype(F32)
    wg_fin[...] = acc
    send(wg_fin, wg_fin_sib, pair_recv.at[1], sib)
    final(1)
    arrived(wg_fin_sib, pair_recv.at[1])

    @pl.when(here.c == 0)
    def _():
        wg_out[:edge, :] = wg_fin[:, :edge]
        wg_out[edge:, :] = wg_fin_sib[:, :edge]

    @pl.when(here.c == 1)
    def _():
        wg_out[:edge, :] = wg_fin_sib[:, edge:]
        wg_out[edge:, :] = wg_fin[:, edge:]

    keep.wait()
    for d, q in enumerate(peers):
        arrived(act_out.at[q], act_recv.at[d])
    send.finish()


def reduce_all(part, act, wgrad):
    n, rows, width = part.shape
    n_rep, k, wide = wgrad.shape
    edge = k // 2
    dma = pltpu.SemaphoreType.DMA
    return pl.pallas_call(
        reduce_kernel,
        in_specs=[ANY] * 3,
        out_specs=[ANY, VM, VM],
        out_shape=[
            jax.ShapeDtypeStruct(act.shape, BF16),
            jax.ShapeDtypeStruct((rows, width), BF16),
            jax.ShapeDtypeStruct((k, wide // n), F32),
        ],
        scratch_shapes=[
            pltpu.VMEM((8, rows, width), BF16),
            pltpu.VMEM((8, rows, width), BF16),
            pltpu.VMEM((2, rows // 2, width), BF16),
            pltpu.VMEM((2, rows // 2, width), BF16),
            pltpu.VMEM((2, rows, width), BF16),
            pltpu.VMEM((2, rows, width), BF16),
            pltpu.VMEM((rows, width), BF16),
            pltpu.VMEM(act.shape[1:], BF16),
            pltpu.VMEM(wgrad.shape, BF16),
            pltpu.VMEM((2, wide // 128, edge, 128), BF16),
            pltpu.VMEM((wide // 128, edge, 128), BF16),
            pltpu.VMEM((wide // 128, edge, 128), BF16),
            pltpu.VMEM((7, edge, 128), BF16),
            pltpu.VMEM((edge, 128), F32),
            pltpu.VMEM((edge, 128), F32),
            dma((15 * CHUNKS + 23,)), dma((8, CHUNKS)), dma((8, CHUNKS)), dma((2, 2, CHUNKS // 2)), dma((2, 2, CHUNKS)),
            dma((CHUNKS,)), dma((7,)), dma((7,)), dma((7,)), dma((2,)), dma((2,)),
        ],
        compiler_params=pltpu.CompilerParams(collective_id=2, has_side_effects=True),
        name="reduce_all",
    )(part, act, wgrad)


SLOTS_AHEAD = 4


GROUP = 4
OUT_CHUNK = 16


def bwd_kernel(cols, counts, tiles, grad, out, acc, tbuf, stage, sems, out_sems):
    blocks, slots, t, _ = tiles.shape
    total = acc.shape[0]
    groups = slots // GROUP

    def copy(b, q):
        s = lax.rem(b, SLOTS_AHEAD)
        at = pl.ds(q * GROUP, GROUP)
        return pltpu.make_async_copy(tiles.at[b, at], tbuf.at[s, at], sems.at[s, q])

    def start(b):
        for q in range(groups):

            @pl.when(q * GROUP < counts[b])
            def _():
                copy(b, q).start()

    for b in range(SLOTS_AHEAD - 1):
        start(b)

    @pl.loop(0, total // 4)
    def _(j):
        for i in range(4):
            acc[4 * j + i] = jnp.zeros(acc.shape[1:], F32)

    @pl.loop(0, blocks)
    def _(b):
        s = lax.rem(b, SLOTS_AHEAD)

        @pl.when(b + SLOTS_AHEAD - 1 < blocks)
        def _():
            start(b + SLOTS_AHEAD - 1)

        n = counts[b]
        for live in range(1, groups + 1):

            @pl.when((n + GROUP - 1) // GROUP == live)
            def _():
                g = grad[pl.ds(pl.multiple_of(b * t, t), t), :]
                for q in range(live):
                    copy(b, q).wait()
                for q in range(live):
                    wide = jnp.concatenate(
                        [tbuf[s, q * GROUP + i] for i in range(GROUP)], axis=1
                    )
                    terms = lax.dot_general(
                        wide, g, (((0,), (0,)), ((), ())), preferred_element_type=F32
                    )
                    for i in range(GROUP):
                        k = q * GROUP + i
                        term = terms[i * t : (i + 1) * t]
                        if q == live - 1 and i > 0:
                            term = jnp.where(k < n, term, 0.0)
                        acc[cols[k, b]] += term

    def flush(c):
        s = lax.rem(c, 2)
        return pltpu.make_async_copy(
            stage.at[s], out.at[pl.ds(c * OUT_CHUNK, OUT_CHUNK)], out_sems.at[s]
        )

    @pl.loop(0, total // OUT_CHUNK)
    def _(c):
        s = lax.rem(c, 2)

        @pl.when(c >= 2)
        def _():
            flush(c - 2).wait()

        @pl.loop(0, OUT_CHUNK // 4)
        def _(j):
            for i in range(4):
                stage[s, 4 * j + i] = acc[c * OUT_CHUNK + 4 * j + i].astype(BF16)

        flush(c).start()

    for c in (total // OUT_CHUNK - 2, total // OUT_CHUNK - 1):
        flush(c).wait()


def spmm_t(grad, tiles, columns, counts, total):
    blocks, slots, t, _ = tiles.shape
    width = grad.shape[-1]
    return pl.pallas_call(
        bwd_kernel,
        grid_spec=pltpu.PrefetchScalarGridSpec(
            num_scalar_prefetch=2,
            grid=(1,),
            in_specs=[
                pl.BlockSpec(memory_space=pl.ANY),
                pl.BlockSpec((blocks * t, width), lambda i, *_: (0, 0)),
            ],
            out_specs=pl.BlockSpec(memory_space=pl.ANY),
            scratch_shapes=[
                pltpu.VMEM((total, t, width), F32),
                pltpu.VMEM((SLOTS_AHEAD, slots, t, t), BF16),
                pltpu.VMEM((2, OUT_CHUNK, t, width), BF16),
                pltpu.SemaphoreType.DMA((SLOTS_AHEAD, slots // GROUP)),
                pltpu.SemaphoreType.DMA((2,)),
            ],
        ),
        out_shape=jax.ShapeDtypeStruct((total, t, width), BF16),
        compiler_params=pltpu.CompilerParams(vmem_limit_bytes=60 * 1024 * 1024),
        name="spmm_t",
    )(columns, counts, tiles, grad)


def local(features, tiles, columns, counts, weight, cotangent):
    rows_here, feat_local = features.shape
    blocks_here, slots, t, _ = tiles.shape
    total_blocks = blocks_here * lax.axis_size("row")
    columns = columns.T
    mixed_grad, act, wgrad = forward(features, cotangent, weight, tiles, columns, counts)
    part = spmm_t(mixed_grad.reshape(features.shape), tiles, columns, counts, total_blocks)
    act, feature_grad, weight_grad = reduce_all(
        part.reshape(N_ROW, rows_here, feat_local), act, wgrad
    )
    return act.reshape(features.shape), feature_grad, weight_grad


def solution(mesh):
    in_specs = (
        P("row", "rep"),
        P("row", None, None, None),
        P("row", None),
        P("row"),
        P(None, "rep"),
        P("row", "rep"),
    )
    out_specs = (P("row", "rep"), P("row", "rep"), P("rep", "row"))
    return jax.shard_map(local, mesh=mesh, in_specs=in_specs, out_specs=out_specs, check_vma=False)
```

```python
import functools

import jax
import jax.numpy as jnp
from jax import lax
from jax.experimental import pallas as pl
from jax.experimental.pallas import tpu as pltpu
from jax.sharding import PartitionSpec as P

F32 = jnp.float32
BF16 = jnp.bfloat16
MESH = pl.DeviceIdType.MESH
ROWS_Y = 4
N_ROW = 16
N_REP = 8
ANY = pl.BlockSpec(memory_space=pl.ANY)
VM = pl.BlockSpec(memory_space=pltpu.VMEM)


class Place:
    def __init__(self):
        self.row = lax.axis_index("row")
        self.rep = lax.axis_index("rep")
        self.c = lax.rem(self.row, 2)
        self.y = lax.rem(self.row // 2, ROWS_Y)
        self.h = self.row // (2 * ROWS_Y)

    def slot(self, other, dy, sib=False):
        h = 1 - self.h if other else self.h
        c = 1 - self.c if sib else self.c
        return (h * ROWS_Y + lax.rem(self.y + dy + ROWS_Y, ROWS_Y)) * 2 + c

    def at(self, other, dy, sib=False):
        return (self.slot(other, dy, sib), self.rep)

    def peer_at(self, d):
        x = lax.rem(self.rep // 4 + d // 4, 2)
        z1 = lax.rem(lax.rem(self.rep, 4) // 2 + lax.rem(d, 4) // 2, 2)
        z0 = lax.rem(self.rep + d, 2)
        return x * 4 + z1 * 2 + z0

    def peer(self, d):
        x, z = self.rep // 4, lax.rem(self.rep, 4)
        if d >= 4:
            x = 1 - x
        if d % 4 == 1:
            z = z + 1 - 2 * lax.rem(z, 2)
        elif d % 4 == 2:
            z = lax.rem(z + 2, 4)
        elif d % 4 == 3:
            z = 3 - z
        return x * 4 + z


def greet(partners):
    barrier = pltpu.get_barrier_semaphore()
    for partner in partners:
        pl.semaphore_signal(barrier, inc=1, device_id=partner, device_id_type=MESH)
    pl.semaphore_wait(barrier, len(partners))


class Sends:
    def __init__(self, sems):
        self.sems, self.live = sems, []

    def __call__(self, src, dst, recv_sem, device):
        copy = pltpu.make_async_remote_copy(
            src_ref=src,
            dst_ref=dst,
            send_sem=self.sems.at[len(self.live)],
            recv_sem=recv_sem,
            device_id=device,
            device_id_type=MESH,
        )
        copy.start()
        self.live.append(copy)

    def finish(self):
        for copy in self.live:
            copy.wait_send()


def arrived(dst, recv_sem):
    pltpu.make_async_copy(dst, dst, recv_sem).wait()


CHUNKS = 4
CROSS = 0


STRIP = 128
PAIR = 2


def forward_kernel(
    feats, cot, weight, tiles, cols, counts, mixed_grad, act, wgrad,
    full, blocks, cots, ws, w, mixed, m, grad, back,
    send_sems, recv_sems, cot_recv, w_recv, w_sib, m_send, m_recv, back_recv, local_sems,
):
    here = Place()
    n_blocks, slots, t, _ = tiles.shape
    step = n_blocks // CHUNKS
    piece = cot.shape[0] // N_REP
    width = cot.shape[1]
    half = weight.shape[0] // 2
    peers = [here.peer(d) for d in range(1, N_REP)]
    sib = here.at(False, 0, True)
    up, down, across = here.at(False, 1), here.at(False, -1), here.at(True, 0)

    def base(slot):
        return slot * n_blocks

    own = [
        pltpu.make_async_copy(feats, full.at[pl.ds(base(here.row), n_blocks)], local_sems.at[0]),
        pltpu.make_async_copy(weight, ws.at[here.rep], local_sems.at[1]),
        pltpu.make_async_copy(
            cot.at[pl.ds(pl.multiple_of(here.rep * piece, piece), piece)],
            cots.at[here.rep], local_sems.at[2],
        ),
        pltpu.make_async_copy(tiles, blocks, local_sems.at[3]),
    ]
    greet([sib, up, down, across] + [(here.row, q) for q in peers])
    send = Sends(send_sems)

    def rows(chunk):
        return pl.ds(chunk * step, step)

    def place(slot, chunk):
        return full.at[pl.ds(base(slot) + chunk * step, step)]

    columns = [
        (False, -1), (False, 1), (False, 2), (True, 0), (True, -1), (True, 1), (True, 2),
    ]
    slots_of = [here.slot(*column) for column in columns]
    opposite = [(i + CHUNKS // 2) % CHUNKS for i in range(CHUNKS)]

    for i in range(CHUNKS):
        send(feats.at[rows(i)], place(here.row, i), recv_sems.at[3, i], across)
    for a, b in enumerate(opposite):
        send(feats.at[rows(a)], place(here.row, a), recv_sems.at[0, a], up)
        send(feats.at[rows(b)], place(here.row, b), recv_sems.at[1, b], down)
    for i in range(CHUNKS):
        send(feats.at[rows(i)], place(here.row, i), recv_sems.at[7, i], sib)
    mine = pl.ds(pl.multiple_of(here.c * half, half), half)
    theirs = pl.ds(pl.multiple_of((1 - here.c) * half, half), half)
    for d, q in enumerate(peers):
        send(weight.at[mine], ws.at[here.rep, mine], w_recv.at[d], (here.row, q))
    for d, q in enumerate(peers):
        send(
            cot.at[pl.ds(pl.multiple_of(q * piece, piece), piece)],
            cots.at[here.rep], cot_recv.at[d], (here.row, q),
        )
    for copy in own:
        copy.start()

    def take(kind, chunk, on=None):
        src = place(slots_of[kind], chunk)
        arrived(src, recv_sems.at[kind, chunk])
        if on is not None:
            send(src, src, recv_sems.at[2 if kind < 3 else 6, chunk], on)
        if kind < 3 and chunk == CROSS:
            send(src, src, recv_sems.at[4 + kind, chunk], across)
        send(src, src, recv_sems.at[8 + kind, chunk], sib)

    for k in (0, 4):
        for a, b in enumerate(opposite):
            take(k, a, up if a < CHUNKS // 2 and (k, a) != (4, CROSS) else None)
            take(k + 1, b, down if b >= CHUNKS // 2 and (k, b) != (4, CROSS) else None)
            if k == 0:
                src = place(slots_of[3], a)
                arrived(src, recv_sems.at[3, a])
                if a != CROSS:
                    send(src, src, recv_sems.at[4, a], up)
                    send(src, src, recv_sems.at[5, a], down)
                send(src, src, recv_sems.at[11, a], sib)
        for i in range(CHUNKS):
            take(k + 2, i)
        if k == 0:
            for d, q in enumerate(peers):
                arrived(ws.at[q, mine], w_recv.at[d])
                send(ws.at[q, mine], ws.at[q, mine], w_sib.at[d], sib)

    for d, q in enumerate(peers):
        arrived(ws.at[q, theirs], w_sib.at[d])
        arrived(cots.at[q], cot_recv.at[d])
    for copy in own:
        copy.wait()
    for r in range(N_REP):
        w[:, r * width : (r + 1) * width] = ws[r]
    for kind, column in enumerate([(False, 0)] + columns):
        for i in range(CHUNKS):
            arrived(place(here.slot(*column, True), i), recv_sems.at[7 + kind, i])

    def mix(dst, q):
        @pl.loop(0, piece // (t * PAIR))
        def _(j):
            for e in range(PAIR):
                i = j * PAIR + e
                b = q * (piece // t) + i
                n = counts[b]
                left = jnp.concatenate(
                    [jnp.where(k < n, blocks[b, k], jnp.zeros((), BF16)) for k in range(slots)],
                    axis=1,
                )
                right = jnp.concatenate([full[cols[k, b]] for k in range(slots)], axis=0)
                dst[pl.ds(pl.multiple_of(i * t, t), t), :] = jnp.dot(
                    left, right, preferred_element_type=F32
                ).astype(BF16)

    def shift(d):
        q = here.peer_at(d)
        return q, pltpu.make_async_remote_copy(
            src_ref=mixed.at[q], dst_ref=m.at[here.rep],
            send_sem=m_send.at[d - 1], recv_sem=m_recv.at[d - 1],
            device_id=(here.row, q), device_id_type=MESH,
        )

    @pl.loop(1, N_REP)
    def _(e):
        q, copy = shift(lax.rem(3 * e, N_REP))
        mix(mixed.at[q], q)
        copy.start()

    mix(m.at[here.rep], here.rep)
    for d, q in enumerate(peers):
        arrived(m.at[q], m_recv.at[d])

    for i in range(piece // STRIP):
        at = pl.ds(i * STRIP, STRIP)
        x = jnp.concatenate([m[r, at, :] for r in range(N_REP)], axis=1)
        c = jnp.concatenate([cots[r, at, :] for r in range(N_REP)], axis=1)
        pre = jnp.dot(x, w[...], preferred_element_type=F32)
        sig = jax.nn.sigmoid(pre)
        out = (pre * sig).astype(BF16)
        g = (c.astype(F32) * sig * (1.0 + pre * (1.0 - sig))).astype(BF16)
        grad[at, :] = g
        b = lax.dot_general(
            g, w[...], (((1,), (1,)), ((), ())), preferred_element_type=F32
        ).astype(BF16)
        for r in range(N_REP):
            act[r, at, :] = out[:, r * width : (r + 1) * width]
            back[r, at, :] = b[:, r * width : (r + 1) * width]
        for d, q in enumerate(peers):
            send(back.at[q, at], mixed_grad.at[here.rep, at], back_recv.at[d, i], (here.row, q))
    last = pltpu.make_async_copy(back.at[here.rep], mixed_grad.at[here.rep], local_sems.at[4])
    last.start()
    for r in range(N_REP):
        wgrad[r] = lax.dot_general(
            m[r], grad[...], (((0,), (0,)), ((), ())), preferred_element_type=F32
        ).astype(BF16)
    last.wait()
    for d, q in enumerate(peers):
        for i in range(piece // STRIP):
            arrived(mixed_grad.at[q, pl.ds(i * STRIP, STRIP)], back_recv.at[d, i])
    for d in range(1, N_REP):
        shift(d)[1].wait_send()
    send.finish()


def forward(features, cotangent, weight, tiles, columns, counts):
    rows, width = features.shape
    n_blocks, _, t, _ = tiles.shape
    piece = rows // N_REP
    strips = piece // STRIP
    dma = pltpu.SemaphoreType.DMA
    smem = pl.BlockSpec(memory_space=pltpu.SMEM)
    stack = pltpu.VMEM((N_REP, piece, width), BF16)
    return pl.pallas_call(
        forward_kernel,
        in_specs=[ANY] * 4 + [smem] * 2,
        out_specs=[ANY, VM, VM],
        out_shape=[
            jax.ShapeDtypeStruct((N_REP, piece, width), BF16),
            jax.ShapeDtypeStruct((N_REP, piece, width), BF16),
            jax.ShapeDtypeStruct((N_REP, width, N_REP * width), BF16),
        ],
        scratch_shapes=[
            pltpu.VMEM((N_ROW * n_blocks, t, width), BF16),
            pltpu.VMEM(tiles.shape, BF16),
            stack,
            pltpu.VMEM((N_REP,) + weight.shape, BF16),
            pltpu.VMEM((N_REP * width, N_REP * width), BF16),
            stack, stack,
            pltpu.VMEM((piece, N_REP * width), BF16),
            stack,
            dma((15 * CHUNKS + 21 + 7 * strips,)), dma((15, CHUNKS)),
            dma((7,)), dma((7,)), dma((7,)), dma((7,)), dma((7,)), dma((7, strips)), dma((5,)),
        ],
        compiler_params=pltpu.CompilerParams(
            collective_id=0, has_side_effects=True, vmem_limit_bytes=60 * 1024 * 1024
        ),
        name="forward",
    )(features.reshape(n_blocks, t, width), cotangent, weight, tiles, columns, counts)


OFFSETS = (2, 1, -1, 0)
SUM_ROWS = 128


def reduce_kernel(
    part, act, wgrad, act_out, out, wg_out,
    own, theirs, far_up, far_down, near_up, near_down, cross, early, own_act,
    wg_own, wg_sib, wg_in, wg_half, wg_row, wg_fin, wg_fin_sib,
    send_sems, load_sems, sib_recv, far_recv, near_recv, cross_recv, early_recv,
    act_recv, wg_recv, row_recv, pair_recv, local_sems,
):
    here = Place()
    step = own.shape[1] // CHUNKS
    half = CHUNKS // 2
    peers = [here.peer(d) for d in range(1, N_REP)]
    sib = here.at(False, 0, True)
    up, down, across = here.at(False, 1), here.at(False, -1), here.at(True, 0)
    columns = [(o, dy) for o in (True, False) for dy in OFFSETS][:-1]

    edge = wg_half.shape[1]
    mine = pl.ds(pl.multiple_of(here.c * edge, edge), edge)
    theirs_of_pair = pl.ds(pl.multiple_of((1 - here.c) * edge, edge), edge)

    def rows(i):
        return pl.ds(i * step, step)

    loads = {}
    for r in range(8):
        slot = here.slot(r < 4, OFFSETS[r % 4])
        for i in range(CHUNKS):
            loads[r, i] = pltpu.make_async_copy(
                part.at[slot, rows(i)], own.at[r, rows(i)], load_sems.at[r, i]
            )
    extra = [
        pltpu.make_async_copy(act.at[here.rep], own_act, local_sems.at[0]),
        pltpu.make_async_copy(wgrad.at[:, mine], wg_own, local_sems.at[1]),
    ]
    for load in extra:
        load.start()
    for load in loads.values():
        load.start()
    greet([sib] + [here.at(*column) for column in columns] + [(here.row, q) for q in peers])

    send = Sends(send_sems)
    first = [(0, i) for i in range(CHUNKS)] + [(r, CROSS) for r in (1, 2, 3)]
    rest = [(r, i) for r in (1, 2, 4, 3, 5, 6, 7) for i in range(CHUNKS)]
    for r, i in first + [k for k in rest if k not in first]:
        slot = here.slot(r < 4, OFFSETS[r % 4], True)
        send(part.at[slot, rows(i)], theirs.at[r, rows(i)], sib_recv.at[r, i], sib)
        if (r, i) == first[-1]:
            send(wgrad.at[:, theirs_of_pair], wg_sib, pair_recv.at[0], sib)

    def total(r, i, more, dst=None):
        loads[r, i].wait()
        arrived(theirs.at[r, rows(i)], sib_recv.at[r, i])
        target = own.at[r] if dst is None else dst

        @pl.loop(0, step // SUM_ROWS)
        def _(j):
            at = pl.ds(pl.multiple_of(i * step + j * SUM_ROWS, SUM_ROWS), SUM_ROWS)
            acc = own[r, at, :].astype(F32) + theirs[r, at, :].astype(F32)
            for ref, base in more:
                at2 = pl.ds(pl.multiple_of(base * step + j * SUM_ROWS, SUM_ROWS), SUM_ROWS)
                acc = acc + ref[at2, :].astype(F32)
            if dst is not None:
                acc = acc.T
            target[at, :] = acc.astype(BF16)

    def plus(hh, k, i, more):
        if hh == 1 and i == CROSS:
            arrived(early.at[k], early_recv.at[k])
            return more + [(early.at[k], 0)]
        return more

    def skip(hh, i):
        return hh == 0 and i == CROSS

    def far(hh):
        r = 4 * hh
        for i in (1, 0):
            for j, land, to in ((i, far_up, up), (i + half, far_down, down)):
                if skip(hh, j):
                    continue
                total(r, j, plus(hh, 0, j, []))
                send(
                    own.at[r, rows(j)], land.at[hh, rows(i)],
                    far_recv.at[hh, int(j >= half), i], to,
                )

    def near(hh, i, j, up_more, down_more):
        r, s = 4 * hh + 1, 4 * hh + 2
        if not skip(hh, i):
            total(r, i, plus(hh, 1, i, up_more))
            send(own.at[r, rows(i)], near_up.at[hh, rows(i)], near_recv.at[hh, 0, i], up)
        if not skip(hh, j):
            total(s, j, plus(hh, 2, j, down_more))
            send(own.at[s, rows(j)], near_down.at[hh, rows(j)], near_recv.at[hh, 1, j], down)

    def near_first(hh):
        for i in (1, 0):
            near(hh, i + half, i, [], [])

    def near_last(hh):
        for i in (1, 0):
            if not skip(hh, i):
                arrived(far_up.at[hh, rows(i)], far_recv.at[hh, 0, i])
            arrived(far_down.at[hh, rows(i)], far_recv.at[hh, 1, i])
            near(hh, i, i + half, [(far_up.at[hh], i)], [(far_down.at[hh], i)])

    def final(hh):
        for i in (3, 1, 2, 0):
            if skip(hh, i):
                continue
            arrived(near_up.at[hh, rows(i)], near_recv.at[hh, 0, i])
            arrived(near_down.at[hh, rows(i)], near_recv.at[hh, 1, i])
            more = [(near_up.at[hh], i), (near_down.at[hh], i)]
            if hh == 0:
                total(3, i, more)
                send(own.at[3, rows(i)], cross.at[rows(i)], cross_recv.at[i], across)
            else:
                arrived(cross.at[rows(i)], cross_recv.at[i])
                total(7, i, more + [(cross, i)], out)

    far(0)
    for k in range(4):
        total(k, CROSS, [])
        if k < 3:
            send(own.at[k, rows(CROSS)], early.at[k], early_recv.at[k], across)
        else:
            send(own.at[k, rows(CROSS)], cross.at[rows(CROSS)], cross_recv.at[CROSS], across)
    near_first(0)

    extra[1].wait()
    arrived(wg_sib, pair_recv.at[0])

    @pl.loop(0, N_REP)
    def _(j):
        wg_own[j] = (wg_own[j].astype(F32) + wg_sib[j].astype(F32)).astype(BF16)

    for d, q in enumerate(peers):
        send(wg_own.at[q], wg_in.at[d], wg_recv.at[d], (here.row, q))
    for d, q in enumerate(peers):
        send(act.at[q], act_out.at[here.rep], act_recv.at[d], (here.row, q))
    extra[0].wait()
    keep = pltpu.make_async_copy(own_act, act_out.at[here.rep], local_sems.at[0])
    keep.start()
    far(1)
    near_last(0)
    near_first(1)
    final(0)
    near_last(1)

    for d in range(N_REP - 1):
        arrived(wg_in.at[d], wg_recv.at[d])

    @pl.loop(0, wg_half.shape[0])
    def _(j):
        at = pl.ds(pl.multiple_of(j * 128, 128), 128)
        acc = wg_own[here.rep, :, at].astype(F32)
        for d in range(N_REP - 1):
            acc = acc + wg_in[d, :, at].astype(F32)
        wg_half[j] = acc.astype(BF16)

    for k, (o, dy) in enumerate(columns):
        send(
            wg_half.at[here.slot(o, dy) // 2], wg_row.at[k], row_recv.at[k], here.at(o, dy)
        )
    for k in range(len(columns)):
        arrived(wg_row.at[k], row_recv.at[k])
    acc = wg_half[here.row // 2].astype(F32)
    for k in range(len(columns)):
        acc = acc + wg_row[k].astype(F32)
    wg_fin[...] = acc
    send(wg_fin, wg_fin_sib, pair_recv.at[1], sib)
    final(1)
    arrived(wg_fin_sib, pair_recv.at[1])

    @pl.when(here.c == 0)
    def _():
        wg_out[:edge, :] = wg_fin[:, :edge]
        wg_out[edge:, :] = wg_fin_sib[:, :edge]

    @pl.when(here.c == 1)
    def _():
        wg_out[:edge, :] = wg_fin_sib[:, edge:]
        wg_out[edge:, :] = wg_fin[:, edge:]

    keep.wait()
    for d, q in enumerate(peers):
        arrived(act_out.at[q], act_recv.at[d])
    send.finish()


def reduce_all(part, act, wgrad):
    n, rows, width = part.shape
    n_rep, k, wide = wgrad.shape
    edge = k // 2
    dma = pltpu.SemaphoreType.DMA
    return pl.pallas_call(
        reduce_kernel,
        in_specs=[ANY] * 3,
        out_specs=[ANY, VM, VM],
        out_shape=[
            jax.ShapeDtypeStruct(act.shape, BF16),
            jax.ShapeDtypeStruct((rows, width), BF16),
            jax.ShapeDtypeStruct((k, wide // n), F32),
        ],
        scratch_shapes=[
            pltpu.VMEM((8, rows, width), BF16),
            pltpu.VMEM((8, rows, width), BF16),
            pltpu.VMEM((2, rows // 2, width), BF16),
            pltpu.VMEM((2, rows // 2, width), BF16),
            pltpu.VMEM((2, rows, width), BF16),
            pltpu.VMEM((2, rows, width), BF16),
            pltpu.VMEM((rows, width), BF16),
            pltpu.VMEM((3, rows // CHUNKS, width), BF16),
            pltpu.VMEM(act.shape[1:], BF16),
            pltpu.VMEM((n_rep, edge, wide), BF16),
            pltpu.VMEM((n_rep, edge, wide), BF16),
            pltpu.VMEM((n_rep - 1, edge, wide), BF16),
            pltpu.VMEM((wide // 128, edge, 128), BF16),
            pltpu.VMEM((7, edge, 128), BF16),
            pltpu.VMEM((edge, 128), F32),
            pltpu.VMEM((edge, 128), F32),
            dma((15 * CHUNKS + 23,)), dma((8, CHUNKS)), dma((8, CHUNKS)), dma((2, 2, CHUNKS // 2)), dma((2, 2, CHUNKS)),
            dma((CHUNKS,)), dma((3,)), dma((7,)), dma((7,)), dma((7,)), dma((2,)), dma((2,)),
        ],
        compiler_params=pltpu.CompilerParams(collective_id=2, has_side_effects=True),
        name="reduce_all",
    )(part, act, wgrad)


SLOTS_AHEAD = 4


GROUP = 4
OUT_CHUNK = 16


def bwd_kernel(cols, counts, tiles, grad, out, acc, tbuf, stage, sems, out_sems):
    blocks, slots, t, _ = tiles.shape
    total = acc.shape[0]
    groups = slots // GROUP

    def copy(b, q):
        s = lax.rem(b, SLOTS_AHEAD)
        at = pl.ds(q * GROUP, GROUP)
        return pltpu.make_async_copy(tiles.at[b, at], tbuf.at[s, at], sems.at[s, q])

    def start(b):
        for q in range(groups):

            @pl.when(q * GROUP < counts[b])
            def _():
                copy(b, q).start()

    for b in range(SLOTS_AHEAD - 1):
        start(b)

    @pl.loop(0, total // 4)
    def _(j):
        for i in range(4):
            acc[4 * j + i] = jnp.zeros(acc.shape[1:], F32)

    @pl.loop(0, blocks)
    def _(b):
        s = lax.rem(b, SLOTS_AHEAD)

        @pl.when(b + SLOTS_AHEAD - 1 < blocks)
        def _():
            start(b + SLOTS_AHEAD - 1)

        n = counts[b]
        for live in range(1, groups + 1):

            @pl.when((n + GROUP - 1) // GROUP == live)
            def _():
                g = grad[pl.ds(pl.multiple_of(b * t, t), t), :].T
                for q in range(live):
                    copy(b, q).wait()
                for q in range(live):
                    wide = jnp.concatenate(
                        [tbuf[s, q * GROUP + i] for i in range(GROUP)], axis=1
                    )
                    terms = jnp.dot(g, wide, preferred_element_type=F32)
                    for i in range(GROUP):
                        k = q * GROUP + i
                        term = terms[:, i * t : (i + 1) * t]
                        if q == live - 1 and i > 0:
                            term = jnp.where(k < n, term, 0.0)
                        acc[cols[k, b]] += term

    def flush(c):
        s = lax.rem(c, 2)
        return pltpu.make_async_copy(
            stage.at[s], out.at[pl.ds(c * OUT_CHUNK, OUT_CHUNK)], out_sems.at[s]
        )

    @pl.loop(0, total // OUT_CHUNK)
    def _(c):
        s = lax.rem(c, 2)

        @pl.when(c >= 2)
        def _():
            flush(c - 2).wait()

        @pl.loop(0, OUT_CHUNK // 4)
        def _(j):
            for i in range(4):
                stage[s, 4 * j + i] = acc[c * OUT_CHUNK + 4 * j + i].astype(BF16)

        flush(c).start()

    for c in (total // OUT_CHUNK - 2, total // OUT_CHUNK - 1):
        flush(c).wait()


def spmm_t(grad, tiles, columns, counts, total):
    blocks, slots, t, _ = tiles.shape
    width = grad.shape[-1]
    return pl.pallas_call(
        bwd_kernel,
        grid_spec=pltpu.PrefetchScalarGridSpec(
            num_scalar_prefetch=2,
            grid=(1,),
            in_specs=[
                pl.BlockSpec(memory_space=pl.ANY),
                pl.BlockSpec((blocks * t, width), lambda i, *_: (0, 0)),
            ],
            out_specs=pl.BlockSpec(memory_space=pl.ANY),
            scratch_shapes=[
                pltpu.VMEM((total, t, width), F32),
                pltpu.VMEM((SLOTS_AHEAD, slots, t, t), BF16),
                pltpu.VMEM((2, OUT_CHUNK, t, width), BF16),
                pltpu.SemaphoreType.DMA((SLOTS_AHEAD, slots // GROUP)),
                pltpu.SemaphoreType.DMA((2,)),
            ],
        ),
        out_shape=jax.ShapeDtypeStruct((total, t, width), BF16),
        compiler_params=pltpu.CompilerParams(vmem_limit_bytes=60 * 1024 * 1024),
        name="spmm_t",
    )(columns, counts, tiles, grad)


def local(features, tiles, columns, counts, weight, cotangent):
    rows_here, feat_local = features.shape
    blocks_here, slots, t, _ = tiles.shape
    total_blocks = blocks_here * lax.axis_size("row")
    columns = columns.T
    mixed_grad, act, wgrad = forward(features, cotangent, weight, tiles, columns, counts)
    part = spmm_t(mixed_grad.reshape(features.shape), tiles, columns, counts, total_blocks)
    act, feature_grad, weight_grad = reduce_all(
        part.reshape(N_ROW, rows_here, feat_local), act, wgrad
    )
    return act.reshape(features.shape), feature_grad, weight_grad


def solution(mesh):
    in_specs = (
        P("row", "rep"),
        P("row", None, None, None),
        P("row", None),
        P("row"),
        P(None, "rep"),
        P("row", "rep"),
    )
    out_specs = (P("row", "rep"), P("row", "rep"), P("rep", "row"))
    return jax.shard_map(local, mesh=mesh, in_specs=in_specs, out_specs=out_specs, check_vma=False)
```

```python
import functools

import jax
import jax.numpy as jnp
from jax import lax
from jax.experimental import pallas as pl
from jax.experimental.pallas import tpu as pltpu
from jax.sharding import PartitionSpec as P

F32 = jnp.float32
BF16 = jnp.bfloat16
MESH = pl.DeviceIdType.MESH
ROWS_Y = 4
N_ROW = 16
N_REP = 8
ANY = pl.BlockSpec(memory_space=pl.ANY)
VM = pl.BlockSpec(memory_space=pltpu.VMEM)


class Place:
    def __init__(self):
        self.row = lax.axis_index("row")
        self.rep = lax.axis_index("rep")
        self.c = lax.rem(self.row, 2)
        self.y = lax.rem(self.row // 2, ROWS_Y)
        self.h = self.row // (2 * ROWS_Y)

    def slot(self, other, dy, sib=False):
        h = 1 - self.h if other else self.h
        c = 1 - self.c if sib else self.c
        return (h * ROWS_Y + lax.rem(self.y + dy + ROWS_Y, ROWS_Y)) * 2 + c

    def at(self, other, dy, sib=False):
        return (self.slot(other, dy, sib), self.rep)

    def peer_at(self, d):
        x = lax.rem(self.rep // 4 + d // 4, 2)
        z1 = lax.rem(lax.rem(self.rep, 4) // 2 + lax.rem(d, 4) // 2, 2)
        z0 = lax.rem(self.rep + d, 2)
        return x * 4 + z1 * 2 + z0

    def peer(self, d):
        x, z = self.rep // 4, lax.rem(self.rep, 4)
        if d >= 4:
            x = 1 - x
        if d % 4 == 1:
            z = z + 1 - 2 * lax.rem(z, 2)
        elif d % 4 == 2:
            z = lax.rem(z + 2, 4)
        elif d % 4 == 3:
            z = 3 - z
        return x * 4 + z


def greet(partners):
    barrier = pltpu.get_barrier_semaphore()
    for partner in partners:
        pl.semaphore_signal(barrier, inc=1, device_id=partner, device_id_type=MESH)
    pl.semaphore_wait(barrier, len(partners))


class Sends:
    def __init__(self, sems):
        self.sems, self.live = sems, []

    def __call__(self, src, dst, recv_sem, device):
        copy = pltpu.make_async_remote_copy(
            src_ref=src,
            dst_ref=dst,
            send_sem=self.sems.at[len(self.live)],
            recv_sem=recv_sem,
            device_id=device,
            device_id_type=MESH,
        )
        copy.start()
        self.live.append(copy)

    def finish(self):
        for copy in self.live:
            copy.wait_send()


def arrived(dst, recv_sem):
    pltpu.make_async_copy(dst, dst, recv_sem).wait()


CHUNKS = 4
CROSS = 0


STRIP = 128
PAIR = 2


def forward_kernel(
    feats, cot, weight, tiles, cols, counts, mixed_grad, act, wgrad,
    full, blocks, cots, ws, w, mixed, m, grad, back,
    send_sems, recv_sems, cot_recv, w_recv, w_sib, m_send, m_recv, back_recv, local_sems,
):
    here = Place()
    n_blocks, slots, t, _ = tiles.shape
    step = n_blocks // CHUNKS
    piece = cot.shape[0] // N_REP
    width = cot.shape[1]
    half = weight.shape[0] // 2
    peers = [here.peer(d) for d in range(1, N_REP)]
    sib = here.at(False, 0, True)
    up, down, across = here.at(False, 1), here.at(False, -1), here.at(True, 0)

    def base(slot):
        return slot * n_blocks

    own = [
        pltpu.make_async_copy(feats, full.at[pl.ds(base(here.row), n_blocks)], local_sems.at[0]),
        pltpu.make_async_copy(weight, ws.at[here.rep], local_sems.at[1]),
        pltpu.make_async_copy(
            cot.at[pl.ds(pl.multiple_of(here.rep * piece, piece), piece)],
            cots.at[here.rep], local_sems.at[2],
        ),
        pltpu.make_async_copy(tiles, blocks, local_sems.at[3]),
    ]
    greet([sib, up, down, across] + [(here.row, q) for q in peers])
    send = Sends(send_sems)

    def rows(chunk):
        return pl.ds(chunk * step, step)

    def place(slot, chunk):
        return full.at[pl.ds(base(slot) + chunk * step, step)]

    columns = [
        (False, -1), (False, 1), (False, 2), (True, 0), (True, -1), (True, 1), (True, 2),
    ]
    slots_of = [here.slot(*column) for column in columns]
    opposite = [(i + CHUNKS // 2) % CHUNKS for i in range(CHUNKS)]

    for i in range(CHUNKS):
        send(feats.at[rows(i)], place(here.row, i), recv_sems.at[3, i], across)
    for a, b in enumerate(opposite):
        send(feats.at[rows(a)], place(here.row, a), recv_sems.at[0, a], up)
        send(feats.at[rows(b)], place(here.row, b), recv_sems.at[1, b], down)
    for i in range(CHUNKS):
        send(feats.at[rows(i)], place(here.row, i), recv_sems.at[7, i], sib)
    mine = pl.ds(pl.multiple_of(here.c * half, half), half)
    theirs = pl.ds(pl.multiple_of((1 - here.c) * half, half), half)
    for d, q in enumerate(peers):
        send(weight.at[mine], ws.at[here.rep, mine], w_recv.at[d], (here.row, q))
    for d, q in enumerate(peers):
        send(
            cot.at[pl.ds(pl.multiple_of(q * piece, piece), piece)],
            cots.at[here.rep], cot_recv.at[d], (here.row, q),
        )
    for copy in own:
        copy.start()

    def take(kind, chunk, on=None):
        src = place(slots_of[kind], chunk)
        arrived(src, recv_sems.at[kind, chunk])
        if on is not None:
            send(src, src, recv_sems.at[2 if kind < 3 else 6, chunk], on)
        if kind < 3 and chunk == CROSS:
            send(src, src, recv_sems.at[4 + kind, chunk], across)
        send(src, src, recv_sems.at[8 + kind, chunk], sib)

    for k in (0, 4):
        for a, b in enumerate(opposite):
            take(k, a, up if a < CHUNKS // 2 and (k, a) != (4, CROSS) else None)
            take(k + 1, b, down if b >= CHUNKS // 2 and (k, b) != (4, CROSS) else None)
            if k == 0:
                src = place(slots_of[3], a)
                arrived(src, recv_sems.at[3, a])
                if a != CROSS:
                    send(src, src, recv_sems.at[4, a], up)
                    send(src, src, recv_sems.at[5, a], down)
                send(src, src, recv_sems.at[11, a], sib)
        for i in range(CHUNKS):
            take(k + 2, i)
        if k == 0:
            for d, q in enumerate(peers):
                arrived(ws.at[q, mine], w_recv.at[d])
                send(ws.at[q, mine], ws.at[q, mine], w_sib.at[d], sib)

    for d, q in enumerate(peers):
        arrived(ws.at[q, theirs], w_sib.at[d])
        arrived(cots.at[q], cot_recv.at[d])
    for copy in own:
        copy.wait()
    for r in range(N_REP):
        w[:, r * width : (r + 1) * width] = ws[r]
    for kind, column in enumerate([(False, 0)] + columns):
        for i in range(CHUNKS):
            arrived(place(here.slot(*column, True), i), recv_sems.at[7 + kind, i])

    def mix(dst, q):
        @pl.loop(0, piece // (t * PAIR))
        def _(j):
            for e in range(PAIR):
                i = j * PAIR + e
                b = q * (piece // t) + i
                n = counts[b]
                left = jnp.concatenate(
                    [jnp.where(k < n, blocks[b, k], jnp.zeros((), BF16)) for k in range(slots)],
                    axis=1,
                )
                right = jnp.concatenate([full[cols[k, b]] for k in range(slots)], axis=0)
                dst[pl.ds(pl.multiple_of(i * t, t), t), :] = jnp.dot(
                    left, right, preferred_element_type=F32
                ).astype(BF16)

    def shift(d):
        q = here.peer_at(d)
        return q, pltpu.make_async_remote_copy(
            src_ref=mixed.at[q], dst_ref=m.at[here.rep],
            send_sem=m_send.at[d - 1], recv_sem=m_recv.at[d - 1],
            device_id=(here.row, q), device_id_type=MESH,
        )

    @pl.loop(1, N_REP)
    def _(e):
        q, copy = shift(lax.rem(3 * e, N_REP))
        mix(mixed.at[q], q)
        copy.start()

    mix(m.at[here.rep], here.rep)
    for d, q in enumerate(peers):
        arrived(m.at[q], m_recv.at[d])

    for i in range(piece // STRIP):
        at = pl.ds(i * STRIP, STRIP)
        x = jnp.concatenate([m[r, at, :] for r in range(N_REP)], axis=1)
        c = jnp.concatenate([cots[r, at, :] for r in range(N_REP)], axis=1)
        pre = jnp.dot(x, w[...], preferred_element_type=F32)
        sig = jax.nn.sigmoid(pre)
        out = (pre * sig).astype(BF16)
        g = (c.astype(F32) * sig * (1.0 + pre * (1.0 - sig))).astype(BF16)
        grad[at, :] = g
        b = lax.dot_general(
            g, w[...], (((1,), (1,)), ((), ())), preferred_element_type=F32
        ).astype(BF16)
        for r in range(N_REP):
            act[r, at, :] = out[:, r * width : (r + 1) * width]
            back[r, at, :] = b[:, r * width : (r + 1) * width]
        for d, q in enumerate(peers):
            send(back.at[q, at], mixed_grad.at[here.rep, at], back_recv.at[d, i], (here.row, q))
    last = pltpu.make_async_copy(back.at[here.rep], mixed_grad.at[here.rep], local_sems.at[4])
    last.start()
    for r in range(N_REP):
        wgrad[r] = lax.dot_general(
            m[r], grad[...], (((0,), (0,)), ((), ())), preferred_element_type=F32
        ).astype(BF16)
    last.wait()
    for d, q in enumerate(peers):
        for i in range(piece // STRIP):
            arrived(mixed_grad.at[q, pl.ds(i * STRIP, STRIP)], back_recv.at[d, i])
    for d in range(1, N_REP):
        shift(d)[1].wait_send()
    send.finish()


def forward(features, cotangent, weight, tiles, columns, counts):
    rows, width = features.shape
    n_blocks, _, t, _ = tiles.shape
    piece = rows // N_REP
    strips = piece // STRIP
    dma = pltpu.SemaphoreType.DMA
    smem = pl.BlockSpec(memory_space=pltpu.SMEM)
    stack = pltpu.VMEM((N_REP, piece, width), BF16)
    return pl.pallas_call(
        forward_kernel,
        in_specs=[ANY] * 4 + [smem] * 2,
        out_specs=[ANY, VM, VM],
        out_shape=[
            jax.ShapeDtypeStruct((N_REP, piece, width), BF16),
            jax.ShapeDtypeStruct((N_REP, piece, width), BF16),
            jax.ShapeDtypeStruct((N_REP, width, N_REP * width), BF16),
        ],
        scratch_shapes=[
            pltpu.VMEM((N_ROW * n_blocks, t, width), BF16),
            pltpu.VMEM(tiles.shape, BF16),
            stack,
            pltpu.VMEM((N_REP,) + weight.shape, BF16),
            pltpu.VMEM((N_REP * width, N_REP * width), BF16),
            stack, stack,
            pltpu.VMEM((piece, N_REP * width), BF16),
            stack,
            dma((15 * CHUNKS + 21 + 7 * strips,)), dma((15, CHUNKS)),
            dma((7,)), dma((7,)), dma((7,)), dma((7,)), dma((7,)), dma((7, strips)), dma((5,)),
        ],
        compiler_params=pltpu.CompilerParams(
            collective_id=0, has_side_effects=True, vmem_limit_bytes=60 * 1024 * 1024
        ),
        name="forward",
    )(features.reshape(n_blocks, t, width), cotangent, weight, tiles, columns, counts)


OFFSETS = (2, 1, -1, 0)
SUM_ROWS = 128


def reduce_kernel(
    part, act, wgrad, act_out, out, wg_out,
    own, theirs, far_up, far_down, near_up, near_down, cross, early, own_act,
    wg_own, wg_sib, wg_in, wg_half, wg_row, wg_fin, wg_fin_sib,
    send_sems, load_sems, sib_recv, far_recv, near_recv, cross_recv, early_recv,
    act_recv, wg_recv, row_recv, pair_recv, local_sems,
):
    here = Place()
    step = own.shape[1] // CHUNKS
    half = CHUNKS // 2
    peers = [here.peer(d) for d in range(1, N_REP)]
    sib = here.at(False, 0, True)
    up, down, across = here.at(False, 1), here.at(False, -1), here.at(True, 0)
    columns = [(o, dy) for o in (True, False) for dy in OFFSETS][:-1]

    edge = wg_half.shape[1]
    mine = pl.ds(pl.multiple_of(here.c * edge, edge), edge)
    theirs_of_pair = pl.ds(pl.multiple_of((1 - here.c) * edge, edge), edge)

    def rows(i):
        return pl.ds(i * step, step)

    loads = {}
    for r in range(8):
        slot = here.slot(r < 4, OFFSETS[r % 4])
        for i in range(CHUNKS):
            loads[r, i] = pltpu.make_async_copy(
                part.at[slot, rows(i)], own.at[r, rows(i)], load_sems.at[r, i]
            )
    extra = [
        pltpu.make_async_copy(act.at[here.rep], own_act, local_sems.at[0]),
        pltpu.make_async_copy(wgrad.at[:, mine], wg_own, local_sems.at[1]),
    ]
    for load in extra:
        load.start()
    for load in loads.values():
        load.start()
    greet([sib] + [here.at(*column) for column in columns] + [(here.row, q) for q in peers])

    send = Sends(send_sems)
    first = [(0, i) for i in range(CHUNKS)] + [(r, CROSS) for r in (1, 2, 3)]
    rest = [(r, i) for r in (1, 2, 4, 3, 5, 6, 7) for i in range(CHUNKS)]
    for r, i in first + [k for k in rest if k not in first]:
        slot = here.slot(r < 4, OFFSETS[r % 4], True)
        send(part.at[slot, rows(i)], theirs.at[r, rows(i)], sib_recv.at[r, i], sib)
        if (r, i) == first[-1]:
            send(wgrad.at[:, theirs_of_pair], wg_sib, pair_recv.at[0], sib)

    def total(r, i, more, dst=None):
        loads[r, i].wait()
        arrived(theirs.at[r, rows(i)], sib_recv.at[r, i])
        target = own.at[r] if dst is None else dst

        @pl.loop(0, step // SUM_ROWS)
        def _(j):
            at = pl.ds(pl.multiple_of(i * step + j * SUM_ROWS, SUM_ROWS), SUM_ROWS)
            acc = own[r, at, :].astype(F32) + theirs[r, at, :].astype(F32)
            for ref, base in more:
                at2 = pl.ds(pl.multiple_of(base * step + j * SUM_ROWS, SUM_ROWS), SUM_ROWS)
                acc = acc + ref[at2, :].astype(F32)
            if dst is not None:
                acc = acc.T
            target[at, :] = acc.astype(BF16)

    def plus(hh, k, i, more):
        if hh == 1 and i == CROSS:
            arrived(early.at[k], early_recv.at[k])
            return more + [(early.at[k], 0)]
        return more

    def skip(hh, i):
        return hh == 0 and i == CROSS

    def far(hh):
        r = 4 * hh
        for i in (1, 0):
            for j, land, to in ((i, far_up, up), (i + half, far_down, down)):
                if skip(hh, j):
                    continue
                total(r, j, plus(hh, 0, j, []))
                send(
                    own.at[r, rows(j)], land.at[hh, rows(i)],
                    far_recv.at[hh, int(j >= half), i], to,
                )

    def near(hh, i, j, up_more, down_more):
        r, s = 4 * hh + 1, 4 * hh + 2
        if not skip(hh, i):
            total(r, i, plus(hh, 1, i, up_more))
            send(own.at[r, rows(i)], near_up.at[hh, rows(i)], near_recv.at[hh, 0, i], up)
        if not skip(hh, j):
            total(s, j, plus(hh, 2, j, down_more))
            send(own.at[s, rows(j)], near_down.at[hh, rows(j)], near_recv.at[hh, 1, j], down)

    def near_first(hh):
        for i in (1, 0):
            near(hh, i + half, i, [], [])

    def near_last(hh):
        for i in (1, 0):
            if not skip(hh, i):
                arrived(far_up.at[hh, rows(i)], far_recv.at[hh, 0, i])
            arrived(far_down.at[hh, rows(i)], far_recv.at[hh, 1, i])
            near(hh, i, i + half, [(far_up.at[hh], i)], [(far_down.at[hh], i)])

    def final(hh):
        for i in (3, 1, 2, 0):
            if skip(hh, i):
                continue
            arrived(near_up.at[hh, rows(i)], near_recv.at[hh, 0, i])
            arrived(near_down.at[hh, rows(i)], near_recv.at[hh, 1, i])
            more = [(near_up.at[hh], i), (near_down.at[hh], i)]
            if hh == 0:
                total(3, i, more)
                send(own.at[3, rows(i)], cross.at[rows(i)], cross_recv.at[i], across)
            else:
                arrived(cross.at[rows(i)], cross_recv.at[i])
                total(7, i, more + [(cross, i)], out)

    far(0)
    for k in range(4):
        total(k, CROSS, [])
        if k < 3:
            send(own.at[k, rows(CROSS)], early.at[k], early_recv.at[k], across)
        else:
            send(own.at[k, rows(CROSS)], cross.at[rows(CROSS)], cross_recv.at[CROSS], across)
    near_first(0)

    extra[1].wait()
    arrived(wg_sib, pair_recv.at[0])

    @pl.loop(0, N_REP)
    def _(j):
        wg_own[j] = (wg_own[j].astype(F32) + wg_sib[j].astype(F32)).astype(BF16)

    for d, q in enumerate(peers):
        send(wg_own.at[q], wg_in.at[d], wg_recv.at[d], (here.row, q))
    for d, q in enumerate(peers):
        send(act.at[q], act_out.at[here.rep], act_recv.at[d], (here.row, q))
    extra[0].wait()
    keep = pltpu.make_async_copy(own_act, act_out.at[here.rep], local_sems.at[0])
    keep.start()
    far(1)
    near_last(0)

    for d in range(N_REP - 1):
        arrived(wg_in.at[d], wg_recv.at[d])

    @pl.loop(0, wg_half.shape[0])
    def _(j):
        at = pl.ds(pl.multiple_of(j * 128, 128), 128)
        acc = wg_own[here.rep, :, at].astype(F32)
        for d in range(N_REP - 1):
            acc = acc + wg_in[d, :, at].astype(F32)
        wg_half[j] = acc.astype(BF16)

    for k, (o, dy) in enumerate(columns):
        send(
            wg_half.at[here.slot(o, dy) // 2], wg_row.at[k], row_recv.at[k], here.at(o, dy)
        )
    near_first(1)
    final(0)
    near_last(1)
    for k in range(len(columns)):
        arrived(wg_row.at[k], row_recv.at[k])
    acc = wg_half[here.row // 2].astype(F32)
    for k in range(len(columns)):
        acc = acc + wg_row[k].astype(F32)
    wg_fin[...] = acc
    send(wg_fin, wg_fin_sib, pair_recv.at[1], sib)
    final(1)
    arrived(wg_fin_sib, pair_recv.at[1])

    @pl.when(here.c == 0)
    def _():
        wg_out[:edge, :] = wg_fin[:, :edge]
        wg_out[edge:, :] = wg_fin_sib[:, :edge]

    @pl.when(here.c == 1)
    def _():
        wg_out[:edge, :] = wg_fin_sib[:, edge:]
        wg_out[edge:, :] = wg_fin[:, edge:]

    keep.wait()
    for d, q in enumerate(peers):
        arrived(act_out.at[q], act_recv.at[d])
    send.finish()


def reduce_all(part, act, wgrad):
    n, rows, width = part.shape
    n_rep, k, wide = wgrad.shape
    edge = k // 2
    dma = pltpu.SemaphoreType.DMA
    return pl.pallas_call(
        reduce_kernel,
        in_specs=[ANY] * 3,
        out_specs=[ANY, VM, VM],
        out_shape=[
            jax.ShapeDtypeStruct(act.shape, BF16),
            jax.ShapeDtypeStruct((rows, width), BF16),
            jax.ShapeDtypeStruct((k, wide // n), F32),
        ],
        scratch_shapes=[
            pltpu.VMEM((8, rows, width), BF16),
            pltpu.VMEM((8, rows, width), BF16),
            pltpu.VMEM((2, rows // 2, width), BF16),
            pltpu.VMEM((2, rows // 2, width), BF16),
            pltpu.VMEM((2, rows, width), BF16),
            pltpu.VMEM((2, rows, width), BF16),
            pltpu.VMEM((rows, width), BF16),
            pltpu.VMEM((3, rows // CHUNKS, width), BF16),
            pltpu.VMEM(act.shape[1:], BF16),
            pltpu.VMEM((n_rep, edge, wide), BF16),
            pltpu.VMEM((n_rep, edge, wide), BF16),
            pltpu.VMEM((n_rep - 1, edge, wide), BF16),
            pltpu.VMEM((wide // 128, edge, 128), BF16),
            pltpu.VMEM((7, edge, 128), BF16),
            pltpu.VMEM((edge, 128), F32),
            pltpu.VMEM((edge, 128), F32),
            dma((15 * CHUNKS + 23,)), dma((8, CHUNKS)), dma((8, CHUNKS)), dma((2, 2, CHUNKS // 2)), dma((2, 2, CHUNKS)),
            dma((CHUNKS,)), dma((3,)), dma((7,)), dma((7,)), dma((7,)), dma((2,)), dma((2,)),
        ],
        compiler_params=pltpu.CompilerParams(collective_id=2, has_side_effects=True),
        name="reduce_all",
    )(part, act, wgrad)


SLOTS_AHEAD = 8


GROUP = 4
OUT_CHUNK = 16
FLUSHES = 8


def bwd_kernel(cols, counts, tiles, grad, out, acc, tbuf, stage, sems, out_sems):
    blocks, slots, t, _ = tiles.shape
    total = acc.shape[0]
    groups = slots // GROUP

    def copy(b, q):
        s = lax.rem(b, SLOTS_AHEAD)
        at = pl.ds(q * GROUP, GROUP)
        return pltpu.make_async_copy(tiles.at[b, at], tbuf.at[s, at], sems.at[s, q])

    def start(b):
        for q in range(groups):

            @pl.when(q * GROUP < counts[b])
            def _():
                copy(b, q).start()

    for b in range(SLOTS_AHEAD - 1):
        start(b)

    @pl.loop(0, total // 4)
    def _(j):
        for i in range(4):
            acc[4 * j + i] = jnp.zeros(acc.shape[1:], F32)

    @pl.loop(0, blocks)
    def _(b):
        s = lax.rem(b, SLOTS_AHEAD)

        @pl.when(b + SLOTS_AHEAD - 1 < blocks)
        def _():
            start(b + SLOTS_AHEAD - 1)

        n = counts[b]
        for live in range(1, groups + 1):

            @pl.when((n + GROUP - 1) // GROUP == live)
            def _():
                g = grad[pl.ds(pl.multiple_of(b * t, t), t), :].T
                for q in range(live):
                    copy(b, q).wait()
                for q in range(live):
                    wide = jnp.concatenate(
                        [tbuf[s, q * GROUP + i] for i in range(GROUP)], axis=1
                    )
                    terms = jnp.dot(g, wide, preferred_element_type=F32)
                    for i in range(GROUP):
                        k = q * GROUP + i
                        term = terms[:, i * t : (i + 1) * t]
                        if q == live - 1 and i > 0:
                            term = jnp.where(k < n, term, 0.0)
                        acc[cols[k, b]] += term

    def flush(c):
        s = lax.rem(c, FLUSHES)
        return pltpu.make_async_copy(
            stage.at[s], out.at[pl.ds(c * OUT_CHUNK, OUT_CHUNK)], out_sems.at[s]
        )

    @pl.loop(0, total // OUT_CHUNK)
    def _(c):
        s = lax.rem(c, FLUSHES)

        @pl.when(c >= FLUSHES)
        def _():
            flush(c - FLUSHES).wait()

        @pl.loop(0, OUT_CHUNK // 4)
        def _(j):
            for i in range(4):
                stage[s, 4 * j + i] = acc[c * OUT_CHUNK + 4 * j + i].astype(BF16)

        flush(c).start()

    for c in range(total // OUT_CHUNK - FLUSHES, total // OUT_CHUNK):
        flush(c).wait()


def spmm_t(grad, tiles, columns, counts, total):
    blocks, slots, t, _ = tiles.shape
    width = grad.shape[-1]
    return pl.pallas_call(
        bwd_kernel,
        grid_spec=pltpu.PrefetchScalarGridSpec(
            num_scalar_prefetch=2,
            grid=(1,),
            in_specs=[
                pl.BlockSpec(memory_space=pl.ANY),
                pl.BlockSpec((blocks * t, width), lambda i, *_: (0, 0)),
            ],
            out_specs=pl.BlockSpec(memory_space=pl.ANY),
            scratch_shapes=[
                pltpu.VMEM((total, t, width), F32),
                pltpu.VMEM((SLOTS_AHEAD, slots, t, t), BF16),
                pltpu.VMEM((FLUSHES, OUT_CHUNK, t, width), BF16),
                pltpu.SemaphoreType.DMA((SLOTS_AHEAD, slots // GROUP)),
                pltpu.SemaphoreType.DMA((FLUSHES,)),
            ],
        ),
        out_shape=jax.ShapeDtypeStruct((total, t, width), BF16),
        compiler_params=pltpu.CompilerParams(vmem_limit_bytes=60 * 1024 * 1024),
        name="spmm_t",
    )(columns, counts, tiles, grad)


PARTS = 4


def settle_kernel(a, b, w, a_out, b_out, w_out, a_buf, b_buf, in_sems, out_sems):
    step = a.shape[0] // PARTS
    ins, outs = [], []
    for j, (src, buf, dst) in enumerate(((a, a_buf, a_out), (b, b_buf, b_out))):
        for i in range(PARTS):
            at = pl.ds(i * step, step)
            ins.append(pltpu.make_async_copy(src.at[at], buf.at[at], in_sems.at[j, i]))
            outs.append(pltpu.make_async_copy(buf.at[at], dst.at[at], out_sems.at[j, i]))
    for copy in ins:
        copy.start()
    w_out[...] = w[...].T
    for first, then in zip(ins, outs):
        first.wait()
        then.start()
    for copy in outs:
        copy.wait()


def settle(a, b, w):
    dma = pltpu.SemaphoreType.DMA((2, PARTS))
    return pl.pallas_call(
        settle_kernel,
        in_specs=[ANY, ANY, VM],
        out_specs=[ANY, ANY, VM],
        out_shape=[
            jax.ShapeDtypeStruct(a.shape, BF16),
            jax.ShapeDtypeStruct(b.shape, BF16),
            jax.ShapeDtypeStruct(w.shape[::-1], F32),
        ],
        scratch_shapes=[pltpu.VMEM(a.shape, BF16), pltpu.VMEM(b.shape, BF16), dma, dma],
        name="settle",
    )(a, b, w)


def local(features, tiles, columns, counts, weight, cotangent):
    rows_here, feat_local = features.shape
    blocks_here, slots, t, _ = tiles.shape
    total_blocks = blocks_here * lax.axis_size("row")
    columns = columns.T
    mixed_grad, act, wgrad = forward(features, cotangent, weight, tiles, columns, counts)
    part = spmm_t(mixed_grad.reshape(features.shape), tiles, columns, counts, total_blocks)
    act, feature_grad, weight_grad = reduce_all(
        part.reshape(N_ROW, rows_here, feat_local), act, wgrad
    )
    act, feature_grad, weight_grad = settle(act.reshape(features.shape), feature_grad, weight_grad)
    return act, feature_grad, weight_grad.T


def solution(mesh):
    in_specs = (
        P("row", "rep"),
        P("row", None, None, None),
        P("row", None),
        P("row"),
        P(None, "rep"),
        P("row", "rep"),
    )
    out_specs = (P("row", "rep"), P("row", "rep"), P("rep", "row"))
    return jax.shard_map(local, mesh=mesh, in_specs=in_specs, out_specs=out_specs, check_vma=False)
```

```python
import functools

import jax
import jax.numpy as jnp
from jax import lax
from jax.experimental import pallas as pl
from jax.experimental.pallas import tpu as pltpu
from jax.sharding import PartitionSpec as P

F32 = jnp.float32
BF16 = jnp.bfloat16
MESH = pl.DeviceIdType.MESH
ROWS_Y = 4
N_ROW = 16
N_REP = 8
ANY = pl.BlockSpec(memory_space=pl.ANY)
VM = pl.BlockSpec(memory_space=pltpu.VMEM)


class Place:
    def __init__(self):
        self.row = lax.axis_index("row")
        self.rep = lax.axis_index("rep")
        self.c = lax.rem(self.row, 2)
        self.y = lax.rem(self.row // 2, ROWS_Y)
        self.h = self.row // (2 * ROWS_Y)

    def slot(self, other, dy, sib=False):
        h = 1 - self.h if other else self.h
        c = 1 - self.c if sib else self.c
        return (h * ROWS_Y + lax.rem(self.y + dy + ROWS_Y, ROWS_Y)) * 2 + c

    def at(self, other, dy, sib=False):
        return (self.slot(other, dy, sib), self.rep)

    def peer_at(self, d):
        x = lax.rem(self.rep // 4 + d // 4, 2)
        z1 = lax.rem(lax.rem(self.rep, 4) // 2 + lax.rem(d, 4) // 2, 2)
        z0 = lax.rem(self.rep + d, 2)
        return x * 4 + z1 * 2 + z0

    def peer(self, d):
        x, z = self.rep // 4, lax.rem(self.rep, 4)
        if d >= 4:
            x = 1 - x
        if d % 4 == 1:
            z = z + 1 - 2 * lax.rem(z, 2)
        elif d % 4 == 2:
            z = lax.rem(z + 2, 4)
        elif d % 4 == 3:
            z = 3 - z
        return x * 4 + z


def greet(partners):
    barrier = pltpu.get_barrier_semaphore()
    for partner in partners:
        pl.semaphore_signal(barrier, inc=1, device_id=partner, device_id_type=MESH)
    pl.semaphore_wait(barrier, len(partners))


class Sends:
    def __init__(self, sems):
        self.sems, self.live = sems, []

    def __call__(self, src, dst, recv_sem, device):
        copy = pltpu.make_async_remote_copy(
            src_ref=src,
            dst_ref=dst,
            send_sem=self.sems.at[len(self.live)],
            recv_sem=recv_sem,
            device_id=device,
            device_id_type=MESH,
        )
        copy.start()
        self.live.append(copy)

    def finish(self):
        for copy in self.live:
            copy.wait_send()


def arrived(dst, recv_sem):
    pltpu.make_async_copy(dst, dst, recv_sem).wait()


CHUNKS = 4
CROSS = 0


PAIR = 2


def forward_kernel(
    feats, cot, weight, tiles, cols, counts, mixed_grad, act, wgrad,
    full, blocks, cots, ws, w, mixed, m, grad, back,
    send_sems, recv_sems, cot_recv, w_recv, w_sib, m_send, m_recv, back_recv, local_sems,
):
    here = Place()
    n_blocks, slots, t, _ = tiles.shape
    step = n_blocks // CHUNKS
    piece = cot.shape[0] // N_REP
    width = cot.shape[1]
    half = weight.shape[0] // 2
    peers = [here.peer(d) for d in range(1, N_REP)]
    sib = here.at(False, 0, True)
    up, down, across = here.at(False, 1), here.at(False, -1), here.at(True, 0)

    def base(slot):
        return slot * n_blocks

    own = [
        pltpu.make_async_copy(feats, full.at[pl.ds(base(here.row), n_blocks)], local_sems.at[0]),
        pltpu.make_async_copy(weight, ws.at[here.rep], local_sems.at[1]),
        pltpu.make_async_copy(
            cot.at[pl.ds(pl.multiple_of(here.rep * piece, piece), piece)],
            cots.at[here.rep], local_sems.at[2],
        ),
        pltpu.make_async_copy(tiles, blocks, local_sems.at[3]),
    ]
    greet([sib, up, down, across] + [(here.row, q) for q in peers])
    send = Sends(send_sems)

    def rows(chunk):
        return pl.ds(chunk * step, step)

    def place(slot, chunk):
        return full.at[pl.ds(base(slot) + chunk * step, step)]

    columns = [
        (False, -1), (False, 1), (False, 2), (True, 0), (True, -1), (True, 1), (True, 2),
    ]
    slots_of = [here.slot(*column) for column in columns]
    opposite = [(i + CHUNKS // 2) % CHUNKS for i in range(CHUNKS)]

    for i in range(CHUNKS):
        send(feats.at[rows(i)], place(here.row, i), recv_sems.at[3, i], across)
    for a, b in enumerate(opposite):
        send(feats.at[rows(a)], place(here.row, a), recv_sems.at[0, a], up)
        send(feats.at[rows(b)], place(here.row, b), recv_sems.at[1, b], down)
    for i in range(CHUNKS):
        send(feats.at[rows(i)], place(here.row, i), recv_sems.at[7, i], sib)
    mine = pl.ds(pl.multiple_of(here.c * half, half), half)
    theirs = pl.ds(pl.multiple_of((1 - here.c) * half, half), half)
    for d, q in enumerate(peers):
        send(weight.at[mine], ws.at[here.rep, mine], w_recv.at[d], (here.row, q))
    for d, q in enumerate(peers):
        send(
            cot.at[pl.ds(pl.multiple_of(q * piece, piece), piece)],
            cots.at[here.rep], cot_recv.at[d], (here.row, q),
        )
    for copy in own:
        copy.start()

    def take(kind, chunk, on=None):
        src = place(slots_of[kind], chunk)
        arrived(src, recv_sems.at[kind, chunk])
        if on is not None:
            send(src, src, recv_sems.at[2 if kind < 3 else 6, chunk], on)
        if kind < 3 and chunk == CROSS:
            send(src, src, recv_sems.at[4 + kind, chunk], across)
        send(src, src, recv_sems.at[8 + kind, chunk], sib)

    for k in (0, 4):
        for a, b in enumerate(opposite):
            take(k, a, up if a < CHUNKS // 2 and (k, a) != (4, CROSS) else None)
            take(k + 1, b, down if b >= CHUNKS // 2 and (k, b) != (4, CROSS) else None)
            if k == 0:
                src = place(slots_of[3], a)
                arrived(src, recv_sems.at[3, a])
                if a != CROSS:
                    send(src, src, recv_sems.at[4, a], up)
                    send(src, src, recv_sems.at[5, a], down)
                send(src, src, recv_sems.at[11, a], sib)
        for i in range(CHUNKS):
            take(k + 2, i)
        if k == 0:
            for d, q in enumerate(peers):
                arrived(ws.at[q, mine], w_recv.at[d])
                send(ws.at[q, mine], ws.at[q, mine], w_sib.at[d], sib)

    for d, q in enumerate(peers):
        arrived(ws.at[q, theirs], w_sib.at[d])
        arrived(cots.at[q], cot_recv.at[d])
    for copy in own:
        copy.wait()
    for r in range(N_REP):
        w[:, r * width : (r + 1) * width] = ws[r]
    for kind, column in enumerate([(False, 0)] + columns):
        for i in range(CHUNKS):
            arrived(place(here.slot(*column, True), i), recv_sems.at[7 + kind, i])

    strips = piece // t

    def shift(d, i):
        q, at = here.peer_at(d), pl.ds(i * t, t)
        return q, pltpu.make_async_remote_copy(
            src_ref=mixed.at[q, at], dst_ref=m.at[here.rep, at],
            send_sem=m_send.at[d - 1, i], recv_sem=m_recv.at[d - 1, i],
            device_id=(here.row, q), device_id_type=MESH,
        )

    def mix(i):
        at = pl.ds(i * t, t)

        @pl.loop(0, N_REP // PAIR)
        def _(j):
            copies = []
            for e in range(PAIR):
                q, copy = shift(lax.rem(3 * (j * PAIR + e), N_REP), i)
                copies.append(copy)
                b = q * strips + i
                n = counts[b]
                left = jnp.concatenate(
                    [jnp.where(k < n, blocks[b, k], jnp.zeros((), BF16)) for k in range(slots)],
                    axis=1,
                )
                right = jnp.concatenate([full[cols[k, b]] for k in range(slots)], axis=0)
                mixed[q, at, :] = jnp.dot(left, right, preferred_element_type=F32).astype(BF16)

            @pl.when(j > 0)
            def _():
                copies[0].start()

            for copy in copies[1:]:
                copy.start()

        m[here.rep, at, :] = mixed[here.rep, at, :]

    def whole(i):
        at = pl.ds(i * t, t)
        for d, q in enumerate(peers):
            arrived(m.at[q, at], m_recv.at[d, i])
        x = jnp.concatenate([m[r, at, :] for r in range(N_REP)], axis=1)
        c = jnp.concatenate([cots[r, at, :] for r in range(N_REP)], axis=1)
        pre = jnp.dot(x, w[...], preferred_element_type=F32)
        sig = jax.nn.sigmoid(pre)
        out = (pre * sig).astype(BF16)
        g = (c.astype(F32) * sig * (1.0 + pre * (1.0 - sig))).astype(BF16)
        grad[at, :] = g
        b = lax.dot_general(
            g, w[...], (((1,), (1,)), ((), ())), preferred_element_type=F32
        ).astype(BF16)
        for r in range(N_REP):
            act[r, at, :] = out[:, r * width : (r + 1) * width]
            back[r, at, :] = b[:, r * width : (r + 1) * width]
        for d, q in enumerate(peers):
            send(back.at[q, at], mixed_grad.at[here.rep, at], back_recv.at[d, i], (here.row, q))

    mix(0)
    for i in range(1, strips):
        mix(i)
        whole(i - 1)
    whole(strips - 1)
    last = pltpu.make_async_copy(back.at[here.rep], mixed_grad.at[here.rep], local_sems.at[4])
    last.start()
    for r in range(N_REP):
        wgrad[r] = lax.dot_general(
            m[r], grad[...], (((0,), (0,)), ((), ())), preferred_element_type=F32
        ).astype(BF16)
    last.wait()
    for d, q in enumerate(peers):
        for i in range(strips):
            arrived(mixed_grad.at[q, pl.ds(i * t, t)], back_recv.at[d, i])
    for d in range(1, N_REP):
        for i in range(strips):
            shift(d, i)[1].wait_send()
    send.finish()


def forward(features, cotangent, weight, tiles, columns, counts):
    rows, width = features.shape
    n_blocks, _, t, _ = tiles.shape
    piece = rows // N_REP
    strips = piece // t
    dma = pltpu.SemaphoreType.DMA
    smem = pl.BlockSpec(memory_space=pltpu.SMEM)
    stack = pltpu.VMEM((N_REP, piece, width), BF16)
    return pl.pallas_call(
        forward_kernel,
        in_specs=[ANY] * 4 + [smem] * 2,
        out_specs=[ANY, VM, VM],
        out_shape=[
            jax.ShapeDtypeStruct((N_REP, piece, width), BF16),
            jax.ShapeDtypeStruct((N_REP, piece, width), BF16),
            jax.ShapeDtypeStruct((N_REP, width, N_REP * width), BF16),
        ],
        scratch_shapes=[
            pltpu.VMEM((N_ROW * n_blocks, t, width), BF16),
            pltpu.VMEM(tiles.shape, BF16),
            stack,
            pltpu.VMEM((N_REP,) + weight.shape, BF16),
            pltpu.VMEM((N_REP * width, N_REP * width), BF16),
            stack, stack,
            pltpu.VMEM((piece, N_REP * width), BF16),
            stack,
            dma((15 * CHUNKS + 21 + 7 * strips,)), dma((15, CHUNKS)),
            dma((7,)), dma((7,)), dma((7,)), dma((7, strips)), dma((7, strips)), dma((7, strips)),
            dma((5,)),
        ],
        compiler_params=pltpu.CompilerParams(
            collective_id=0, has_side_effects=True, vmem_limit_bytes=60 * 1024 * 1024
        ),
        name="forward",
    )(features.reshape(n_blocks, t, width), cotangent, weight, tiles, columns, counts)


OFFSETS = (2, 1, -1, 0)
SUM_ROWS = 128


def reduce_kernel(
    part, act, wgrad, act_out, out, wg_out,
    own, theirs, far_up, far_down, near_up, near_down, cross, early, own_act,
    wg_own, wg_sib, wg_in, wg_half, wg_row, wg_fin, wg_fin_sib,
    send_sems, load_sems, sib_recv, far_recv, near_recv, cross_recv, early_recv,
    act_recv, wg_recv, row_recv, pair_recv, local_sems,
):
    here = Place()
    step = own.shape[1] // CHUNKS
    half = CHUNKS // 2
    peers = [here.peer(d) for d in range(1, N_REP)]
    sib = here.at(False, 0, True)
    up, down, across = here.at(False, 1), here.at(False, -1), here.at(True, 0)
    columns = [(o, dy) for o in (True, False) for dy in OFFSETS][:-1]

    edge = wg_half.shape[1]
    mine = pl.ds(pl.multiple_of(here.c * edge, edge), edge)
    theirs_of_pair = pl.ds(pl.multiple_of((1 - here.c) * edge, edge), edge)

    def rows(i):
        return pl.ds(i * step, step)

    loads = {}
    for r in range(8):
        slot = here.slot(r < 4, OFFSETS[r % 4])
        for i in range(CHUNKS):
            loads[r, i] = pltpu.make_async_copy(
                part.at[slot, rows(i)], own.at[r, rows(i)], load_sems.at[r, i]
            )
    extra = [
        pltpu.make_async_copy(act.at[here.rep], own_act, local_sems.at[0]),
        pltpu.make_async_copy(wgrad.at[:, mine], wg_own, local_sems.at[1]),
    ]
    for load in extra:
        load.start()
    for load in loads.values():
        load.start()
    greet([sib] + [here.at(*column) for column in columns] + [(here.row, q) for q in peers])

    send = Sends(send_sems)
    first = [(0, i) for i in range(CHUNKS)] + [(r, CROSS) for r in (1, 2, 3)]
    rest = [(r, i) for r in (1, 2, 4, 3, 5, 6, 7) for i in range(CHUNKS)]
    for r, i in first + [k for k in rest if k not in first]:
        slot = here.slot(r < 4, OFFSETS[r % 4], True)
        send(part.at[slot, rows(i)], theirs.at[r, rows(i)], sib_recv.at[r, i], sib)
        if (r, i) == first[-1]:
            send(wgrad.at[:, theirs_of_pair], wg_sib, pair_recv.at[0], sib)

    def total(r, i, more, dst=None):
        loads[r, i].wait()
        arrived(theirs.at[r, rows(i)], sib_recv.at[r, i])
        target = own.at[r] if dst is None else dst

        @pl.loop(0, step // SUM_ROWS, unroll=2)
        def _(j):
            at = pl.ds(pl.multiple_of(i * step + j * SUM_ROWS, SUM_ROWS), SUM_ROWS)
            acc = own[r, at, :].astype(F32) + theirs[r, at, :].astype(F32)
            for ref, base in more:
                at2 = pl.ds(pl.multiple_of(base * step + j * SUM_ROWS, SUM_ROWS), SUM_ROWS)
                acc = acc + ref[at2, :].astype(F32)
            if dst is not None:
                acc = acc.T
            target[at, :] = acc.astype(BF16)

    def plus(hh, k, i, more):
        if hh == 1 and i == CROSS:
            arrived(early.at[k], early_recv.at[k])
            return more + [(early.at[k], 0)]
        return more

    def skip(hh, i):
        return hh == 0 and i == CROSS

    def far(hh):
        r = 4 * hh
        for i in (1, 0):
            for j, land, to in ((i, far_up, up), (i + half, far_down, down)):
                if skip(hh, j):
                    continue
                total(r, j, plus(hh, 0, j, []))
                send(
                    own.at[r, rows(j)], land.at[hh, rows(i)],
                    far_recv.at[hh, int(j >= half), i], to,
                )

    def near(hh, i, j, up_more, down_more):
        r, s = 4 * hh + 1, 4 * hh + 2
        if not skip(hh, i):
            total(r, i, plus(hh, 1, i, up_more))
            send(own.at[r, rows(i)], near_up.at[hh, rows(i)], near_recv.at[hh, 0, i], up)
        if not skip(hh, j):
            total(s, j, plus(hh, 2, j, down_more))
            send(own.at[s, rows(j)], near_down.at[hh, rows(j)], near_recv.at[hh, 1, j], down)

    def near_first(hh):
        for i in (1, 0):
            near(hh, i + half, i, [], [])

    def near_last(hh):
        for i in (1, 0):
            if not skip(hh, i):
                arrived(far_up.at[hh, rows(i)], far_recv.at[hh, 0, i])
            arrived(far_down.at[hh, rows(i)], far_recv.at[hh, 1, i])
            near(hh, i, i + half, [(far_up.at[hh], i)], [(far_down.at[hh], i)])

    def final(hh):
        for i in (3, 1, 2, 0):
            if skip(hh, i):
                continue
            arrived(near_up.at[hh, rows(i)], near_recv.at[hh, 0, i])
            arrived(near_down.at[hh, rows(i)], near_recv.at[hh, 1, i])
            more = [(near_up.at[hh], i), (near_down.at[hh], i)]
            if hh == 0:
                total(3, i, more)
                send(own.at[3, rows(i)], cross.at[rows(i)], cross_recv.at[i], across)
            else:
                arrived(cross.at[rows(i)], cross_recv.at[i])
                total(7, i, more + [(cross, i)], out)

    far(0)
    for k in range(4):
        total(k, CROSS, [])
        if k < 3:
            send(own.at[k, rows(CROSS)], early.at[k], early_recv.at[k], across)
        else:
            send(own.at[k, rows(CROSS)], cross.at[rows(CROSS)], cross_recv.at[CROSS], across)
    near_first(0)

    extra[1].wait()
    arrived(wg_sib, pair_recv.at[0])

    @pl.loop(0, N_REP)
    def _(j):
        wg_own[j] = (wg_own[j].astype(F32) + wg_sib[j].astype(F32)).astype(BF16)

    for d, q in enumerate(peers):
        send(wg_own.at[q], wg_in.at[d], wg_recv.at[d], (here.row, q))
    for d, q in enumerate(peers):
        send(act.at[q], act_out.at[here.rep], act_recv.at[d], (here.row, q))
    extra[0].wait()
    keep = pltpu.make_async_copy(own_act, act_out.at[here.rep], local_sems.at[0])
    keep.start()
    far(1)
    near_last(0)

    for d in range(N_REP - 1):
        arrived(wg_in.at[d], wg_recv.at[d])

    @pl.loop(0, wg_half.shape[0])
    def _(j):
        at = pl.ds(pl.multiple_of(j * 128, 128), 128)
        acc = wg_own[here.rep, :, at].astype(F32)
        for d in range(N_REP - 1):
            acc = acc + wg_in[d, :, at].astype(F32)
        wg_half[j] = acc.astype(BF16)

    for k, (o, dy) in enumerate(columns):
        send(
            wg_half.at[here.slot(o, dy) // 2], wg_row.at[k], row_recv.at[k], here.at(o, dy)
        )
    near_first(1)
    final(0)
    near_last(1)
    for k in range(len(columns)):
        arrived(wg_row.at[k], row_recv.at[k])
    acc = wg_half[here.row // 2].astype(F32)
    for k in range(len(columns)):
        acc = acc + wg_row[k].astype(F32)
    wg_fin[...] = acc
    send(wg_fin, wg_fin_sib, pair_recv.at[1], sib)
    final(1)
    arrived(wg_fin_sib, pair_recv.at[1])

    @pl.when(here.c == 0)
    def _():
        wg_out[:edge, :] = wg_fin[:, :edge]
        wg_out[edge:, :] = wg_fin_sib[:, :edge]

    @pl.when(here.c == 1)
    def _():
        wg_out[:edge, :] = wg_fin_sib[:, edge:]
        wg_out[edge:, :] = wg_fin[:, edge:]

    keep.wait()
    for d, q in enumerate(peers):
        arrived(act_out.at[q], act_recv.at[d])
    send.finish()


def reduce_all(part, act, wgrad):
    n, rows, width = part.shape
    n_rep, k, wide = wgrad.shape
    edge = k // 2
    dma = pltpu.SemaphoreType.DMA
    return pl.pallas_call(
        reduce_kernel,
        in_specs=[ANY] * 3,
        out_specs=[ANY, VM, VM],
        out_shape=[
            jax.ShapeDtypeStruct(act.shape, BF16),
            jax.ShapeDtypeStruct((rows, width), BF16),
            jax.ShapeDtypeStruct((k, wide // n), F32),
        ],
        scratch_shapes=[
            pltpu.VMEM((8, rows, width), BF16),
            pltpu.VMEM((8, rows, width), BF16),
            pltpu.VMEM((2, rows // 2, width), BF16),
            pltpu.VMEM((2, rows // 2, width), BF16),
            pltpu.VMEM((2, rows, width), BF16),
            pltpu.VMEM((2, rows, width), BF16),
            pltpu.VMEM((rows, width), BF16),
            pltpu.VMEM((3, rows // CHUNKS, width), BF16),
            pltpu.VMEM(act.shape[1:], BF16),
            pltpu.VMEM((n_rep, edge, wide), BF16),
            pltpu.VMEM((n_rep, edge, wide), BF16),
            pltpu.VMEM((n_rep - 1, edge, wide), BF16),
            pltpu.VMEM((wide // 128, edge, 128), BF16),
            pltpu.VMEM((7, edge, 128), BF16),
            pltpu.VMEM((edge, 128), F32),
            pltpu.VMEM((edge, 128), F32),
            dma((15 * CHUNKS + 23,)), dma((8, CHUNKS)), dma((8, CHUNKS)), dma((2, 2, CHUNKS // 2)), dma((2, 2, CHUNKS)),
            dma((CHUNKS,)), dma((3,)), dma((7,)), dma((7,)), dma((7,)), dma((2,)), dma((2,)),
        ],
        compiler_params=pltpu.CompilerParams(collective_id=2, has_side_effects=True),
        name="reduce_all",
    )(part, act, wgrad)


SLOTS_AHEAD = 8


GROUP = 4
OUT_CHUNK = 16
FLUSHES = 8


def bwd_kernel(cols, counts, tiles, grad, out, acc, tbuf, stage, sems, out_sems):
    blocks, slots, t, _ = tiles.shape
    total = acc.shape[0]
    groups = slots // GROUP

    def copy(b, q):
        s = lax.rem(b, SLOTS_AHEAD)
        at = pl.ds(q * GROUP, GROUP)
        return pltpu.make_async_copy(tiles.at[b, at], tbuf.at[s, at], sems.at[s, q])

    def start(b):
        for q in range(groups):

            @pl.when(q * GROUP < counts[b])
            def _():
                copy(b, q).start()

    for b in range(SLOTS_AHEAD - 1):
        start(b)

    @pl.loop(0, total // 4)
    def _(j):
        for i in range(4):
            acc[4 * j + i] = jnp.zeros(acc.shape[1:], F32)

    @pl.loop(0, blocks)
    def _(b):
        s = lax.rem(b, SLOTS_AHEAD)

        @pl.when(b + SLOTS_AHEAD - 1 < blocks)
        def _():
            start(b + SLOTS_AHEAD - 1)

        n = counts[b]
        for live in range(1, groups + 1):

            @pl.when((n + GROUP - 1) // GROUP == live)
            def _():
                g = grad[pl.ds(pl.multiple_of(b * t, t), t), :].T
                for q in range(live):
                    copy(b, q).wait()
                for q in range(live):
                    wide = jnp.concatenate(
                        [tbuf[s, q * GROUP + i] for i in range(GROUP)], axis=1
                    )
                    terms = jnp.dot(g, wide, preferred_element_type=F32)
                    for i in range(GROUP):
                        k = q * GROUP + i
                        term = terms[:, i * t : (i + 1) * t]
                        if q == live - 1 and i > 0:
                            term = jnp.where(k < n, term, 0.0)
                        acc[cols[k, b]] += term

    def flush(c):
        s = lax.rem(c, FLUSHES)
        return pltpu.make_async_copy(
            stage.at[s], out.at[pl.ds(c * OUT_CHUNK, OUT_CHUNK)], out_sems.at[s]
        )

    @pl.loop(0, total // OUT_CHUNK)
    def _(c):
        s = lax.rem(c, FLUSHES)

        @pl.when(c >= FLUSHES)
        def _():
            flush(c - FLUSHES).wait()

        @pl.loop(0, OUT_CHUNK // 4)
        def _(j):
            for i in range(4):
                stage[s, 4 * j + i] = acc[c * OUT_CHUNK + 4 * j + i].astype(BF16)

        flush(c).start()

    for c in range(total // OUT_CHUNK - FLUSHES, total // OUT_CHUNK):
        flush(c).wait()


def spmm_t(grad, tiles, columns, counts, total):
    blocks, slots, t, _ = tiles.shape
    width = grad.shape[-1]
    return pl.pallas_call(
        bwd_kernel,
        grid_spec=pltpu.PrefetchScalarGridSpec(
            num_scalar_prefetch=2,
            grid=(1,),
            in_specs=[
                pl.BlockSpec(memory_space=pl.ANY),
                pl.BlockSpec((blocks * t, width), lambda i, *_: (0, 0)),
            ],
            out_specs=pl.BlockSpec(memory_space=pl.ANY),
            scratch_shapes=[
                pltpu.VMEM((total, t, width), F32),
                pltpu.VMEM((SLOTS_AHEAD, slots, t, t), BF16),
                pltpu.VMEM((FLUSHES, OUT_CHUNK, t, width), BF16),
                pltpu.SemaphoreType.DMA((SLOTS_AHEAD, slots // GROUP)),
                pltpu.SemaphoreType.DMA((FLUSHES,)),
            ],
        ),
        out_shape=jax.ShapeDtypeStruct((total, t, width), BF16),
        compiler_params=pltpu.CompilerParams(vmem_limit_bytes=60 * 1024 * 1024),
        name="spmm_t",
    )(columns, counts, tiles, grad)


PARTS = 4


def settle_kernel(a, b, w, a_out, b_out, w_out, a_buf, b_buf, in_sems, out_sems):
    step = a.shape[0] // PARTS
    ins, outs = [], []
    for j, (src, buf, dst) in enumerate(((a, a_buf, a_out), (b, b_buf, b_out))):
        for i in range(PARTS):
            at = pl.ds(i * step, step)
            ins.append(pltpu.make_async_copy(src.at[at], buf.at[at], in_sems.at[j, i]))
            outs.append(pltpu.make_async_copy(buf.at[at], dst.at[at], out_sems.at[j, i]))
    for copy in ins:
        copy.start()
    w_out[...] = w[...].T
    for first, then in zip(ins, outs):
        first.wait()
        then.start()
    for copy in outs:
        copy.wait()


def settle(a, b, w):
    dma = pltpu.SemaphoreType.DMA((2, PARTS))
    return pl.pallas_call(
        settle_kernel,
        in_specs=[ANY, ANY, VM],
        out_specs=[ANY, ANY, VM],
        out_shape=[
            jax.ShapeDtypeStruct(a.shape, BF16),
            jax.ShapeDtypeStruct(b.shape, BF16),
            jax.ShapeDtypeStruct(w.shape[::-1], F32),
        ],
        scratch_shapes=[pltpu.VMEM(a.shape, BF16), pltpu.VMEM(b.shape, BF16), dma, dma],
        name="settle",
    )(a, b, w)


def local(features, tiles, columns, counts, weight, cotangent):
    rows_here, feat_local = features.shape
    blocks_here, slots, t, _ = tiles.shape
    total_blocks = blocks_here * lax.axis_size("row")
    columns = columns.T
    mixed_grad, act, wgrad = forward(features, cotangent, weight, tiles, columns, counts)
    part = spmm_t(mixed_grad.reshape(features.shape), tiles, columns, counts, total_blocks)
    act, feature_grad, weight_grad = reduce_all(
        part.reshape(N_ROW, rows_here, feat_local), act, wgrad
    )
    act, feature_grad, weight_grad = settle(act.reshape(features.shape), feature_grad, weight_grad)
    return act, feature_grad, weight_grad.T


def solution(mesh):
    in_specs = (
        P("row", "rep"),
        P("row", None, None, None),
        P("row", None),
        P("row"),
        P(None, "rep"),
        P("row", "rep"),
    )
    out_specs = (P("row", "rep"), P("row", "rep"), P("rep", "row"))
    return jax.shard_map(local, mesh=mesh, in_specs=in_specs, out_specs=out_specs, check_vma=False)
```

```python
import functools

import jax
import jax.numpy as jnp
from jax import lax
from jax.experimental import pallas as pl
from jax.experimental.pallas import tpu as pltpu
from jax.sharding import PartitionSpec as P

F32 = jnp.float32
BF16 = jnp.bfloat16
MESH = pl.DeviceIdType.MESH
ROWS_Y = 4
N_ROW = 16
N_REP = 8
ANY = pl.BlockSpec(memory_space=pl.ANY)
VM = pl.BlockSpec(memory_space=pltpu.VMEM)


class Place:
    def __init__(self):
        self.row = lax.axis_index("row")
        self.rep = lax.axis_index("rep")
        self.c = lax.rem(self.row, 2)
        self.y = lax.rem(self.row // 2, ROWS_Y)
        self.h = self.row // (2 * ROWS_Y)

    def slot(self, other, dy, sib=False):
        h = 1 - self.h if other else self.h
        c = 1 - self.c if sib else self.c
        return (h * ROWS_Y + lax.rem(self.y + dy + ROWS_Y, ROWS_Y)) * 2 + c

    def at(self, other, dy, sib=False):
        return (self.slot(other, dy, sib), self.rep)

    def peer_at(self, d):
        x = lax.rem(self.rep // 4 + d // 4, 2)
        z1 = lax.rem(lax.rem(self.rep, 4) // 2 + lax.rem(d, 4) // 2, 2)
        z0 = lax.rem(self.rep + d, 2)
        return x * 4 + z1 * 2 + z0

    def peer(self, d):
        x, z = self.rep // 4, lax.rem(self.rep, 4)
        if d >= 4:
            x = 1 - x
        if d % 4 == 1:
            z = z + 1 - 2 * lax.rem(z, 2)
        elif d % 4 == 2:
            z = lax.rem(z + 2, 4)
        elif d % 4 == 3:
            z = 3 - z
        return x * 4 + z


def greet(partners):
    barrier = pltpu.get_barrier_semaphore()
    for partner in partners:
        pl.semaphore_signal(barrier, inc=1, device_id=partner, device_id_type=MESH)
    pl.semaphore_wait(barrier, len(partners))


class Sends:
    def __init__(self, sems):
        self.sems, self.live = sems, []

    def __call__(self, src, dst, recv_sem, device):
        copy = pltpu.make_async_remote_copy(
            src_ref=src,
            dst_ref=dst,
            send_sem=self.sems.at[len(self.live)],
            recv_sem=recv_sem,
            device_id=device,
            device_id_type=MESH,
        )
        copy.start()
        self.live.append(copy)

    def finish(self):
        for copy in self.live:
            copy.wait_send()


def arrived(dst, recv_sem):
    pltpu.make_async_copy(dst, dst, recv_sem).wait()


CHUNKS = 4
CROSS = 0


PAIR = 2


def forward_kernel(
    feats, cot, weight, tiles, cols, counts, mixed_grad, act, wgrad,
    full, blocks, cots, ws, w, mixed, m, grad, back,
    send_sems, recv_sems, cot_recv, w_recv, w_sib, m_send, m_recv, back_recv, local_sems,
):
    here = Place()
    n_blocks, slots, t, _ = tiles.shape
    step = n_blocks // CHUNKS
    piece = cot.shape[0] // N_REP
    width = cot.shape[1]
    half = weight.shape[0] // 2
    peers = [here.peer(d) for d in range(1, N_REP)]
    sib = here.at(False, 0, True)
    up, down, across = here.at(False, 1), here.at(False, -1), here.at(True, 0)

    def base(slot):
        return slot * n_blocks

    own = [
        pltpu.make_async_copy(feats, full.at[pl.ds(base(here.row), n_blocks)], local_sems.at[0]),
        pltpu.make_async_copy(weight, ws.at[here.rep], local_sems.at[1]),
        pltpu.make_async_copy(
            cot.at[pl.ds(pl.multiple_of(here.rep * piece, piece), piece)],
            cots.at[here.rep], local_sems.at[2],
        ),
        pltpu.make_async_copy(tiles, blocks, local_sems.at[3]),
    ]
    greet([sib, up, down, across] + [(here.row, q) for q in peers])
    send = Sends(send_sems)

    def rows(chunk):
        return pl.ds(chunk * step, step)

    def place(slot, chunk):
        return full.at[pl.ds(base(slot) + chunk * step, step)]

    columns = [
        (False, -1), (False, 1), (False, 2), (True, 0), (True, -1), (True, 1), (True, 2),
    ]
    slots_of = [here.slot(*column) for column in columns]
    opposite = [(i + CHUNKS // 2) % CHUNKS for i in range(CHUNKS)]

    mine = pl.ds(pl.multiple_of(here.c * half, half), half)
    theirs = pl.ds(pl.multiple_of((1 - here.c) * half, half), half)
    beside = peers[3]
    for d in (4, 1, 2, 3):
        send(weight.at[mine], ws.at[here.rep, mine], w_recv.at[d - 1], (here.row, peers[d - 1]))
    for i in range(CHUNKS):
        send(feats.at[rows(i)], place(here.row, i), recv_sems.at[3, i], across)
    for a, b in enumerate(opposite):
        send(feats.at[rows(a)], place(here.row, a), recv_sems.at[0, a], up)
        send(feats.at[rows(b)], place(here.row, b), recv_sems.at[1, b], down)
    for i in range(CHUNKS):
        send(feats.at[rows(i)], place(here.row, i), recv_sems.at[7, i], sib)
    for d, q in enumerate(peers):
        send(
            cot.at[pl.ds(pl.multiple_of(q * piece, piece), piece)],
            cots.at[here.rep], cot_recv.at[d], (here.row, q),
        )
    for copy in own:
        copy.start()

    def take(kind, chunk, on=None):
        src = place(slots_of[kind], chunk)
        arrived(src, recv_sems.at[kind, chunk])
        if on is not None:
            send(src, src, recv_sems.at[2 if kind < 3 else 6, chunk], on)
        if kind < 3 and chunk == CROSS:
            send(src, src, recv_sems.at[4 + kind, chunk], across)
        send(src, src, recv_sems.at[8 + kind, chunk], sib)

    for k in (0, 4):
        for a, b in enumerate(opposite):
            take(k, a, up if a < CHUNKS // 2 and (k, a) != (4, CROSS) else None)
            take(k + 1, b, down if b >= CHUNKS // 2 and (k, b) != (4, CROSS) else None)
            if k == 0:
                src = place(slots_of[3], a)
                arrived(src, recv_sems.at[3, a])
                if a != CROSS:
                    send(src, src, recv_sems.at[4, a], up)
                    send(src, src, recv_sems.at[5, a], down)
                send(src, src, recv_sems.at[11, a], sib)
        if k == 0:
            arrived(ws.at[beside, mine], w_recv.at[3])
            for d in (1, 2, 3):
                send(
                    ws.at[beside, mine], ws.at[beside, mine], w_recv.at[d + 3],
                    (here.row, peers[d - 1]),
                )
        for i in range(CHUNKS):
            take(k + 2, i)
    for d, q in enumerate(peers):
        if d != 3:
            arrived(ws.at[q, mine], w_recv.at[d])
        send(ws.at[q, mine], ws.at[q, mine], w_sib.at[d], sib)

    for d, q in enumerate(peers):
        arrived(ws.at[q, theirs], w_sib.at[d])
        arrived(cots.at[q], cot_recv.at[d])
    for copy in own:
        copy.wait()
    for r in range(N_REP):
        w[:, r * width : (r + 1) * width] = ws[r]
    for kind, column in enumerate([(False, 0)] + columns):
        for i in range(CHUNKS):
            arrived(place(here.slot(*column, True), i), recv_sems.at[7 + kind, i])

    strips = piece // t

    def shift(d, i):
        q, at = here.peer_at(d), pl.ds(i * t, t)
        return q, pltpu.make_async_remote_copy(
            src_ref=mixed.at[q, at], dst_ref=m.at[here.rep, at],
            send_sem=m_send.at[d - 1, i], recv_sem=m_recv.at[d - 1, i],
            device_id=(here.row, q), device_id_type=MESH,
        )

    def mix(i):
        at = pl.ds(i * t, t)

        @pl.loop(0, N_REP // PAIR)
        def _(j):
            copies = []
            for e in range(PAIR):
                q, copy = shift(lax.rem(3 * (j * PAIR + e), N_REP), i)
                copies.append(copy)
                b = q * strips + i
                n = counts[b]
                left = jnp.concatenate(
                    [jnp.where(k < n, blocks[b, k], jnp.zeros((), BF16)) for k in range(slots)],
                    axis=1,
                )
                right = jnp.concatenate([full[cols[k, b]] for k in range(slots)], axis=0)
                mixed[q, at, :] = jnp.dot(left, right, preferred_element_type=F32).astype(BF16)

            @pl.when(j > 0)
            def _():
                copies[0].start()

            for copy in copies[1:]:
                copy.start()

        m[here.rep, at, :] = mixed[here.rep, at, :]

    def whole(i):
        at = pl.ds(i * t, t)
        for d, q in enumerate(peers):
            arrived(m.at[q, at], m_recv.at[d, i])
        x = jnp.concatenate([m[r, at, :] for r in range(N_REP)], axis=1)
        c = jnp.concatenate([cots[r, at, :] for r in range(N_REP)], axis=1)
        pre = jnp.dot(x, w[...], preferred_element_type=F32)
        sig = jax.nn.sigmoid(pre)
        out = (pre * sig).astype(BF16)
        g = (c.astype(F32) * sig * (1.0 + pre * (1.0 - sig))).astype(BF16)
        grad[at, :] = g
        b = lax.dot_general(
            g, w[...], (((1,), (1,)), ((), ())), preferred_element_type=F32
        ).astype(BF16)
        for r in range(N_REP):
            act[r, at, :] = out[:, r * width : (r + 1) * width]
            back[r, at, :] = b[:, r * width : (r + 1) * width]
        for d, q in enumerate(peers):
            send(back.at[q, at], mixed_grad.at[here.rep, at], back_recv.at[d, i], (here.row, q))

    mix(0)
    for i in range(1, strips):
        mix(i)
        whole(i - 1)
    whole(strips - 1)
    last = pltpu.make_async_copy(back.at[here.rep], mixed_grad.at[here.rep], local_sems.at[4])
    last.start()
    for r in range(N_REP):
        wgrad[r] = lax.dot_general(
            m[r], grad[...], (((0,), (0,)), ((), ())), preferred_element_type=F32
        ).astype(BF16)
    last.wait()
    for d, q in enumerate(peers):
        for i in range(strips):
            arrived(mixed_grad.at[q, pl.ds(i * t, t)], back_recv.at[d, i])
    for d in range(1, N_REP):
        for i in range(strips):
            shift(d, i)[1].wait_send()
    send.finish()


def forward(features, cotangent, weight, tiles, columns, counts):
    rows, width = features.shape
    n_blocks, _, t, _ = tiles.shape
    piece = rows // N_REP
    strips = piece // t
    dma = pltpu.SemaphoreType.DMA
    smem = pl.BlockSpec(memory_space=pltpu.SMEM)
    stack = pltpu.VMEM((N_REP, piece, width), BF16)
    return pl.pallas_call(
        forward_kernel,
        in_specs=[ANY] * 4 + [smem] * 2,
        out_specs=[ANY, VM, VM],
        out_shape=[
            jax.ShapeDtypeStruct((N_REP, piece, width), BF16),
            jax.ShapeDtypeStruct((N_REP, piece, width), BF16),
            jax.ShapeDtypeStruct((N_REP, width, N_REP * width), BF16),
        ],
        scratch_shapes=[
            pltpu.VMEM((N_ROW * n_blocks, t, width), BF16),
            pltpu.VMEM(tiles.shape, BF16),
            stack,
            pltpu.VMEM((N_REP,) + weight.shape, BF16),
            pltpu.VMEM((N_REP * width, N_REP * width), BF16),
            stack, stack,
            pltpu.VMEM((piece, N_REP * width), BF16),
            stack,
            dma((15 * CHUNKS + 21 + 7 * strips,)), dma((15, CHUNKS)),
            dma((7,)), dma((7,)), dma((7,)), dma((7, strips)), dma((7, strips)), dma((7, strips)),
            dma((5,)),
        ],
        compiler_params=pltpu.CompilerParams(
            collective_id=0, has_side_effects=True, vmem_limit_bytes=60 * 1024 * 1024
        ),
        name="forward",
    )(features.reshape(n_blocks, t, width), cotangent, weight, tiles, columns, counts)


OFFSETS = (2, 1, -1, 0)
SUM_ROWS = 128


def reduce_kernel(
    part, act, wgrad, act_out, out, wg_out,
    own, theirs, far_up, far_down, near_up, near_down, cross, early, own_act,
    wg_own, wg_sib, wg_in, wg_x, wg_half, wg_row, wg_fin, wg_fin_sib,
    send_sems, load_sems, sib_recv, far_recv, near_recv, cross_recv, early_recv,
    act_recv, wg_recv, row_recv, pair_recv, local_sems,
):
    here = Place()
    step = own.shape[1] // CHUNKS
    half = CHUNKS // 2
    peers = [here.peer(d) for d in range(1, N_REP)]
    sib = here.at(False, 0, True)
    up, down, across = here.at(False, 1), here.at(False, -1), here.at(True, 0)
    columns = [(o, dy) for o in (True, False) for dy in OFFSETS][:-1]

    edge = wg_half.shape[1]
    mine = pl.ds(pl.multiple_of(here.c * edge, edge), edge)
    theirs_of_pair = pl.ds(pl.multiple_of((1 - here.c) * edge, edge), edge)

    def rows(i):
        return pl.ds(i * step, step)

    loads = {}
    for r in range(8):
        slot = here.slot(r < 4, OFFSETS[r % 4])
        for i in range(CHUNKS):
            loads[r, i] = pltpu.make_async_copy(
                part.at[slot, rows(i)], own.at[r, rows(i)], load_sems.at[r, i]
            )
    extra = [
        pltpu.make_async_copy(act.at[here.rep], own_act, local_sems.at[0]),
        pltpu.make_async_copy(wgrad.at[:, mine], wg_own, local_sems.at[1]),
    ]
    for load in extra:
        load.start()
    for load in loads.values():
        load.start()
    greet([sib] + [here.at(*column) for column in columns] + [(here.row, q) for q in peers])

    send = Sends(send_sems)
    first = [(0, i) for i in range(CHUNKS)] + [(r, CROSS) for r in (1, 2, 3)]
    rest = [(r, i) for r in (1, 2, 4, 3, 5, 6, 7) for i in range(CHUNKS)]
    for r, i in first + [k for k in rest if k not in first]:
        slot = here.slot(r < 4, OFFSETS[r % 4], True)
        send(part.at[slot, rows(i)], theirs.at[r, rows(i)], sib_recv.at[r, i], sib)
        if (r, i) == first[-1]:
            send(wgrad.at[:, theirs_of_pair], wg_sib, pair_recv.at[0], sib)

    def total(r, i, more, dst=None):
        loads[r, i].wait()
        arrived(theirs.at[r, rows(i)], sib_recv.at[r, i])
        target = own.at[r] if dst is None else dst

        @pl.loop(0, step // SUM_ROWS, unroll=2)
        def _(j):
            at = pl.ds(pl.multiple_of(i * step + j * SUM_ROWS, SUM_ROWS), SUM_ROWS)
            acc = own[r, at, :].astype(F32) + theirs[r, at, :].astype(F32)
            for ref, base in more:
                at2 = pl.ds(pl.multiple_of(base * step + j * SUM_ROWS, SUM_ROWS), SUM_ROWS)
                acc = acc + ref[at2, :].astype(F32)
            if dst is not None:
                acc = acc.T
            target[at, :] = acc.astype(BF16)

    def plus(hh, k, i, more):
        if hh == 1 and i == CROSS:
            arrived(early.at[k], early_recv.at[k])
            return more + [(early.at[k], 0)]
        return more

    def skip(hh, i):
        return hh == 0 and i == CROSS

    def far(hh):
        r = 4 * hh
        for i in (1, 0):
            for j, land, to in ((i, far_up, up), (i + half, far_down, down)):
                if skip(hh, j):
                    continue
                total(r, j, plus(hh, 0, j, []))
                send(
                    own.at[r, rows(j)], land.at[hh, rows(i)],
                    far_recv.at[hh, int(j >= half), i], to,
                )

    def near(hh, i, j, up_more, down_more):
        r, s = 4 * hh + 1, 4 * hh + 2
        if not skip(hh, i):
            total(r, i, plus(hh, 1, i, up_more))
            send(own.at[r, rows(i)], near_up.at[hh, rows(i)], near_recv.at[hh, 0, i], up)
        if not skip(hh, j):
            total(s, j, plus(hh, 2, j, down_more))
            send(own.at[s, rows(j)], near_down.at[hh, rows(j)], near_recv.at[hh, 1, j], down)

    def near_first(hh):
        for i in (1, 0):
            near(hh, i + half, i, [], [])

    def near_last(hh):
        for i in (1, 0):
            if not skip(hh, i):
                arrived(far_up.at[hh, rows(i)], far_recv.at[hh, 0, i])
            arrived(far_down.at[hh, rows(i)], far_recv.at[hh, 1, i])
            near(hh, i, i + half, [(far_up.at[hh], i)], [(far_down.at[hh], i)])

    def final(hh):
        for i in (3, 1, 2, 0):
            if skip(hh, i):
                continue
            arrived(near_up.at[hh, rows(i)], near_recv.at[hh, 0, i])
            arrived(near_down.at[hh, rows(i)], near_recv.at[hh, 1, i])
            more = [(near_up.at[hh], i), (near_down.at[hh], i)]
            if hh == 0:
                total(3, i, more)
                send(own.at[3, rows(i)], cross.at[rows(i)], cross_recv.at[i], across)
            else:
                arrived(cross.at[rows(i)], cross_recv.at[i])
                total(7, i, more + [(cross, i)], out)

    far(0)
    for k in range(4):
        total(k, CROSS, [])
        if k < 3:
            send(own.at[k, rows(CROSS)], early.at[k], early_recv.at[k], across)
        else:
            send(own.at[k, rows(CROSS)], cross.at[rows(CROSS)], cross_recv.at[CROSS], across)
    near_first(0)

    extra[1].wait()
    arrived(wg_sib, pair_recv.at[0])

    @pl.loop(0, N_REP)
    def _(j):
        wg_own[j] = (wg_own[j].astype(F32) + wg_sib[j].astype(F32)).astype(BF16)

    for d in range(3):
        to = (here.row, peers[d])
        send(wg_own.at[peers[d + 4]], wg_in.at[d], wg_recv.at[d], to)
        send(wg_own.at[peers[d]], wg_in.at[d + 3], wg_recv.at[d + 3], to)
    for d, q in enumerate(peers):
        send(act.at[q], act_out.at[here.rep], act_recv.at[d], (here.row, q))
    extra[0].wait()
    keep = pltpu.make_async_copy(own_act, act_out.at[here.rep], local_sems.at[0])
    keep.start()
    far(1)

    for d in range(3):
        arrived(wg_in.at[d], wg_recv.at[d])

    @pl.loop(0, wg_half.shape[0])
    def _(j):
        at = pl.ds(pl.multiple_of(j * 128, 128), 128)
        acc = wg_own[peers[3], :, at].astype(F32)
        for d in range(3):
            acc = acc + wg_in[d, :, at].astype(F32)
        wg_x[:, at] = acc.astype(BF16)

    send(wg_x, wg_in.at[6], wg_recv.at[6], (here.row, peers[3]))
    near_last(0)

    for d in range(3, 7):
        arrived(wg_in.at[d], wg_recv.at[d])

    @pl.loop(0, wg_half.shape[0])
    def _(j):
        at = pl.ds(pl.multiple_of(j * 128, 128), 128)
        acc = wg_own[here.rep, :, at].astype(F32)
        for d in range(3, 7):
            acc = acc + wg_in[d, :, at].astype(F32)
        wg_half[j] = acc.astype(BF16)

    for k, (o, dy) in enumerate(columns):
        send(
            wg_half.at[here.slot(o, dy) // 2], wg_row.at[k], row_recv.at[k], here.at(o, dy)
        )
    near_first(1)
    final(0)
    near_last(1)
    for k in range(len(columns)):
        arrived(wg_row.at[k], row_recv.at[k])
    acc = wg_half[here.row // 2].astype(F32)
    for k in range(len(columns)):
        acc = acc + wg_row[k].astype(F32)
    wg_fin[...] = acc
    send(wg_fin, wg_fin_sib, pair_recv.at[1], sib)
    final(1)
    arrived(wg_fin_sib, pair_recv.at[1])

    @pl.when(here.c == 0)
    def _():
        wg_out[:edge, :] = wg_fin[:, :edge]
        wg_out[edge:, :] = wg_fin_sib[:, :edge]

    @pl.when(here.c == 1)
    def _():
        wg_out[:edge, :] = wg_fin_sib[:, edge:]
        wg_out[edge:, :] = wg_fin[:, edge:]

    keep.wait()
    for d, q in enumerate(peers):
        arrived(act_out.at[q], act_recv.at[d])
    send.finish()


def reduce_all(part, act, wgrad):
    n, rows, width = part.shape
    n_rep, k, wide = wgrad.shape
    edge = k // 2
    dma = pltpu.SemaphoreType.DMA
    return pl.pallas_call(
        reduce_kernel,
        in_specs=[ANY] * 3,
        out_specs=[ANY, VM, VM],
        out_shape=[
            jax.ShapeDtypeStruct(act.shape, BF16),
            jax.ShapeDtypeStruct((rows, width), BF16),
            jax.ShapeDtypeStruct((k, wide // n), F32),
        ],
        scratch_shapes=[
            pltpu.VMEM((8, rows, width), BF16),
            pltpu.VMEM((8, rows, width), BF16),
            pltpu.VMEM((2, rows // 2, width), BF16),
            pltpu.VMEM((2, rows // 2, width), BF16),
            pltpu.VMEM((2, rows, width), BF16),
            pltpu.VMEM((2, rows, width), BF16),
            pltpu.VMEM((rows, width), BF16),
            pltpu.VMEM((3, rows // CHUNKS, width), BF16),
            pltpu.VMEM(act.shape[1:], BF16),
            pltpu.VMEM((n_rep, edge, wide), BF16),
            pltpu.VMEM((n_rep, edge, wide), BF16),
            pltpu.VMEM((n_rep - 1, edge, wide), BF16),
            pltpu.VMEM((edge, wide), BF16),
            pltpu.VMEM((wide // 128, edge, 128), BF16),
            pltpu.VMEM((7, edge, 128), BF16),
            pltpu.VMEM((edge, 128), F32),
            pltpu.VMEM((edge, 128), F32),
            dma((15 * CHUNKS + 23,)), dma((8, CHUNKS)), dma((8, CHUNKS)), dma((2, 2, CHUNKS // 2)), dma((2, 2, CHUNKS)),
            dma((CHUNKS,)), dma((3,)), dma((7,)), dma((7,)), dma((7,)), dma((2,)), dma((2,)),
        ],
        compiler_params=pltpu.CompilerParams(collective_id=2, has_side_effects=True),
        name="reduce_all",
    )(part, act, wgrad)


SLOTS_AHEAD = 8


GROUP = 4
OUT_CHUNK = 16
FLUSHES = 8


def bwd_kernel(cols, counts, tiles, grad, out, acc, tbuf, stage, sems, out_sems):
    blocks, slots, t, _ = tiles.shape
    total = acc.shape[0]
    groups = slots // GROUP

    def copy(b, q):
        s = lax.rem(b, SLOTS_AHEAD)
        at = pl.ds(q * GROUP, GROUP)
        return pltpu.make_async_copy(tiles.at[b, at], tbuf.at[s, at], sems.at[s, q])

    def start(b):
        for q in range(groups):

            @pl.when(q * GROUP < counts[b])
            def _():
                copy(b, q).start()

    for b in range(SLOTS_AHEAD - 1):
        start(b)

    @pl.loop(0, total // 4)
    def _(j):
        for i in range(4):
            acc[4 * j + i] = jnp.zeros(acc.shape[1:], F32)

    @pl.loop(0, blocks)
    def _(b):
        s = lax.rem(b, SLOTS_AHEAD)

        @pl.when(b + SLOTS_AHEAD - 1 < blocks)
        def _():
            start(b + SLOTS_AHEAD - 1)

        n = counts[b]
        for live in range(1, groups + 1):

            @pl.when((n + GROUP - 1) // GROUP == live)
            def _():
                g = grad[pl.ds(pl.multiple_of(b * t, t), t), :].T
                for q in range(live):
                    copy(b, q).wait()
                for q in range(live):
                    wide = jnp.concatenate(
                        [tbuf[s, q * GROUP + i] for i in range(GROUP)], axis=1
                    )
                    terms = jnp.dot(g, wide, preferred_element_type=F32)
                    for i in range(GROUP):
                        k = q * GROUP + i
                        term = terms[:, i * t : (i + 1) * t]
                        if q == live - 1 and i > 0:
                            term = jnp.where(k < n, term, 0.0)
                        acc[cols[k, b]] += term

    def flush(c):
        s = lax.rem(c, FLUSHES)
        return pltpu.make_async_copy(
            stage.at[s], out.at[pl.ds(c * OUT_CHUNK, OUT_CHUNK)], out_sems.at[s]
        )

    @pl.loop(0, total // OUT_CHUNK)
    def _(c):
        s = lax.rem(c, FLUSHES)

        @pl.when(c >= FLUSHES)
        def _():
            flush(c - FLUSHES).wait()

        @pl.loop(0, OUT_CHUNK // 4)
        def _(j):
            for i in range(4):
                stage[s, 4 * j + i] = acc[c * OUT_CHUNK + 4 * j + i].astype(BF16)

        flush(c).start()

    for c in range(total // OUT_CHUNK - FLUSHES, total // OUT_CHUNK):
        flush(c).wait()


def spmm_t(grad, tiles, columns, counts, total):
    blocks, slots, t, _ = tiles.shape
    width = grad.shape[-1]
    return pl.pallas_call(
        bwd_kernel,
        grid_spec=pltpu.PrefetchScalarGridSpec(
            num_scalar_prefetch=2,
            grid=(1,),
            in_specs=[
                pl.BlockSpec(memory_space=pl.ANY),
                pl.BlockSpec((blocks * t, width), lambda i, *_: (0, 0)),
            ],
            out_specs=pl.BlockSpec(memory_space=pl.ANY),
            scratch_shapes=[
                pltpu.VMEM((total, t, width), F32),
                pltpu.VMEM((SLOTS_AHEAD, slots, t, t), BF16),
                pltpu.VMEM((FLUSHES, OUT_CHUNK, t, width), BF16),
                pltpu.SemaphoreType.DMA((SLOTS_AHEAD, slots // GROUP)),
                pltpu.SemaphoreType.DMA((FLUSHES,)),
            ],
        ),
        out_shape=jax.ShapeDtypeStruct((total, t, width), BF16),
        compiler_params=pltpu.CompilerParams(vmem_limit_bytes=60 * 1024 * 1024),
        name="spmm_t",
    )(columns, counts, tiles, grad)


PARTS = 4


def settle_kernel(a, b, w, a_out, b_out, w_out, a_buf, b_buf, in_sems, out_sems):
    step = a.shape[0] // PARTS
    ins, outs = [], []
    for j, (src, buf, dst) in enumerate(((a, a_buf, a_out), (b, b_buf, b_out))):
        for i in range(PARTS):
            at = pl.ds(i * step, step)
            ins.append(pltpu.make_async_copy(src.at[at], buf.at[at], in_sems.at[j, i]))
            outs.append(pltpu.make_async_copy(buf.at[at], dst.at[at], out_sems.at[j, i]))
    for copy in ins:
        copy.start()
    w_out[...] = w[...].T
    for first, then in zip(ins, outs):
        first.wait()
        then.start()
    for copy in outs:
        copy.wait()


def settle(a, b, w):
    dma = pltpu.SemaphoreType.DMA((2, PARTS))
    return pl.pallas_call(
        settle_kernel,
        in_specs=[ANY, ANY, VM],
        out_specs=[ANY, ANY, VM],
        out_shape=[
            jax.ShapeDtypeStruct(a.shape, BF16),
            jax.ShapeDtypeStruct(b.shape, BF16),
            jax.ShapeDtypeStruct(w.shape[::-1], F32),
        ],
        scratch_shapes=[pltpu.VMEM(a.shape, BF16), pltpu.VMEM(b.shape, BF16), dma, dma],
        name="settle",
    )(a, b, w)


def local(features, tiles, columns, counts, weight, cotangent):
    rows_here, feat_local = features.shape
    blocks_here, slots, t, _ = tiles.shape
    total_blocks = blocks_here * lax.axis_size("row")
    columns = columns.T
    mixed_grad, act, wgrad = forward(features, cotangent, weight, tiles, columns, counts)
    part = spmm_t(mixed_grad.reshape(features.shape), tiles, columns, counts, total_blocks)
    act, feature_grad, weight_grad = reduce_all(
        part.reshape(N_ROW, rows_here, feat_local), act, wgrad
    )
    act, feature_grad, weight_grad = settle(act.reshape(features.shape), feature_grad, weight_grad)
    return act, feature_grad, weight_grad.T


def solution(mesh):
    in_specs = (
        P("row", "rep"),
        P("row", None, None, None),
        P("row", None),
        P("row"),
        P(None, "rep"),
        P("row", "rep"),
    )
    out_specs = (P("row", "rep"), P("row", "rep"), P("rep", "row"))
    return jax.shard_map(local, mesh=mesh, in_specs=in_specs, out_specs=out_specs, check_vma=False)
```

```python
import functools

import jax
import jax.numpy as jnp
from jax import lax
from jax.experimental import pallas as pl
from jax.experimental.pallas import tpu as pltpu
from jax.sharding import PartitionSpec as P

F32 = jnp.float32
BF16 = jnp.bfloat16
MESH = pl.DeviceIdType.MESH
ROWS_Y = 4
N_ROW = 16
N_REP = 8
ANY = pl.BlockSpec(memory_space=pl.ANY)
VM = pl.BlockSpec(memory_space=pltpu.VMEM)


class Place:
    def __init__(self):
        self.row = lax.axis_index("row")
        self.rep = lax.axis_index("rep")
        self.c = lax.rem(self.row, 2)
        self.y = lax.rem(self.row // 2, ROWS_Y)
        self.h = self.row // (2 * ROWS_Y)

    def slot(self, other, dy, sib=False):
        h = 1 - self.h if other else self.h
        c = 1 - self.c if sib else self.c
        return (h * ROWS_Y + lax.rem(self.y + dy + ROWS_Y, ROWS_Y)) * 2 + c

    def at(self, other, dy, sib=False):
        return (self.slot(other, dy, sib), self.rep)

    def peer_at(self, d):
        x = lax.rem(self.rep // 4 + d // 4, 2)
        z1 = lax.rem(lax.rem(self.rep, 4) // 2 + lax.rem(d, 4) // 2, 2)
        z0 = lax.rem(self.rep + d, 2)
        return x * 4 + z1 * 2 + z0

    def peer(self, d):
        x, z = self.rep // 4, lax.rem(self.rep, 4)
        if d >= 4:
            x = 1 - x
        if d % 4 == 1:
            z = z + 1 - 2 * lax.rem(z, 2)
        elif d % 4 == 2:
            z = lax.rem(z + 2, 4)
        elif d % 4 == 3:
            z = 3 - z
        return x * 4 + z


def greet(partners):
    barrier = pltpu.get_barrier_semaphore()
    for partner in partners:
        pl.semaphore_signal(barrier, inc=1, device_id=partner, device_id_type=MESH)
    pl.semaphore_wait(barrier, len(partners))


class Sends:
    def __init__(self, sems):
        self.sems, self.live = sems, []

    def __call__(self, src, dst, recv_sem, device):
        copy = pltpu.make_async_remote_copy(
            src_ref=src,
            dst_ref=dst,
            send_sem=self.sems.at[len(self.live)],
            recv_sem=recv_sem,
            device_id=device,
            device_id_type=MESH,
        )
        copy.start()
        self.live.append(copy)

    def finish(self):
        for copy in self.live:
            copy.wait_send()


def arrived(dst, recv_sem):
    pltpu.make_async_copy(dst, dst, recv_sem).wait()


CHUNKS = 4
CROSS = 0


PAIR = 2


def forward_kernel(
    feats, cot, weight, tiles, cols, counts, mixed_grad, act, wgrad,
    full, blocks, cots, ws, w, mixed, m, grad, back,
    send_sems, recv_sems, cot_recv, w_recv, w_sib, m_send, m_recv, back_recv, local_sems,
):
    here = Place()
    n_blocks, slots, t, _ = tiles.shape
    step = n_blocks // CHUNKS
    piece = cot.shape[0] // N_REP
    width = cot.shape[1]
    half = weight.shape[0] // 2
    peers = [here.peer(d) for d in range(1, N_REP)]
    sib = here.at(False, 0, True)
    up, down, across = here.at(False, 1), here.at(False, -1), here.at(True, 0)

    def base(slot):
        return slot * n_blocks

    own = [
        pltpu.make_async_copy(feats, full.at[pl.ds(base(here.row), n_blocks)], local_sems.at[0]),
        pltpu.make_async_copy(weight, ws.at[here.rep], local_sems.at[1]),
        pltpu.make_async_copy(
            cot.at[pl.ds(pl.multiple_of(here.rep * piece, piece), piece)],
            cots.at[here.rep], local_sems.at[2],
        ),
        pltpu.make_async_copy(tiles, blocks, local_sems.at[3]),
    ]
    greet([sib, up, down, across] + [(here.row, q) for q in peers])
    send = Sends(send_sems)

    def rows(chunk):
        return pl.ds(chunk * step, step)

    def place(slot, chunk):
        return full.at[pl.ds(base(slot) + chunk * step, step)]

    columns = [
        (False, -1), (False, 1), (False, 2), (True, 0), (True, -1), (True, 1), (True, 2),
    ]
    slots_of = [here.slot(*column) for column in columns]
    opposite = [(i + CHUNKS // 2) % CHUNKS for i in range(CHUNKS)]

    mine = pl.ds(pl.multiple_of(here.c * half, half), half)
    theirs = pl.ds(pl.multiple_of((1 - here.c) * half, half), half)
    beside = peers[3]
    for d in (4, 1, 2, 3):
        send(weight.at[mine], ws.at[here.rep, mine], w_recv.at[d - 1], (here.row, peers[d - 1]))
    for i in range(CHUNKS):
        send(feats.at[rows(i)], place(here.row, i), recv_sems.at[3, i], across)
    for a, b in enumerate(opposite):
        send(feats.at[rows(a)], place(here.row, a), recv_sems.at[0, a], up)
        send(feats.at[rows(b)], place(here.row, b), recv_sems.at[1, b], down)
    for i in range(CHUNKS):
        send(feats.at[rows(i)], place(here.row, i), recv_sems.at[7, i], sib)
    for copy in own:
        copy.start()

    def take(kind, chunk, on=None):
        src = place(slots_of[kind], chunk)
        arrived(src, recv_sems.at[kind, chunk])
        if on is not None:
            send(src, src, recv_sems.at[2 if kind < 3 else 6, chunk], on)
        if kind < 3 and chunk == CROSS:
            send(src, src, recv_sems.at[4 + kind, chunk], across)
        send(src, src, recv_sems.at[8 + kind, chunk], sib)

    for k in (0, 4):
        for a, b in enumerate(opposite):
            take(k, a, up if a < CHUNKS // 2 and (k, a) != (4, CROSS) else None)
            take(k + 1, b, down if b >= CHUNKS // 2 and (k, b) != (4, CROSS) else None)
            if k == 0:
                src = place(slots_of[3], a)
                arrived(src, recv_sems.at[3, a])
                if a != CROSS:
                    send(src, src, recv_sems.at[4, a], up)
                    send(src, src, recv_sems.at[5, a], down)
                send(src, src, recv_sems.at[11, a], sib)
        if k == 0:
            arrived(ws.at[beside, mine], w_recv.at[3])
            for d in (1, 2, 3):
                send(
                    ws.at[beside, mine], ws.at[beside, mine], w_recv.at[d + 3],
                    (here.row, peers[d - 1]),
                )
        for i in range(CHUNKS):
            take(k + 2, i)
        if k == 0:
            for d, q in enumerate(peers):
                send(
                    cot.at[pl.ds(pl.multiple_of(q * piece, piece), piece)],
                    cots.at[here.rep], cot_recv.at[d], (here.row, q),
                )
    for d, q in enumerate(peers):
        if d != 3:
            arrived(ws.at[q, mine], w_recv.at[d])
        send(ws.at[q, mine], ws.at[q, mine], w_sib.at[d], sib)

    for d, q in enumerate(peers):
        arrived(ws.at[q, theirs], w_sib.at[d])
        arrived(cots.at[q], cot_recv.at[d])
    for copy in own:
        copy.wait()
    for r in range(N_REP):
        w[:, r * width : (r + 1) * width] = ws[r]
    for kind, column in enumerate([(False, 0)] + columns):
        for i in range(CHUNKS):
            arrived(place(here.slot(*column, True), i), recv_sems.at[7 + kind, i])

    strips = piece // t

    def shift(d, i):
        q, at = here.peer_at(d), pl.ds(i * t, t)
        return q, pltpu.make_async_remote_copy(
            src_ref=mixed.at[q, at], dst_ref=m.at[here.rep, at],
            send_sem=m_send.at[d - 1, i], recv_sem=m_recv.at[d - 1, i],
            device_id=(here.row, q), device_id_type=MESH,
        )

    def mix(i):
        at = pl.ds(i * t, t)

        @pl.loop(0, N_REP // PAIR)
        def _(j):
            copies = []
            for e in range(PAIR):
                q, copy = shift(lax.rem(3 * (j * PAIR + e), N_REP), i)
                copies.append(copy)
                b = q * strips + i
                n = counts[b]
                left = jnp.concatenate(
                    [jnp.where(k < n, blocks[b, k], jnp.zeros((), BF16)) for k in range(slots)],
                    axis=1,
                )
                right = jnp.concatenate([full[cols[k, b]] for k in range(slots)], axis=0)
                mixed[q, at, :] = jnp.dot(left, right, preferred_element_type=F32).astype(BF16)

            @pl.when(j > 0)
            def _():
                copies[0].start()

            for copy in copies[1:]:
                copy.start()

        m[here.rep, at, :] = mixed[here.rep, at, :]

    def whole(i):
        at = pl.ds(i * t, t)
        for d, q in enumerate(peers):
            arrived(m.at[q, at], m_recv.at[d, i])
        x = jnp.concatenate([m[r, at, :] for r in range(N_REP)], axis=1)
        c = jnp.concatenate([cots[r, at, :] for r in range(N_REP)], axis=1)
        pre = jnp.dot(x, w[...], preferred_element_type=F32)
        sig = jax.nn.sigmoid(pre)
        out = (pre * sig).astype(BF16)
        g = (c.astype(F32) * sig * (1.0 + pre * (1.0 - sig))).astype(BF16)
        grad[at, :] = g
        b = lax.dot_general(
            g, w[...], (((1,), (1,)), ((), ())), preferred_element_type=F32
        ).astype(BF16)
        for r in range(N_REP):
            act[r, at, :] = out[:, r * width : (r + 1) * width]
            back[r, at, :] = b[:, r * width : (r + 1) * width]
        for d, q in enumerate(peers):
            send(back.at[q, at], mixed_grad.at[here.rep, at], back_recv.at[d, i], (here.row, q))

    mix(0)
    for i in range(1, strips):
        mix(i)
        whole(i - 1)
    whole(strips - 1)
    last = pltpu.make_async_copy(back.at[here.rep], mixed_grad.at[here.rep], local_sems.at[4])
    last.start()
    for r in range(N_REP):
        wgrad[r] = lax.dot_general(
            m[r], grad[...], (((0,), (0,)), ((), ())), preferred_element_type=F32
        ).astype(BF16)
    last.wait()
    for d, q in enumerate(peers):
        for i in range(strips):
            arrived(mixed_grad.at[q, pl.ds(i * t, t)], back_recv.at[d, i])
    for d in range(1, N_REP):
        for i in range(strips):
            shift(d, i)[1].wait_send()
    send.finish()


def forward(features, cotangent, weight, tiles, columns, counts):
    rows, width = features.shape
    n_blocks, _, t, _ = tiles.shape
    piece = rows // N_REP
    strips = piece // t
    dma = pltpu.SemaphoreType.DMA
    smem = pl.BlockSpec(memory_space=pltpu.SMEM)
    stack = pltpu.VMEM((N_REP, piece, width), BF16)
    return pl.pallas_call(
        forward_kernel,
        in_specs=[ANY] * 4 + [smem] * 2,
        out_specs=[ANY, VM, VM],
        out_shape=[
            jax.ShapeDtypeStruct((N_REP, piece, width), BF16),
            jax.ShapeDtypeStruct((N_REP, piece, width), BF16),
            jax.ShapeDtypeStruct((N_REP, width, N_REP * width), BF16),
        ],
        scratch_shapes=[
            pltpu.VMEM((N_ROW * n_blocks, t, width), BF16),
            pltpu.VMEM(tiles.shape, BF16),
            stack,
            pltpu.VMEM((N_REP,) + weight.shape, BF16),
            pltpu.VMEM((N_REP * width, N_REP * width), BF16),
            stack, stack,
            pltpu.VMEM((piece, N_REP * width), BF16),
            stack,
            dma((15 * CHUNKS + 21 + 7 * strips,)), dma((15, CHUNKS)),
            dma((7,)), dma((7,)), dma((7,)), dma((7, strips)), dma((7, strips)), dma((7, strips)),
            dma((5,)),
        ],
        compiler_params=pltpu.CompilerParams(
            collective_id=0, has_side_effects=True, vmem_limit_bytes=60 * 1024 * 1024
        ),
        name="forward",
    )(features.reshape(n_blocks, t, width), cotangent, weight, tiles, columns, counts)


OFFSETS = (2, 1, -1, 0)
SUM_ROWS = 128


def reduce_kernel(
    part, act, wgrad, act_out, out, wg_out,
    own, theirs, far_up, far_down, near_up, near_down, cross, early, own_act,
    wg_own, wg_sib, wg_in, wg_x, wg_half, wg_row, wg_fin, wg_fin_sib,
    send_sems, load_sems, sib_recv, far_recv, near_recv, cross_recv, early_recv,
    act_recv, wg_recv, row_recv, pair_recv, local_sems,
):
    here = Place()
    step = own.shape[1] // CHUNKS
    half = CHUNKS // 2
    peers = [here.peer(d) for d in range(1, N_REP)]
    sib = here.at(False, 0, True)
    up, down, across = here.at(False, 1), here.at(False, -1), here.at(True, 0)
    columns = [(o, dy) for o in (True, False) for dy in OFFSETS][:-1]

    edge = wg_half.shape[1]
    mine = pl.ds(pl.multiple_of(here.c * edge, edge), edge)
    theirs_of_pair = pl.ds(pl.multiple_of((1 - here.c) * edge, edge), edge)

    def rows(i):
        return pl.ds(i * step, step)

    loads = {}
    for r in range(8):
        slot = here.slot(r < 4, OFFSETS[r % 4])
        for i in range(CHUNKS):
            loads[r, i] = pltpu.make_async_copy(
                part.at[slot, rows(i)], own.at[r, rows(i)], load_sems.at[r, i]
            )
    extra = [
        pltpu.make_async_copy(act.at[here.rep], own_act, local_sems.at[0]),
        pltpu.make_async_copy(wgrad.at[:, mine], wg_own, local_sems.at[1]),
    ]
    for load in extra:
        load.start()
    for load in loads.values():
        load.start()
    greet([sib] + [here.at(*column) for column in columns] + [(here.row, q) for q in peers])

    send = Sends(send_sems)
    first = [(0, i) for i in range(CHUNKS)] + [(r, CROSS) for r in (1, 2, 3)]
    rest = [(r, i) for r in (1, 2, 4, 3, 5, 6, 7) for i in range(CHUNKS)]
    for r, i in first + [k for k in rest if k not in first]:
        slot = here.slot(r < 4, OFFSETS[r % 4], True)
        send(part.at[slot, rows(i)], theirs.at[r, rows(i)], sib_recv.at[r, i], sib)
        if (r, i) == first[-1]:
            send(wgrad.at[:, theirs_of_pair], wg_sib, pair_recv.at[0], sib)

    def total(r, i, more, dst=None):
        loads[r, i].wait()
        arrived(theirs.at[r, rows(i)], sib_recv.at[r, i])
        target = own.at[r] if dst is None else dst

        @pl.loop(0, step // SUM_ROWS, unroll=4)
        def _(j):
            at = pl.ds(pl.multiple_of(i * step + j * SUM_ROWS, SUM_ROWS), SUM_ROWS)
            acc = own[r, at, :].astype(F32) + theirs[r, at, :].astype(F32)
            for ref, base in more:
                at2 = pl.ds(pl.multiple_of(base * step + j * SUM_ROWS, SUM_ROWS), SUM_ROWS)
                acc = acc + ref[at2, :].astype(F32)
            if dst is not None:
                acc = acc.T
            target[at, :] = acc.astype(BF16)

    def plus(hh, k, i, more):
        if hh == 1 and i == CROSS:
            arrived(early.at[k], early_recv.at[k])
            return more + [(early.at[k], 0)]
        return more

    def skip(hh, i):
        return hh == 0 and i == CROSS

    def far(hh):
        r = 4 * hh
        for i in (1, 0):
            for j, land, to in ((i, far_up, up), (i + half, far_down, down)):
                if skip(hh, j):
                    continue
                total(r, j, plus(hh, 0, j, []))
                send(
                    own.at[r, rows(j)], land.at[hh, rows(i)],
                    far_recv.at[hh, int(j >= half), i], to,
                )

    def near(hh, i, j, up_more, down_more):
        r, s = 4 * hh + 1, 4 * hh + 2
        if not skip(hh, i):
            total(r, i, plus(hh, 1, i, up_more))
            send(own.at[r, rows(i)], near_up.at[hh, rows(i)], near_recv.at[hh, 0, i], up)
        if not skip(hh, j):
            total(s, j, plus(hh, 2, j, down_more))
            send(own.at[s, rows(j)], near_down.at[hh, rows(j)], near_recv.at[hh, 1, j], down)

    def near_first(hh):
        for i in (1, 0):
            near(hh, i + half, i, [], [])

    def near_last(hh):
        for i in (1, 0):
            if not skip(hh, i):
                arrived(far_up.at[hh, rows(i)], far_recv.at[hh, 0, i])
            arrived(far_down.at[hh, rows(i)], far_recv.at[hh, 1, i])
            near(hh, i, i + half, [(far_up.at[hh], i)], [(far_down.at[hh], i)])

    def final(hh):
        for i in (3, 1, 2, 0):
            if skip(hh, i):
                continue
            arrived(near_up.at[hh, rows(i)], near_recv.at[hh, 0, i])
            arrived(near_down.at[hh, rows(i)], near_recv.at[hh, 1, i])
            more = [(near_up.at[hh], i), (near_down.at[hh], i)]
            if hh == 0:
                total(3, i, more)
                send(own.at[3, rows(i)], cross.at[rows(i)], cross_recv.at[i], across)
            else:
                arrived(cross.at[rows(i)], cross_recv.at[i])
                total(7, i, more + [(cross, i)], out)

    far(0)
    for k in range(4):
        total(k, CROSS, [])
        if k < 3:
            send(own.at[k, rows(CROSS)], early.at[k], early_recv.at[k], across)
        else:
            send(own.at[k, rows(CROSS)], cross.at[rows(CROSS)], cross_recv.at[CROSS], across)
    near_first(0)

    extra[1].wait()
    arrived(wg_sib, pair_recv.at[0])

    @pl.loop(0, N_REP)
    def _(j):
        wg_own[j] = (wg_own[j].astype(F32) + wg_sib[j].astype(F32)).astype(BF16)

    for d in range(3):
        to = (here.row, peers[d])
        send(wg_own.at[peers[d + 4]], wg_in.at[d], wg_recv.at[d], to)
        send(wg_own.at[peers[d]], wg_in.at[d + 3], wg_recv.at[d + 3], to)
    for d, q in enumerate(peers):
        send(act.at[q], act_out.at[here.rep], act_recv.at[d], (here.row, q))
    extra[0].wait()
    keep = pltpu.make_async_copy(own_act, act_out.at[here.rep], local_sems.at[0])
    keep.start()
    far(1)

    for d in range(3):
        arrived(wg_in.at[d], wg_recv.at[d])

    @pl.loop(0, wg_half.shape[0])
    def _(j):
        at = pl.ds(pl.multiple_of(j * 128, 128), 128)
        acc = wg_own[peers[3], :, at].astype(F32)
        for d in range(3):
            acc = acc + wg_in[d, :, at].astype(F32)
        wg_x[:, at] = acc.astype(BF16)

    send(wg_x, wg_in.at[6], wg_recv.at[6], (here.row, peers[3]))
    near_last(0)

    for d in range(3, 7):
        arrived(wg_in.at[d], wg_recv.at[d])

    @pl.loop(0, wg_half.shape[0])
    def _(j):
        at = pl.ds(pl.multiple_of(j * 128, 128), 128)
        acc = wg_own[here.rep, :, at].astype(F32)
        for d in range(3, 7):
            acc = acc + wg_in[d, :, at].astype(F32)
        wg_half[j] = acc.astype(BF16)

    for k, (o, dy) in enumerate(columns):
        send(
            wg_half.at[here.slot(o, dy) // 2], wg_row.at[k], row_recv.at[k], here.at(o, dy)
        )
    near_first(1)
    final(0)
    near_last(1)
    for k in range(len(columns)):
        arrived(wg_row.at[k], row_recv.at[k])
    acc = wg_half[here.row // 2].astype(F32)
    for k in range(len(columns)):
        acc = acc + wg_row[k].astype(F32)
    wg_fin[...] = acc
    send(wg_fin, wg_fin_sib, pair_recv.at[1], sib)
    final(1)
    arrived(wg_fin_sib, pair_recv.at[1])

    @pl.when(here.c == 0)
    def _():
        wg_out[:edge, :] = wg_fin[:, :edge]
        wg_out[edge:, :] = wg_fin_sib[:, :edge]

    @pl.when(here.c == 1)
    def _():
        wg_out[:edge, :] = wg_fin_sib[:, edge:]
        wg_out[edge:, :] = wg_fin[:, edge:]

    keep.wait()
    for d, q in enumerate(peers):
        arrived(act_out.at[q], act_recv.at[d])
    send.finish()


def reduce_all(part, act, wgrad):
    n, rows, width = part.shape
    n_rep, k, wide = wgrad.shape
    edge = k // 2
    dma = pltpu.SemaphoreType.DMA
    return pl.pallas_call(
        reduce_kernel,
        in_specs=[ANY] * 3,
        out_specs=[ANY, VM, VM],
        out_shape=[
            jax.ShapeDtypeStruct(act.shape, BF16),
            jax.ShapeDtypeStruct((rows, width), BF16),
            jax.ShapeDtypeStruct((k, wide // n), F32),
        ],
        scratch_shapes=[
            pltpu.VMEM((8, rows, width), BF16),
            pltpu.VMEM((8, rows, width), BF16),
            pltpu.VMEM((2, rows // 2, width), BF16),
            pltpu.VMEM((2, rows // 2, width), BF16),
            pltpu.VMEM((2, rows, width), BF16),
            pltpu.VMEM((2, rows, width), BF16),
            pltpu.VMEM((rows, width), BF16),
            pltpu.VMEM((3, rows // CHUNKS, width), BF16),
            pltpu.VMEM(act.shape[1:], BF16),
            pltpu.VMEM((n_rep, edge, wide), BF16),
            pltpu.VMEM((n_rep, edge, wide), BF16),
            pltpu.VMEM((n_rep - 1, edge, wide), BF16),
            pltpu.VMEM((edge, wide), BF16),
            pltpu.VMEM((wide // 128, edge, 128), BF16),
            pltpu.VMEM((7, edge, 128), BF16),
            pltpu.VMEM((edge, 128), F32),
            pltpu.VMEM((edge, 128), F32),
            dma((15 * CHUNKS + 23,)), dma((8, CHUNKS)), dma((8, CHUNKS)), dma((2, 2, CHUNKS // 2)), dma((2, 2, CHUNKS)),
            dma((CHUNKS,)), dma((3,)), dma((7,)), dma((7,)), dma((7,)), dma((2,)), dma((2,)),
        ],
        compiler_params=pltpu.CompilerParams(collective_id=2, has_side_effects=True),
        name="reduce_all",
    )(part, act, wgrad)


SLOTS_AHEAD = 8


GROUP = 4
OUT_CHUNK = 16
FLUSHES = 8


def bwd_kernel(cols, counts, tiles, grad, out, acc, tbuf, stage, sems, out_sems):
    blocks, slots, t, _ = tiles.shape
    total = acc.shape[0]
    groups = slots // GROUP

    def copy(b, q):
        s = lax.rem(b, SLOTS_AHEAD)
        at = pl.ds(q * GROUP, GROUP)
        return pltpu.make_async_copy(tiles.at[b, at], tbuf.at[s, at], sems.at[s, q])

    def start(b):
        for q in range(groups):

            @pl.when(q * GROUP < counts[b])
            def _():
                copy(b, q).start()

    for b in range(SLOTS_AHEAD - 1):
        start(b)

    @pl.loop(0, total // 4)
    def _(j):
        for i in range(4):
            acc[4 * j + i] = jnp.zeros(acc.shape[1:], F32)

    @pl.loop(0, blocks)
    def _(b):
        s = lax.rem(b, SLOTS_AHEAD)

        @pl.when(b + SLOTS_AHEAD - 1 < blocks)
        def _():
            start(b + SLOTS_AHEAD - 1)

        n = counts[b]
        for live in range(1, groups + 1):

            @pl.when((n + GROUP - 1) // GROUP == live)
            def _():
                g = grad[pl.ds(pl.multiple_of(b * t, t), t), :].T
                for q in range(live):
                    copy(b, q).wait()
                for q in range(live):
                    wide = jnp.concatenate(
                        [tbuf[s, q * GROUP + i] for i in range(GROUP)], axis=1
                    )
                    terms = jnp.dot(g, wide, preferred_element_type=F32)
                    for i in range(GROUP):
                        k = q * GROUP + i
                        term = terms[:, i * t : (i + 1) * t]
                        if q == live - 1 and i > 0:
                            term = jnp.where(k < n, term, 0.0)
                        acc[cols[k, b]] += term

    def flush(c):
        s = lax.rem(c, FLUSHES)
        return pltpu.make_async_copy(
            stage.at[s], out.at[pl.ds(c * OUT_CHUNK, OUT_CHUNK)], out_sems.at[s]
        )

    @pl.loop(0, total // OUT_CHUNK)
    def _(c):
        s = lax.rem(c, FLUSHES)

        @pl.when(c >= FLUSHES)
        def _():
            flush(c - FLUSHES).wait()

        @pl.loop(0, OUT_CHUNK // 4)
        def _(j):
            for i in range(4):
                stage[s, 4 * j + i] = acc[c * OUT_CHUNK + 4 * j + i].astype(BF16)

        flush(c).start()

    for c in range(total // OUT_CHUNK - FLUSHES, total // OUT_CHUNK):
        flush(c).wait()


def spmm_t(grad, tiles, columns, counts, total):
    blocks, slots, t, _ = tiles.shape
    width = grad.shape[-1]
    return pl.pallas_call(
        bwd_kernel,
        grid_spec=pltpu.PrefetchScalarGridSpec(
            num_scalar_prefetch=2,
            grid=(1,),
            in_specs=[
                pl.BlockSpec(memory_space=pl.ANY),
                pl.BlockSpec((blocks * t, width), lambda i, *_: (0, 0)),
            ],
            out_specs=pl.BlockSpec(memory_space=pl.ANY),
            scratch_shapes=[
                pltpu.VMEM((total, t, width), F32),
                pltpu.VMEM((SLOTS_AHEAD, slots, t, t), BF16),
                pltpu.VMEM((FLUSHES, OUT_CHUNK, t, width), BF16),
                pltpu.SemaphoreType.DMA((SLOTS_AHEAD, slots // GROUP)),
                pltpu.SemaphoreType.DMA((FLUSHES,)),
            ],
        ),
        out_shape=jax.ShapeDtypeStruct((total, t, width), BF16),
        compiler_params=pltpu.CompilerParams(vmem_limit_bytes=60 * 1024 * 1024),
        name="spmm_t",
    )(columns, counts, tiles, grad)


PARTS = 4


def settle_kernel(a, b, w, a_out, b_out, w_out, a_buf, b_buf, in_sems, out_sems):
    step = a.shape[0] // PARTS
    ins, outs = [], []
    for j, (src, buf, dst) in enumerate(((a, a_buf, a_out), (b, b_buf, b_out))):
        for i in range(PARTS):
            at = pl.ds(i * step, step)
            ins.append(pltpu.make_async_copy(src.at[at], buf.at[at], in_sems.at[j, i]))
            outs.append(pltpu.make_async_copy(buf.at[at], dst.at[at], out_sems.at[j, i]))
    for copy in ins:
        copy.start()
    w_out[...] = w[...].T
    for first, then in zip(ins, outs):
        first.wait()
        then.start()
    for copy in outs:
        copy.wait()


def settle(a, b, w):
    dma = pltpu.SemaphoreType.DMA((2, PARTS))
    return pl.pallas_call(
        settle_kernel,
        in_specs=[ANY, ANY, VM],
        out_specs=[ANY, ANY, VM],
        out_shape=[
            jax.ShapeDtypeStruct(a.shape, BF16),
            jax.ShapeDtypeStruct(b.shape, BF16),
            jax.ShapeDtypeStruct(w.shape[::-1], F32),
        ],
        scratch_shapes=[pltpu.VMEM(a.shape, BF16), pltpu.VMEM(b.shape, BF16), dma, dma],
        name="settle",
    )(a, b, w)


def local(features, tiles, columns, counts, weight, cotangent):
    rows_here, feat_local = features.shape
    blocks_here, slots, t, _ = tiles.shape
    total_blocks = blocks_here * lax.axis_size("row")
    columns = columns.T
    mixed_grad, act, wgrad = forward(features, cotangent, weight, tiles, columns, counts)
    part = spmm_t(mixed_grad.reshape(features.shape), tiles, columns, counts, total_blocks)
    act, feature_grad, weight_grad = reduce_all(
        part.reshape(N_ROW, rows_here, feat_local), act, wgrad
    )
    act, feature_grad, weight_grad = settle(act.reshape(features.shape), feature_grad, weight_grad)
    return act, feature_grad, weight_grad.T


def solution(mesh):
    in_specs = (
        P("row", "rep"),
        P("row", None, None, None),
        P("row", None),
        P("row"),
        P(None, "rep"),
        P("row", "rep"),
    )
    out_specs = (P("row", "rep"), P("row", "rep"), P("rep", "row"))
    return jax.shard_map(local, mesh=mesh, in_specs=in_specs, out_specs=out_specs, check_vma=False)
```
